32 devices in a mesh: dp: 8 (over y, x, core), fsdp: 4 (over z).
Axes of the slice: x: 2, y: 2, z: 4, core: 2. Of those that a mesh axis runs over, the one named last changes fastest.
Arguments:
- tokens: bfloat16 [46400, 1024], P(('dp', 'fsdp')), may hold values from -6 to 6
- output_grad: bfloat16 [46400, 1024], P(('dp', 'fsdp')), may hold values from -6 to 6
- group_member: int32 [8], P('dp'), may hold values from 0 to 1, as said below
- image_counts: int32 [2], replicated, may hold values from 64 to 4095
- position_source: int32 [145, 4], replicated, may hold values from 0 to 49
- position_table: bfloat16 [50, 1024], P(None, 'fsdp'), may hold values from -3 to 3
- first_gain: bfloat16 [1024], P('fsdp'), may hold values from 0.5 to 1.5
- first_shift: bfloat16 [1024], P('fsdp'), may hold values from -1 to 1
- input_proj: bfloat16 [1024, 3072], P('fsdp'), may hold values from -0.1875 to 0.1875
- query_bias: bfloat16 [1024], P('fsdp'), may hold values from -1 to 1
- value_bias: bfloat16 [1024], P('fsdp'), may hold values from -1 to 1
- output_proj: bfloat16 [1024, 1024], P('fsdp'), may hold values from -0.75 to 0.75
- output_bias: bfloat16 [1024], P('fsdp'), may hold values from -1 to 1
- second_gain: bfloat16 [1024], P('fsdp'), may hold values from 0.5 to 1.5
- second_shift: bfloat16 [1024], P('fsdp'), may hold values from -1 to 1
- hidden_weight: bfloat16 [1024, 4096], P('fsdp'), may hold values from -0.1875 to 0.1875
- hidden_bias: bfloat16 [4096], P('fsdp'), may hold values from -1 to 1
- return_weight: bfloat16 [4096, 1024], P('fsdp'), may hold values from -0.09375 to 0.09375
- return_bias: bfloat16 [1024], P('fsdp'), may hold values from -1 to 1
Outputs:
- block_out: bfloat16 [46400, 1024], P(('dp', 'fsdp'))
- tokens_grad: bfloat16 [46400, 1024], P(('dp', 'fsdp'))
- table_grad: float32 [50, 1024], P(None, 'fsdp')
- first_gain_grad: float32 [1024], P('fsdp')
- first_shift_grad: float32 [1024], P('fsdp')
- input_proj_grad: float32 [1024, 3072], P('fsdp')
- query_bias_grad: float32 [1024], P('fsdp')
- value_bias_grad: float32 [1024], P('fsdp')
- output_proj_grad: float32 [1024, 1024], P('fsdp')
- output_bias_grad: float32 [1024], P('fsdp')
- second_gain_grad: float32 [1024], P('fsdp')
- second_shift_grad: float32 [1024], P('fsdp')
- hidden_weight_grad: float32 [1024, 4096], P('fsdp')
- hidden_bias_grad: float32 [4096], P('fsdp')
- return_weight_grad: float32 [4096, 1024], P('fsdp')
- return_bias_grad: float32 [1024], P('fsdp')
The draws below stay inside these ranges and needn't reach their ends.
Inputs may be any that keep to these rules, and one draw needn't show every extreme that they name: `group_member`: exactly 3 entries are 1, the others 0.
All inputs are finite; a program needn't handle non-finite values.
Results may differ from the reference program's by a relative error of at most 0.02.
Values may be sent and summed in bfloat16 or wider, within the bound.
No kernel may reach another device: no remote copies, remote signals or barrier semaphores. Data moves between devices by JAX's collectives and lax.ppermute only.
A program may use at most 320 MiB of HBM per device.

```python
import jax
import jax.numpy as jnp
from jax import lax

D = 1024
HEADS = 16
HEAD_DIM = 64
FF = 4096
SG = 7
LG = 12
SMALL_LEN = 50
LARGE_LEN = 145
ROWS = 1450
TOKENS = 46400
GROUP_HI = 3
GROUP_LO = 5
N_DP = 8
N_FSDP = 4


def draw_group_member(key, part):
    order = jax.random.permutation(key, N_DP)
    return (order < GROUP_HI).astype(jnp.int32)


def place_ends(values, own_key, smallest, high):
    longest = values.shape.index(max(values.shape))
    spots = []
    for shift in (0, 1):
        where = [jax.random.randint(jax.random.fold_in(own_key, axis), (), 0, length) for axis, length in enumerate(values.shape)]
        where[longest] = (where[longest] + shift) % values.shape[longest]
        spots.append(tuple(where))
    return values.at[spots[0]].set(smallest).at[spots[1]].set(high)


def shard_levels(own_key, dims, split, low, largest):
    def one(axis_at, parts):
        heights = jax.random.uniform(jax.random.fold_in(jax.random.fold_in(own_key, 6), axis_at), (parts,), jnp.float32, low / len(split), largest / len(split))
        return jnp.repeat(jnp.exp(heights), dims[axis_at] // parts).reshape((-1,) + (1,) * (len(dims) - axis_at - 1))

    level = one(*split[0])
    for cut in split[1:]:
        level = level * one(*cut)
    return level


def noise(own_key, dims, spread, most, shards=(), kind=jnp.bfloat16):
    array = spread * jax.random.normal(own_key, dims, jnp.float32)
    if shards:
        array = array * shard_levels(own_key, dims, shards, -0.22, 0.18)
    return jnp.clip(array, -most, most).astype(kind)


def setup_inputs(seed: int = 0) -> dict:
    streams_of = jax.random.split(jax.random.key(seed), 20)
    return {
        "tokens": noise(streams_of[0], (TOKENS, D), 1.0, 6.0, ((0, 32),)),
        "output_grad": noise(streams_of[1], (TOKENS, D), 1.0, 6.0, ((0, 32),)),
        "group_member": draw_group_member(jax.random.fold_in(streams_of[19], 71), 0),
        "image_counts": jax.random.randint(streams_of[3], (2,), 64, 4096).astype(jnp.int32),
        "position_source": place_ends(jax.random.randint(streams_of[4], (LARGE_LEN, 4), 0, SMALL_LEN), jax.random.fold_in(streams_of[4], 1), 0, SMALL_LEN - 1).astype(jnp.int32),
        "position_table": noise(streams_of[5], (SMALL_LEN, D), 0.5, 3.0, ((1, 4),)),
        "first_gain": jnp.clip(1.0 + 0.1 * jax.random.normal(streams_of[6], (D,), jnp.float32), 0.5, 1.5).astype(jnp.bfloat16),
        "first_shift": noise(streams_of[7], (D,), 0.2, 1.0, ((0, 4),)),
        "input_proj": noise(streams_of[8], (D, 3 * D), D ** -0.5, 0.1875, ((0, 4),)),
        "query_bias": noise(streams_of[9], (D,), 0.2, 1.0, ((0, 4),)),
        "value_bias": noise(streams_of[10], (D,), 0.2, 1.0, ((0, 4),)),
        "output_proj": noise(streams_of[11], (D, D), (D // 16) ** -0.5, 0.75, ((0, 4),)),
        "output_bias": noise(streams_of[12], (D,), 0.2, 1.0, ((0, 4),)),
        "second_gain": jnp.clip(1.0 + 0.1 * jax.random.normal(streams_of[13], (D,), jnp.float32), 0.5, 1.5).astype(jnp.bfloat16),
        "second_shift": noise(streams_of[14], (D,), 0.2, 1.0, ((0, 4),)),
        "hidden_weight": noise(streams_of[15], (D, FF), D ** -0.5, 0.1875, ((0, 4),)),
        "hidden_bias": noise(streams_of[16], (FF,), 0.2, 1.0, ((0, 4),)),
        "return_weight": noise(streams_of[17], (FF, D), FF ** -0.5, 0.09375, ((0, 4),)),
        "return_bias": noise(streams_of[18], (D,), 0.2, 1.0, ((0, 4),)),
    }


EPS = 1e-06

@jax.custom_vjp
def low(v):
    return lax.optimization_barrier(v.astype(jnp.bfloat16)).astype(jnp.float32)

@jax.custom_vjp
def low_back(v):
    return v

def low_keep(v):
    return (low(v), None)

def low_pass(kept, grad):
    return (grad,)

def back_keep(v):
    return (v, None)

def back_low(kept, grad):
    return (low(grad),)
low.defvjp(low_keep, low_pass)
low_back.defvjp(back_keep, back_low)

def grid_fraction(index):
    scaled = jnp.maximum((2 * index + 1) * SG - LG, 0)
    lower = scaled // (2 * LG)
    return (scaled - 2 * LG * lower).astype(jnp.float32) / (2.0 * LG)

def interp_table(position_source):
    position = jnp.arange(LARGE_LEN, dtype=jnp.int32)
    patch = jnp.maximum(position - 1, 0)
    frac_row = grid_fraction(patch // LG)
    frac_col = grid_fraction(patch % LG)
    weights = jnp.stack([(1.0 - frac_row) * (1.0 - frac_col), (1.0 - frac_row) * frac_col, frac_row * (1.0 - frac_col), frac_row * frac_col], axis=1)
    class_row = (jnp.arange(4, dtype=jnp.int32) == 0).astype(jnp.float32)
    weights = jnp.where((position == 0)[:, None], class_row[None, :], weights)
    onehot = (position_source[:, :, None] == jnp.arange(SMALL_LEN, dtype=jnp.int32)[None, None, :]).astype(jnp.float32)
    return lax.optimization_barrier(jnp.sum(weights[:, :, None] * onehot, axis=1))

def matmul(left, right):
    return jnp.dot(left, right, precision=lax.Precision.HIGHEST)

def layer_norm(values, gain, shift):
    average = lax.optimization_barrier(jnp.mean(values, axis=-1, keepdims=True))
    centred = values - average
    variance = lax.optimization_barrier(jnp.mean(centred * centred, axis=-1, keepdims=True))
    return centred * lax.rsqrt(variance + EPS) * gain + shift

def block_forward(stream_in, params, mixing, length):
    table, gain_one, shift_one, joint, query_add, value_add, outproj, output_add, gain_two, shift_two, hidden_w, hidden_add, return_w, return_add = params
    images = ROWS // length
    position = matmul(mixing, table)
    stream = stream_in + jnp.tile(position, (images, 1))
    first = low(layer_norm(stream, gain_one, shift_one))
    projected = matmul(first, joint)
    query = low_back(low(projected[:, :D] + query_add)).reshape(images, length, HEADS, HEAD_DIM)
    keys = low_back(low(projected[:, D:2 * D])).reshape(images, length, HEADS, HEAD_DIM)
    values = low_back(low(projected[:, 2 * D:] + value_add)).reshape(images, length, HEADS, HEAD_DIM)
    scores = low_back(jnp.einsum('nqhd,nkhd->nhqk', query, keys, precision=lax.Precision.HIGHEST) / jnp.sqrt(jnp.float32(HEAD_DIM)))
    probs = low(jax.nn.softmax(scores, axis=-1))
    attended = jnp.einsum('nhqk,nkhd->nqhd', probs, values, precision=lax.Precision.HIGHEST).reshape(ROWS, D)
    attended = low_back(low(attended))
    branch = low_back(matmul(attended, outproj) + output_add)
    mid = stream + branch
    second = low(layer_norm(mid, gain_two, shift_two))
    hidden = low_back(matmul(second, hidden_w) + hidden_add)
    activ = low(jax.nn.gelu(hidden, approximate=False))
    returned = low_back(matmul(activ, return_w) + return_add)
    return mid + returned

def run_group(tokens, output_grad, group_member, params, member_value, count, length, mixing):
    index = jnp.nonzero(group_member == member_value, size=count)[0].astype(jnp.int32)
    blocks_in = tokens.reshape(N_DP, N_FSDP, ROWS, D)[index].reshape(count * N_FSDP, ROWS, D)
    blocks_grad = output_grad.reshape(N_DP, N_FSDP, ROWS, D)[index].reshape(count * N_FSDP, ROWS, D)

    def step(carry, pair):
        block_in, block_grad = pair

        def forward(stream_in, *param_list):
            return block_forward(stream_in, param_list, mixing, length)
        result, pull = jax.vjp(forward, block_in.astype(jnp.float32), *params)
        grads = pull(block_grad.astype(jnp.float32))
        summed = tuple((total + piece for total, piece in zip(carry, grads[1:])))
        return (summed, (result.astype(jnp.bfloat16), grads[0].astype(jnp.bfloat16)))
    start = tuple((jnp.zeros_like(piece) for piece in params))
    sums, (results, input_grads) = lax.scan(step, start, (blocks_in, blocks_grad))
    return (index, sums, results.reshape(count, N_FSDP, ROWS, D), input_grads.reshape(count, N_FSDP, ROWS, D))

def reference(tokens, output_grad, group_member, image_counts, position_source, position_table, first_gain, first_shift, input_proj, query_bias, value_bias, output_proj, output_bias, second_gain, second_shift, hidden_weight, hidden_bias, return_weight, return_bias):
    params = tuple((piece.astype(jnp.float32) for piece in (position_table, first_gain, first_shift, input_proj, query_bias, value_bias, output_proj, output_bias, second_gain, second_shift, hidden_weight, hidden_bias, return_weight, return_bias)))
    inter = interp_table(position_source)
    identity = jnp.eye(SMALL_LEN, dtype=jnp.float32)
    high_index, high_sums, high_out, high_grad = run_group(tokens, output_grad, group_member, params, 1, GROUP_HI, LARGE_LEN, inter)
    low_index, low_sums, low_out, low_grad = run_group(tokens, output_grad, group_member, params, 0, GROUP_LO, SMALL_LEN, identity)
    block_out = jnp.zeros((N_DP, N_FSDP, ROWS, D), jnp.bfloat16).at[high_index].set(high_out).at[low_index].set(low_out)
    tokens_grad = jnp.zeros((N_DP, N_FSDP, ROWS, D), jnp.bfloat16).at[high_index].set(high_grad).at[low_index].set(low_grad)
    counts = image_counts.astype(jnp.float32)
    total = counts[0] + counts[1]
    factor_high = counts[1] / total / (GROUP_HI * N_FSDP * (ROWS // LARGE_LEN))
    factor_low = counts[0] / total / (GROUP_LO * N_FSDP * (ROWS // SMALL_LEN))
    grads = tuple((factor_high * high_piece + factor_low * low_piece for high_piece, low_piece in zip(high_sums, low_sums)))
    return (block_out.reshape(TOKENS, D), tokens_grad.reshape(TOKENS, D), grads[0], grads[1], grads[2], grads[3], grads[4], grads[5], grads[6], grads[7], grads[8], grads[9], grads[10], grads[11], grads[12], grads[13])
```

```python
from functools import partial
import math

import jax
import jax.numpy as jnp
from jax import lax
from jax.experimental import pallas as pl
from jax.experimental.pallas import tpu as pltpu
from jax.sharding import PartitionSpec as P

D = 1024
HEADS = 16
HEAD_DIM = 64
SG = 7
LG = 12
SMALL_LEN = 50
LARGE_LEN = 145
ROWS = 1450


EPS = 1e-06


def shortened(value):
    return jax.tree.map(lambda a: a.astype(jnp.bfloat16) if a.dtype == jnp.float32 else a, value)


def grid_fraction(index):
    scaled = jnp.maximum((2 * index + 1) * SG - LG, 0)
    lower = scaled // (2 * LG)
    return (scaled - 2 * LG * lower).astype(jnp.float32) / (2.0 * LG)


def interp_table(position_source):
    position = jnp.arange(LARGE_LEN, dtype=jnp.int32)
    patch = jnp.maximum(position - 1, 0)
    frac_row = grid_fraction(patch // LG)
    frac_col = grid_fraction(patch % LG)
    weights = jnp.stack(
        [
            (1.0 - frac_row) * (1.0 - frac_col),
            (1.0 - frac_row) * frac_col,
            frac_row * (1.0 - frac_col),
            frac_row * frac_col,
        ],
        axis=1,
    )
    class_row = (jnp.arange(4, dtype=jnp.int32) == 0).astype(jnp.float32)
    weights = jnp.where((position == 0)[:, None], class_row[None, :], weights)
    onehot = (
        position_source[:, :, None] == jnp.arange(SMALL_LEN, dtype=jnp.int32)[None, None, :]
    ).astype(jnp.float32)
    return jnp.sum(weights[:, :, None] * onehot, axis=1)


def layer_norm(values, gain, shift):
    average = jnp.mean(values, axis=-1, keepdims=True)
    centred = values - average
    variance = jnp.mean(centred * centred, axis=-1, keepdims=True)
    inv_std = lax.rsqrt(variance + EPS)
    normed = centred * inv_std
    return (normed * gain + shift, normed, inv_std)


def norm_back(grad_norm, normed, inv_std, gain):
    scaled = grad_norm * gain
    inner = (
        scaled
        - jnp.mean(scaled, axis=-1, keepdims=True)
        - normed * jnp.mean(scaled * normed, axis=-1, keepdims=True)
    )
    return (inv_std * inner, jnp.sum(grad_norm * normed, axis=0), jnp.sum(grad_norm, axis=0))


def image_scores(query_low, keys_low, length):
    images = ROWS // length
    query_img = query_low.reshape(images, length, HEADS, HEAD_DIM)
    keys_img = keys_low.reshape(images, length, HEADS, HEAD_DIM)
    logits = jnp.einsum("nqhd,nkhd->nhqk", query_img, keys_img, preferred_element_type=jnp.float32)
    return (logits / math.sqrt(HEAD_DIM), query_img, keys_img)


def attend_forward(query_low, keys_low, values_low, length):
    images = ROWS // length
    scores, _, _ = image_scores(query_low, keys_low, length)
    highest = jnp.max(scores, axis=-1, keepdims=True)
    log_total = highest + jnp.log(jnp.sum(jnp.exp(scores - highest), axis=-1, keepdims=True))
    probs = jnp.exp(scores - log_total)
    values_img = values_low.reshape(images, length, HEADS, HEAD_DIM)
    attended = jnp.einsum(
        "nhqk,nkhd->nqhd",
        probs.astype(jnp.bfloat16),
        values_img,
        preferred_element_type=jnp.float32,
    )
    lse_rows = jnp.transpose(log_total[..., 0], (0, 2, 1)).reshape(ROWS, HEADS)
    return (attended.reshape(ROWS, D).astype(jnp.bfloat16), lse_rows)


def attend_backward(query_low, keys_low, values_low, lse_rows, grad_att_low, length):
    images = ROWS // length
    scores, query_img, keys_img = image_scores(query_low, keys_low, length)
    log_total = jnp.transpose(lse_rows.reshape(images, length, HEADS), (0, 2, 1))[..., None]
    probs = jnp.exp(scores - log_total)
    values_img = values_low.reshape(images, length, HEADS, HEAD_DIM)
    grad_img = grad_att_low.reshape(images, length, HEADS, HEAD_DIM)
    grad_values = jnp.einsum(
        "nhqk,nqhd->nkhd", probs.astype(jnp.bfloat16), grad_img, preferred_element_type=jnp.float32
    )
    grad_probs = jnp.einsum(
        "nqhd,nkhd->nhqk", grad_img, values_img, preferred_element_type=jnp.float32
    )
    grad_scores = probs * (grad_probs - jnp.sum(grad_probs * probs, axis=-1, keepdims=True))
    grad_scores_low = grad_scores.astype(jnp.bfloat16)
    grad_query = jnp.einsum(
        "nhqk,nkhd->nqhd", grad_scores_low, keys_img, preferred_element_type=jnp.float32
    ) / math.sqrt(HEAD_DIM)
    grad_keys = jnp.einsum(
        "nhqk,nqhd->nkhd", grad_scores_low, query_img, preferred_element_type=jnp.float32
    ) / math.sqrt(HEAD_DIM)
    return (
        grad_query.reshape(ROWS, D).astype(jnp.bfloat16),
        grad_keys.reshape(ROWS, D).astype(jnp.bfloat16),
        grad_values.reshape(ROWS, D).astype(jnp.bfloat16),
    )


GROUP = 8


def swap(value, bit):
    size = lax.axis_size("dp")
    return lax.ppermute(value, "dp", [(i, i ^ (1 << bit)) for i in range(size)])


def assemble_kernel(half, d_ref, *refs):
    near, far, out, sem = refs[0:5], refs[5:10], refs[10], refs[11]
    copies = []
    for flip, (own, ax, by, a2, b2) in enumerate((near, far)):
        base = d_ref[0] ^ flip
        jobs = (
            (own, out.at[:, base]),
            (ax, out.at[pl.ds(0, half), base ^ 2]),
            (by, out.at[pl.ds(half, half), base ^ 4]),
            (a2.at[0], out.at[pl.ds(0, half), base ^ 4]),
            (a2.at[1], out.at[pl.ds(0, half), base ^ 6]),
            (b2.at[0], out.at[pl.ds(half, half), base ^ 2]),
            (b2.at[1], out.at[pl.ds(half, half), base ^ 6]),
        )
        for source, target in jobs:
            copies.append(pltpu.make_async_copy(source, target, sem.at[len(copies)]))
    for copy in copies:
        copy.start()
    for copy in copies:
        copy.wait()


def gather_rows(shard):
    shards = lax.axis_size("fsdp")
    rows, cols = shard.shape
    part = rows // GROUP
    place = lax.axis_index("dp") % GROUP
    piece = lax.dynamic_slice_in_dim(shard, place * part, part, 0)
    own = lax.all_gather(piece, "fsdp", axis=0, tiled=False)
    half = shards // 2
    top, low = own[:half], own[half:]
    ax, by = swap(top, 1), swap(low, 2)
    a2 = swap(jnp.stack([top, ax]), 2)
    b2 = swap(jnp.stack([low, by]), 1)
    near = (own, ax, by, a2, b2)
    far = tuple(swap(v, 0) for v in near)
    full = pl.pallas_call(
        partial(assemble_kernel, half),
        out_shape=jax.ShapeDtypeStruct((shards, GROUP, part, cols), shard.dtype),
        grid_spec=pltpu.PrefetchScalarGridSpec(
            num_scalar_prefetch=1,
            grid=(1,),
            in_specs=[pl.BlockSpec(memory_space=pl.ANY)] * 10,
            out_specs=pl.BlockSpec(memory_space=pl.ANY),
            scratch_shapes=[pltpu.SemaphoreType.DMA((14,))],
        ),
        name="assemble",
    )(place.astype(jnp.int32).reshape(1), *near, *far)
    return full.reshape(shards * rows, cols)


def gather_native(shard):
    rows = shard.shape[0]
    part = rows // GROUP
    place = lax.axis_index("dp") % GROUP
    piece = lax.dynamic_slice_in_dim(shard, place * part, part, 0)
    own = lax.all_gather(piece, "fsdp", axis=0, tiled=False)
    full = plane_gather(own, axis=1)
    return full.reshape(rows * own.shape[0], shard.shape[1])


def plane_gather(value, axis):
    size = lax.axis_size("dp")
    groups = None
    if size > GROUP:
        groups = [[g * GROUP + i for i in range(GROUP)] for g in range(size // GROUP)]
    return lax.all_gather(value, "dp", axis=axis, tiled=False, axis_index_groups=groups)


def rest_sum(value):
    size = lax.axis_size("dp")
    if size == GROUP:
        return value
    groups = [[g * GROUP + i for g in range(size // GROUP)] for i in range(GROUP)]
    return lax.psum(value, "dp", axis_index_groups=groups)


def pick(value, index, axis):
    return lax.dynamic_index_in_dim(value, index, axis, keepdims=False)


def add_low(left, right):
    return (left.astype(jnp.float32) + right.astype(jnp.float32)).astype(jnp.bfloat16)


def scatter_sum(grad):
    shards = lax.axis_size("fsdp")
    rows, cols = grad.shape
    part = rows // (shards * GROUP)
    half = shards // 2
    place = lax.axis_index("dp") % GROUP
    c, x, y = place & 1, (place >> 1) & 1, place >> 2
    cube = grad.reshape(shards, 2, 2, 2, part, cols)
    got = swap(pick(cube, 1 - c, 3), 0)
    pair = add_low(pick(cube, c, 3), got)
    top, low = pair[:half], pair[half:]
    top_got = swap(pick(top, 1 - x, 2), 1)
    low_got = swap(pick(low, 1 - y, 1), 2)
    top = add_low(pick(top, x, 2), top_got)
    low = add_low(pick(low, y, 1), low_got)
    top_got = swap(pick(top, 1 - y, 1), 2)
    low_got = swap(pick(low, 1 - x, 1), 1)
    top = add_low(pick(top, y, 1), top_got)
    low = add_low(pick(low, x, 1), low_got)
    both = jnp.concatenate([top, low], axis=0).reshape(shards * part, cols)
    piece = lax.psum_scatter(both, "fsdp", scatter_dimension=0, tiled=True)
    piece = rest_sum(piece)
    return plane_gather(piece, axis=0).reshape(GROUP * part, cols).astype(jnp.float32)


def small_sum(value):
    shards = lax.axis_size("fsdp")
    value = value.astype(jnp.bfloat16)
    for bit in range(3):
        value = add_low(value, swap(value, bit))
    value = rest_sum(value)
    me = lax.axis_index("fsdp")
    total = pick(value, me, 0).astype(jnp.float32)
    for step in range(1, shards):
        send = pick(value, (me + step) % shards, 0)
        got = lax.ppermute(send, "fsdp", [(i, (i + step) % shards) for i in range(shards)])
        total = total + got.astype(jnp.float32)
    return total


def per_device(
    tokens,
    output_grad,
    group_member,
    image_counts,
    position_source,
    position_table,
    first_gain,
    first_shift,
    input_proj,
    query_bias,
    value_bias,
    output_proj,
    output_bias,
    second_gain,
    second_shift,
    hidden_weight,
    hidden_bias,
    return_weight,
    return_bias,
):
    dp_size = lax.axis_size("dp")
    fsdp_size = lax.axis_size("fsdp")
    small_parts = (
        first_gain,
        first_shift,
        query_bias,
        value_bias,
        output_bias,
        second_gain,
        second_shift,
        return_bias,
        hidden_bias,
        position_table.reshape(-1),
    )
    sizes = [v.shape[0] for v in small_parts]
    joined = jnp.concatenate(small_parts)
    pad = -joined.shape[0] % 2048
    joined = jnp.pad(joined, (0, pad)).reshape(-1, 128)
    smalls = lax.all_gather(joined, "fsdp", axis=0, tiled=False).reshape(fsdp_size, -1)
    smalls = smalls.astype(jnp.float32)
    offsets = [sum(sizes[:i]) for i in range(len(sizes))]
    vectors = [smalls[:, o : o + n] for o, n in zip(offsets, sizes)]
    (
        gain_one,
        shift_one,
        query_add,
        value_add,
        output_add,
        gain_two,
        shift_two,
        return_add,
        hidden_add,
    ) = [v.reshape(-1) for v in vectors[:9]]
    table_full = (
        vectors[9].reshape(fsdp_size, SMALL_LEN, -1).transpose(1, 0, 2).reshape(SMALL_LEN, D)
    )
    joint_proj = gather_rows(input_proj)
    hidden_full = gather_rows(hidden_weight)
    outproj_full = gather_native(output_proj)
    return_full = gather_rows(return_weight)
    member = group_member[0]
    is_large = member == 1
    length = jnp.where(is_large, LARGE_LEN, SMALL_LEN)
    group_high = dp_size * 7 // 16
    group_low = dp_size - group_high
    counts = image_counts.astype(jnp.float32)
    share = jnp.where(is_large, counts[1], counts[0]) / (counts[0] + counts[1])
    images = jnp.where(
        is_large,
        group_high * fsdp_size * (ROWS // LARGE_LEN),
        group_low * fsdp_size * (ROWS // SMALL_LEN),
    ).astype(jnp.float32)
    factor = share / images

    def weight_grad(left, right):
        product = lax.dot_general(
            left, right, (((0,), (0,)), ((), ())), preferred_element_type=jnp.float32
        )
        return scatter_sum((product * factor).astype(jnp.bfloat16))

    row_index = jnp.arange(ROWS, dtype=jnp.int32)
    place = row_index % length
    inter = interp_table(position_source)
    identity = (
        jnp.arange(LARGE_LEN, dtype=jnp.int32)[:, None]
        == jnp.arange(SMALL_LEN, dtype=jnp.int32)[None, :]
    ).astype(jnp.float32)
    mixing = jnp.where(is_large, inter, identity)
    picker = (place[:, None] == jnp.arange(LARGE_LEN, dtype=jnp.int32)[None, :]).astype(jnp.float32)
    spread = jnp.dot(picker, mixing, precision=lax.Precision.HIGHEST)
    position = jnp.dot(spread, table_full, precision=lax.Precision.HIGHEST)
    stream = tokens.astype(jnp.float32) + position
    first_out, first_hat, first_inv = layer_norm(stream, gain_one, shift_one)
    first_low = first_out.astype(jnp.bfloat16)
    joint_add = jnp.concatenate([query_add, jnp.zeros_like(query_add), value_add])
    projected = jnp.dot(first_low, joint_proj, preferred_element_type=jnp.float32)
    projected = (projected + joint_add).astype(jnp.bfloat16)
    query_low = projected[:, :D]
    keys_low = projected[:, D : 2 * D]
    values_low = projected[:, 2 * D :]
    attended_low, lse_rows = lax.cond(
        is_large,
        partial(attend_forward, length=LARGE_LEN),
        partial(attend_forward, length=SMALL_LEN),
        query_low,
        keys_low,
        values_low,
    )
    mid = stream + jnp.dot(attended_low, outproj_full, preferred_element_type=jnp.float32) + output_add
    second_out, second_hat, second_inv = layer_norm(mid, gain_two, shift_two)
    second_low = second_out.astype(jnp.bfloat16)
    hidden_pre = jnp.dot(second_low, hidden_full, preferred_element_type=jnp.float32) + hidden_add
    activ, gelu_back = jax.vjp(partial(jax.nn.gelu, approximate=False), hidden_pre)
    activ_low = activ.astype(jnp.bfloat16)
    return_w_out = weight_grad(activ_low, output_grad)
    returned = jnp.dot(activ_low, return_full, preferred_element_type=jnp.float32) + return_add
    block_out = (mid + returned).astype(jnp.bfloat16)
    grad_out = output_grad.astype(jnp.float32)
    grad_return_add = jnp.sum(grad_out, axis=0)
    grad_activ = jnp.einsum(
        "rd,fd->rf", output_grad, return_full, preferred_element_type=jnp.float32
    )
    grad_hidden_low = gelu_back(grad_activ)[0].astype(jnp.bfloat16)
    hidden_w_out = weight_grad(second_low, grad_hidden_low)
    grad_hidden_add = jnp.sum(grad_hidden_low.astype(jnp.float32), axis=0)
    grad_second = jnp.einsum(
        "rf,df->rd", grad_hidden_low, hidden_full, preferred_element_type=jnp.float32
    )
    grad_mid_norm, grad_gain_two, grad_shift_two = norm_back(
        grad_second, second_hat, second_inv, gain_two
    )
    grad_mid = grad_out + grad_mid_norm
    grad_branch_low = grad_mid.astype(jnp.bfloat16)
    outproj_out = weight_grad(attended_low, grad_branch_low)
    grad_output_add = jnp.sum(grad_branch_low.astype(jnp.float32), axis=0)
    grad_attended = jnp.einsum(
        "re,de->rd", grad_branch_low, outproj_full, preferred_element_type=jnp.float32
    )
    grad_att_low = grad_attended.astype(jnp.bfloat16)
    grad_query_low, grad_keys_low, grad_values_low = lax.cond(
        is_large,
        partial(attend_backward, length=LARGE_LEN),
        partial(attend_backward, length=SMALL_LEN),
        query_low,
        keys_low,
        values_low,
        lse_rows,
        grad_att_low,
    )
    grad_joint_low = jnp.concatenate([grad_query_low, grad_keys_low, grad_values_low], axis=1)
    joint_out = weight_grad(first_low, grad_joint_low)
    grad_query_add = jnp.sum(grad_query_low.astype(jnp.float32), axis=0)
    grad_value_add = jnp.sum(grad_values_low.astype(jnp.float32), axis=0)
    grad_first = jnp.einsum(
        "re,de->rd", grad_joint_low, joint_proj, preferred_element_type=jnp.float32
    )
    grad_stream_norm, grad_gain_one, grad_shift_one = norm_back(
        grad_first, first_hat, first_inv, gain_one
    )
    grad_stream = grad_mid + grad_stream_norm
    tokens_grad = grad_stream.astype(jnp.bfloat16)
    grad_table = jnp.dot(spread.T, grad_stream, precision=lax.Precision.HIGHEST)
    table_rows = grad_table.reshape(SMALL_LEN, fsdp_size, -1).transpose(1, 0, 2)
    small_grads = (
        grad_gain_one,
        grad_shift_one,
        grad_query_add,
        grad_value_add,
        grad_output_add,
        grad_gain_two,
        grad_shift_two,
        grad_return_add,
        grad_hidden_add,
        table_rows,
    )
    packed = jnp.concatenate([v.reshape(fsdp_size, -1) for v in small_grads], axis=1) * factor
    packed = jnp.pad(packed, ((0, 0), (0, pad))).reshape(fsdp_size, -1, 128)
    summed = small_sum(packed).reshape(-1)
    small_outs = [summed[o : o + n] for o, n in zip(offsets, sizes)]
    return (
        block_out,
        tokens_grad,
        small_outs[9].reshape(SMALL_LEN, -1),
        small_outs[0],
        small_outs[1],
        joint_out,
        small_outs[2],
        small_outs[3],
        outproj_out,
        small_outs[4],
        small_outs[5],
        small_outs[6],
        hidden_w_out,
        small_outs[8],
        return_w_out,
        small_outs[7],
    )


def solution(mesh):
    in_specs = (
        P(("dp", "fsdp"), None),
        P(("dp", "fsdp"), None),
        P("dp"),
        P(),
        P(),
        P(None, "fsdp"),
        P("fsdp"),
        P("fsdp"),
        P("fsdp", None),
        P("fsdp"),
        P("fsdp"),
        P("fsdp", None),
        P("fsdp"),
        P("fsdp"),
        P("fsdp"),
        P("fsdp", None),
        P("fsdp"),
        P("fsdp", None),
        P("fsdp"),
    )
    out_specs = (
        P(("dp", "fsdp"), None),
        P(("dp", "fsdp"), None),
        P(None, "fsdp"),
        P("fsdp"),
        P("fsdp"),
        P("fsdp", None),
        P("fsdp"),
        P("fsdp"),
        P("fsdp", None),
        P("fsdp"),
        P("fsdp"),
        P("fsdp"),
        P("fsdp", None),
        P("fsdp"),
        P("fsdp", None),
        P("fsdp"),
    )
    return jax.shard_map(
        per_device, mesh=mesh, in_specs=in_specs, out_specs=out_specs, check_vma=False
    )
```

```python
from functools import partial

import jax
import jax.numpy as jnp
from jax import lax
from jax.experimental import pallas as pl
from jax.experimental.pallas import tpu as pltpu
from jax.sharding import PartitionSpec as P

D = 1024
HEADS = 16
HEAD_DIM = 64
SG = 7
LG = 12
SMALL_LEN = 50
LARGE_LEN = 145
ROWS = 1450
PAD = 1472
GROUP = 8
WINDOW = 176
WINDOWS = 10
PAIRS = 4
FAR = -1e30
LOW = jnp.bfloat16


EPS = 1e-06


def grid_fraction(index):
    scaled = jnp.maximum((2 * index + 1) * SG - LG, 0)
    lower = scaled // (2 * LG)
    return (scaled - 2 * LG * lower).astype(jnp.float32) / (2.0 * LG)


def interp_table(position_source):
    position = jnp.arange(LARGE_LEN, dtype=jnp.int32)
    patch = jnp.maximum(position - 1, 0)
    frac_row = grid_fraction(patch // LG)
    frac_col = grid_fraction(patch % LG)
    weights = jnp.stack(
        [
            (1.0 - frac_row) * (1.0 - frac_col),
            (1.0 - frac_row) * frac_col,
            frac_row * (1.0 - frac_col),
            frac_row * frac_col,
        ],
        axis=1,
    )
    class_row = (jnp.arange(4, dtype=jnp.int32) == 0).astype(jnp.float32)
    weights = jnp.where((position == 0)[:, None], class_row[None, :], weights)
    onehot = (
        position_source[:, :, None] == jnp.arange(SMALL_LEN, dtype=jnp.int32)[None, None, :]
    ).astype(jnp.float32)
    return jnp.sum(weights[:, :, None] * onehot, axis=1)


def layer_norm(values, gain, shift):
    average = jnp.mean(values, axis=-1, keepdims=True)
    centred = values - average
    variance = jnp.mean(centred * centred, axis=-1, keepdims=True)
    inv_std = lax.rsqrt(variance + EPS)
    normed = centred * inv_std
    return (normed * gain + shift, normed, inv_std)


def norm_back(grad_norm, normed, inv_std, gain):
    scaled = grad_norm * gain
    inner = (
        scaled
        - jnp.mean(scaled, axis=-1, keepdims=True)
        - normed * jnp.mean(scaled * normed, axis=-1, keepdims=True)
    )
    return (inv_std * inner, jnp.sum(grad_norm * normed, axis=0), jnp.sum(grad_norm, axis=0))

def dot_nt(left, right):
    return lax.dot_general(
        left, right, (((1,), (1,)), ((), ())), preferred_element_type=jnp.float32
    )


def dot_nn(left, right):
    return lax.dot_general(
        left, right, (((1,), (0,)), ((), ())), preferred_element_type=jnp.float32
    )


def dot_tn(left, right):
    return lax.dot_general(
        left, right, (((0,), (0,)), ((), ())), preferred_element_type=jnp.float32
    )


def after(value, *others):
    return lax.optimization_barrier((value, *others))[0]


def window_start(window, step):
    return pl.multiple_of(jnp.minimum(window * step // 16 * 16, PAD - WINDOW), 16)


def image_of(row, length, step):
    image = jnp.where(row >= length, 1, 0) + jnp.where(row >= 2 * length, 1, 0)
    return jnp.where(row < 0, -1, jnp.where(row >= step, 3, image))


def fill_masks(mask_ref, length, step):
    def one(window, carry):
        base = window_start(window, step) - window * step
        shape = (WINDOW, WINDOW)
        rows = image_of(lax.broadcasted_iota(jnp.int32, shape, 0) + base, length, step)
        cols = image_of(lax.broadcasted_iota(jnp.int32, shape, 1) + base, length, step)
        mask_ref[window] = jnp.where(rows == cols, 0.0, FAR).astype(jnp.float32)
        return carry

    lax.fori_loop(0, WINDOWS, one, 0)


def split_heads(value):
    lane = lax.broadcasted_iota(jnp.int32, value.shape, 1)
    zero = jnp.zeros_like(value)
    return jnp.where(lane < HEAD_DIM, value, zero), jnp.where(lane < HEAD_DIM, zero, value)


def slabs(ref, at):
    return [ref[at, 128 * i : 128 * i + 128] for i in range(PAIRS)]


def join_heads(even, odd):
    lane = lax.broadcasted_iota(jnp.int32, even.shape, 1)
    return jnp.where(lane < HEAD_DIM, even, odd)


def keep_rows(ref, start, first, value):
    row = lax.broadcasted_iota(jnp.int32, value.shape, 0) + start
    value = jnp.where(row < ROWS, value, 0.0)
    at = pl.ds(start, WINDOW)
    old = ref[at, :].astype(jnp.float32)
    ref[at, :] = jnp.where(row >= first, value, old).astype(ref.dtype)


def forward_kernel(s_ref, q_ref, k_ref, v_ref, o_ref, mask_ref):
    length, step = s_ref[0], s_ref[1]

    @pl.when(pl.program_id(0) == 0)
    def _():
        fill_masks(mask_ref, length, step)

    def one(window, carry):
        start = window_start(window, step)
        at = pl.ds(start, WINDOW)
        query = [h for v in slabs(q_ref, at) for h in split_heads(v * LOW(0.125))]
        keys, values = slabs(k_ref, at), slabs(v_ref, at)
        mask = mask_ref[window]
        each = range(2 * PAIRS)
        scores = [dot_nt(query[i], keys[i // 2]) + mask for i in each]
        top = [jnp.max(v, axis=1, keepdims=True) for v in scores]
        raised = [jnp.exp(scores[i] - top[i]) for i in each]
        total = [jnp.sum(v, axis=1, keepdims=True) for v in raised]
        out = [dot_nn(raised[i].astype(LOW), values[i // 2]) for i in each]
        out = [out[i] * (1.0 / total[i]) for i in each]
        for j in range(PAIRS):
            piece = join_heads(out[2 * j], out[2 * j + 1])
            keep_rows(o_ref.at[:, 128 * j : 128 * j + 128], start, window * step, piece)
        return carry

    lax.fori_loop(0, WINDOWS, one, 0)


def backward_kernel(s_ref, q_ref, k_ref, v_ref, g_ref, out_ref, mask_ref):
    length, step = s_ref[0], s_ref[1]
    fill_masks(mask_ref, length, step)

    def one(window, carry):
        start = window_start(window, step)
        at = pl.ds(start, WINDOW)
        query = [h for v in slabs(q_ref, at) for h in split_heads(v * LOW(0.125))]
        grad = [h for v in slabs(g_ref, at) for h in split_heads(v)]
        keys, values = slabs(k_ref, at), slabs(v_ref, at)
        mask = mask_ref[window]
        each = range(2 * PAIRS)
        scores = [dot_nt(keys[i // 2], query[i]) + mask for i in each]
        grad_probs = [dot_nt(values[i // 2], grad[i]) for i in each]
        top = [jnp.max(v, axis=0, keepdims=True) for v in scores]
        raised = [jnp.exp(scores[i] - top[i]) for i in each]
        scale = [1.0 / jnp.sum(v, axis=0, keepdims=True) for v in raised]
        probs = [raised[i] * scale[i] for i in each]
        inner = [jnp.sum(grad_probs[i] * probs[i], axis=0, keepdims=True) for i in each]
        grad_scores = [(probs[i] * (grad_probs[i] - inner[i])).astype(LOW) for i in each]
        grad_v = [dot_nn(probs[i].astype(LOW), grad[i]) for i in each]
        grad_k = [dot_nn(grad_scores[i], query[i]) for i in each]
        grad_q = [dot_tn(grad_scores[i], keys[i // 2]) for i in each]
        for j in range(PAIRS):
            cols = slice(128 * j, 128 * j + 128)
            first = window * step
            both = join_heads(grad_q[2 * j], grad_q[2 * j + 1]) * 0.125
            keep_rows(out_ref.at[0, :, cols], start, first, both)
            keep_rows(out_ref.at[1, :, cols], start, first, grad_k[2 * j] + grad_k[2 * j + 1])
            keep_rows(out_ref.at[2, :, cols], start, first, grad_v[2 * j] + grad_v[2 * j + 1])
        return carry

    lax.fori_loop(0, WINDOWS, one, 0)


def attend_forward(lengths, projected):
    width = 128 * PAIRS
    blocks = D // width

    def part(base):
        return pl.BlockSpec((PAD, width), lambda h, s: (0, h + base))

    return pl.pallas_call(
        forward_kernel,
        out_shape=jax.ShapeDtypeStruct((PAD, D), LOW),
        grid_spec=pltpu.PrefetchScalarGridSpec(
            num_scalar_prefetch=1,
            grid=(blocks,),
            in_specs=[part(0), part(blocks), part(2 * blocks)],
            out_specs=part(0),
            scratch_shapes=[pltpu.VMEM((WINDOWS, WINDOW, WINDOW), jnp.float32)],
        ),
        name="attend_forward",
    )(lengths, projected, projected, projected)


def attend_backward(numbers, projected, grad):
    width = 128 * PAIRS
    blocks = D // width

    def part(base):
        return pl.BlockSpec((PAD, width), lambda i, s: (0, s[2] + base))

    return pl.pallas_call(
        backward_kernel,
        out_shape=jax.ShapeDtypeStruct((3, PAD, width), LOW),
        grid_spec=pltpu.PrefetchScalarGridSpec(
            num_scalar_prefetch=1,
            grid=(1,),
            in_specs=[part(0), part(blocks), part(2 * blocks), part(0)],
            out_specs=pl.BlockSpec((3, PAD, width), lambda i, s: (0, 0, 0)),
            scratch_shapes=[pltpu.VMEM((WINDOWS, WINDOW, WINDOW), jnp.float32)],
        ),
        name="attend_backward",
    )(numbers, projected, projected, projected, grad)


def hidden_kernel(rows, x_ref, w_ref, b_ref, activ_ref, slope_ref):
    for i in range(PAD // rows):
        at = slice(i * rows, (i + 1) * rows)
        hidden = dot_nn(x_ref[at, :], w_ref[...]) + b_ref[...]
        cdf = 0.5 * lax.erf(hidden * 0.7071067811865476) + 0.5
        density = jnp.exp(-0.5 * hidden * hidden) * 0.3989422804014327
        activ_ref[at, :] = (hidden * cdf).astype(LOW)
        slope_ref[at, :] = (cdf + hidden * density).astype(LOW)


def hidden_layer(second, weight, bias):
    width = weight.shape[1]
    tile = 512
    return pl.pallas_call(
        partial(hidden_kernel, 184),
        out_shape=[jax.ShapeDtypeStruct((PAD, width), LOW)] * 2,
        grid=(width // tile,),
        in_specs=[
            pl.BlockSpec((PAD, D), lambda n: (0, 0)),
            pl.BlockSpec((D, tile), lambda n: (0, n)),
            pl.BlockSpec((1, tile), lambda n: (0, n)),
        ],
        out_specs=[pl.BlockSpec((PAD, tile), lambda n: (0, n))] * 2,
        name="hidden_layer",
    )(second, weight, bias.reshape(1, width))


def hidden_back_kernel(rows, g_ref, w_ref, slope_ref, out_ref, sum_ref):
    total = jnp.zeros_like(sum_ref)
    for i in range(PAD // rows):
        at = slice(i * rows, (i + 1) * rows)
        grad = dot_nt(g_ref[at, :], w_ref[...]) * slope_ref[at, :].astype(jnp.float32)
        grad = grad.astype(LOW)
        out_ref[at, :] = grad
        total = total + jnp.sum(grad.astype(jnp.float32), axis=0, keepdims=True)
    sum_ref[...] = total


def hidden_back(grad, weight, slope):
    width = weight.shape[0]
    tile = 512
    return pl.pallas_call(
        partial(hidden_back_kernel, 368),
        out_shape=[
            jax.ShapeDtypeStruct((PAD, width), LOW),
            jax.ShapeDtypeStruct((1, width), jnp.float32),
        ],
        grid=(width // tile,),
        in_specs=[
            pl.BlockSpec((PAD, D), lambda n: (0, 0)),
            pl.BlockSpec((tile, D), lambda n: (n, 0)),
            pl.BlockSpec((PAD, tile), lambda n: (0, n)),
        ],
        out_specs=[
            pl.BlockSpec((PAD, tile), lambda n: (0, n)),
            pl.BlockSpec((1, tile), lambda n: (0, n)),
        ],
        name="hidden_back",
    )(grad, weight, slope)


def grad_kernel(c_ref, f_ref, a_ref, b_ref, *refs):
    out_ref = refs[-1]
    right = b_ref[...].reshape(b_ref.shape[-2:])
    value = dot_tn(a_ref[...], right) * f_ref[0]
    if len(refs) == 2:
        value = value + refs[0][...].astype(jnp.float32)
    out_ref[...] = value.astype(LOW)


def grad_half(core, factor, left, right, got=None, tile_m=512, tile_n=512):
    rows = left.shape[1]
    stacked = right.ndim == 3
    cols = 3 * right.shape[2] if stacked else right.shape[1] // 2
    steps = cols // tile_n
    in_specs = [
        pl.BlockSpec(memory_space=pltpu.SMEM),
        pl.BlockSpec((PAD, tile_m), lambda m, n, c: (0, m)),
    ]
    if stacked:
        in_specs.append(pl.BlockSpec((1, PAD, tile_n), lambda m, n, c: (n, 0, 0)))
    else:
        in_specs.append(pl.BlockSpec((PAD, tile_n), lambda m, n, c: (0, n + c[0] * steps)))
    out_spec = pl.BlockSpec((tile_m, tile_n), lambda m, n, c: (m, n))
    operands = [core, factor, left, right]
    if got is not None:
        in_specs.append(out_spec)
        operands.append(got)
    return pl.pallas_call(
        grad_kernel,
        out_shape=jax.ShapeDtypeStruct((rows, cols), LOW),
        grid_spec=pltpu.PrefetchScalarGridSpec(
            num_scalar_prefetch=1,
            grid=(rows // tile_m, steps),
            in_specs=in_specs,
            out_specs=out_spec,
        ),
        name="grad_keep" if got is not None else "grad_send",
    )(*operands)


def swap(value, bit):
    size = lax.axis_size("dp")
    return lax.ppermute(value, "dp", [(i, i ^ (1 << bit)) for i in range(size)])


def assemble_kernel(half, d_ref, *refs):
    near, far, out, held, sem = refs[0:5], refs[5:10], refs[10], refs[11], refs[12]
    copies = []
    for flip, (own, ax, by, a2, b2) in enumerate((near, far)):
        base = d_ref[0] ^ flip
        jobs = (
            (own, held.at[:, base]),
            (ax, held.at[pl.ds(0, half), base ^ 2]),
            (by, held.at[pl.ds(half, half), base ^ 4]),
            (a2.at[0], held.at[pl.ds(0, half), base ^ 4]),
            (a2.at[1], held.at[pl.ds(0, half), base ^ 6]),
            (b2.at[0], held.at[pl.ds(half, half), base ^ 2]),
            (b2.at[1], held.at[pl.ds(half, half), base ^ 6]),
        )
        for source, target in jobs:
            copies.append(pltpu.make_async_copy(source, target, sem.at[len(copies)]))
    for copy in copies:
        copy.start()
    for copy in copies:
        copy.wait()
    last = pltpu.make_async_copy(held, out, sem.at[0])
    last.start()
    last.wait()


def gather_piece(shard):
    part = shard.shape[0] // GROUP
    place = lax.axis_index("dp") % GROUP
    piece = lax.dynamic_slice_in_dim(shard, place * part, part, 0)
    return lax.all_gather(piece, "fsdp", axis=0, tiled=False)


def gather_first(own):
    half = own.shape[0] // 2
    return swap(own[:half], 1), swap(own[half:], 2)


def gather_second(own, ax, by):
    half = own.shape[0] // 2
    return swap(jnp.stack([own[:half], ax]), 2), swap(jnp.stack([own[half:], by]), 1)


def gather_last(own, ax, by, a2, b2):
    shards, part, cols = own.shape
    place = lax.axis_index("dp") % GROUP
    near = (own, ax, by, a2, b2)
    far = tuple(swap(v, 0) for v in near)
    full = pl.pallas_call(
        partial(assemble_kernel, shards // 2),
        out_shape=jax.ShapeDtypeStruct((shards, GROUP, part, cols), own.dtype),
        grid_spec=pltpu.PrefetchScalarGridSpec(
            num_scalar_prefetch=1,
            grid=(1,),
            in_specs=[pl.BlockSpec(memory_space=pl.ANY)] * 10,
            out_specs=pl.BlockSpec(memory_space=pl.ANY),
            scratch_shapes=[
                pltpu.VMEM((shards, GROUP, part, cols), own.dtype),
                pltpu.SemaphoreType.DMA((14,)),
            ],
        ),
        name="assemble",
    )(place.astype(jnp.int32).reshape(1), *near, *far)
    return full.reshape(shards * GROUP * part, cols)


def plane_gather(value, axis):
    size = lax.axis_size("dp")
    groups = None
    if size > GROUP:
        groups = [[g * GROUP + i for i in range(GROUP)] for g in range(size // GROUP)]
    return lax.all_gather(value, "dp", axis=axis, tiled=False, axis_index_groups=groups)


def rest_sum(value):
    size = lax.axis_size("dp")
    if size == GROUP:
        return value
    groups = [[g * GROUP + i for g in range(size // GROUP)] for i in range(GROUP)]
    return lax.psum(value, "dp", axis_index_groups=groups)


def pick(value, index, axis):
    return lax.dynamic_index_in_dim(value, index, axis, keepdims=False)


def add_low(left, right):
    return (left.astype(jnp.float32) + right.astype(jnp.float32)).astype(LOW)


def axes():
    place = lax.axis_index("dp") % GROUP
    return (place >> 1) & 1, place >> 2


def sum_first(pair):
    shards = lax.axis_size("fsdp")
    rows, cols = pair.shape
    cube = pair.reshape(shards, 2, 2, rows // shards // 4, cols)
    x, y = axes()
    half = shards // 2
    top, low = cube[:half], cube[half:]
    return top, low, swap(pick(top, 1 - x, 2), 1), swap(pick(low, 1 - y, 1), 2)


def sum_second(top, low, top_got, low_got):
    x, y = axes()
    top = add_low(pick(top, x, 2), top_got)
    low = add_low(pick(low, y, 1), low_got)
    return top, low, swap(pick(top, 1 - y, 1), 2), swap(pick(low, 1 - x, 1), 1)


def sum_third(top, low, top_got, low_got):
    x, y = axes()
    top = add_low(pick(top, y, 1), top_got)
    low = add_low(pick(low, x, 1), low_got)
    both = jnp.concatenate([top, low], axis=0)
    shards, part, cols = both.shape
    piece = lax.psum_scatter(
        both.reshape(shards * part, cols), "fsdp", scatter_dimension=0, tiled=True
    )
    return rest_sum(piece)


def sum_last(piece, blocks):
    part, cols = piece.shape
    every = plane_gather(piece, axis=0).reshape(4, 2, part, blocks, cols // blocks)
    every = every.transpose(0, 2, 3, 1, 4)
    return every.reshape(4 * part, 2 * cols).astype(jnp.float32)


def small_sum(value):
    shards = lax.axis_size("fsdp")
    value = value.astype(LOW)
    for bit in range(3):
        value = add_low(value, swap(value, bit))
    value = rest_sum(value)
    me = lax.axis_index("fsdp")
    total = pick(value, me, 0).astype(jnp.float32)
    for step in range(1, shards):
        send = pick(value, (me + step) % shards, 0)
        got = lax.ppermute(send, "fsdp", [(i, (i + step) % shards) for i in range(shards)])
        total = total + got.astype(jnp.float32)
    return total


def per_device(
    tokens,
    output_grad,
    group_member,
    image_counts,
    position_source,
    position_table,
    first_gain,
    first_shift,
    input_proj,
    query_bias,
    value_bias,
    output_proj,
    output_bias,
    second_gain,
    second_shift,
    hidden_weight,
    hidden_bias,
    return_weight,
    return_bias,
):
    dp_size = lax.axis_size("dp")
    fsdp_size = lax.axis_size("fsdp")
    core = (lax.axis_index("dp") & 1).astype(jnp.int32)
    mine, other = core.reshape(1), (1 - core).reshape(1)
    small_parts = (
        first_gain,
        first_shift,
        query_bias,
        value_bias,
        output_bias,
        second_gain,
        second_shift,
        return_bias,
        hidden_bias,
        position_table.reshape(-1),
    )
    sizes = [v.shape[0] for v in small_parts]
    joined = jnp.concatenate(small_parts)
    pad = -joined.shape[0] % 2048
    joined = jnp.pad(joined, (0, pad)).reshape(-1, 128)
    joint_own = gather_piece(input_proj)
    smalls = lax.all_gather(joined, "fsdp", axis=0, tiled=False).reshape(fsdp_size, -1)
    smalls = smalls.astype(jnp.float32)
    offsets = [sum(sizes[:i]) for i in range(len(sizes))]
    vectors = [smalls[:, o : o + n] for o, n in zip(offsets, sizes)]
    (
        gain_one,
        shift_one,
        query_add,
        value_add,
        output_add,
        gain_two,
        shift_two,
        return_add,
        hidden_add,
    ) = [v.reshape(-1) for v in vectors[:9]]
    table_full = (
        vectors[9].reshape(fsdp_size, SMALL_LEN, -1).transpose(1, 0, 2).reshape(SMALL_LEN, D)
    )
    member = group_member[0]
    is_large = member == 1
    length = jnp.where(is_large, LARGE_LEN, SMALL_LEN)
    step = jnp.where(is_large, LARGE_LEN, 3 * SMALL_LEN)
    group_high = dp_size * 7 // 16
    group_low = dp_size - group_high
    counts = image_counts.astype(jnp.float32)
    share = jnp.where(is_large, counts[1], counts[0]) / (counts[0] + counts[1])
    images = jnp.where(
        is_large,
        group_high * fsdp_size * (ROWS // LARGE_LEN),
        group_low * fsdp_size * (ROWS // SMALL_LEN),
    ).astype(jnp.float32)
    factor = share / images
    scale = factor.reshape(1)

    row_index = jnp.arange(PAD, dtype=jnp.int32)
    place = row_index % length
    inter = interp_table(position_source)
    identity = (
        jnp.arange(LARGE_LEN, dtype=jnp.int32)[:, None]
        == jnp.arange(SMALL_LEN, dtype=jnp.int32)[None, :]
    ).astype(jnp.float32)
    mixing = jnp.where(is_large, inter, identity)
    picker = (place[:, None] == jnp.arange(LARGE_LEN, dtype=jnp.int32)[None, :]).astype(jnp.float32)
    spread = jnp.dot(picker, mixing, precision=lax.Precision.HIGHEST)
    position = jnp.dot(spread, table_full, precision=lax.Precision.HIGHEST)
    grad_pad = jnp.pad(output_grad, ((0, PAD - ROWS), (0, 0)))
    stream = jnp.pad(tokens, ((0, PAD - ROWS), (0, 0))).astype(jnp.float32) + position
    first_out, first_hat, first_inv = layer_norm(stream, gain_one, shift_one)
    first_low = first_out.astype(LOW)

    ax, by = gather_first(joint_own)
    a2, b2 = gather_second(joint_own, ax, by)
    outer_own = gather_piece(after(jnp.concatenate([output_proj, hidden_weight], axis=1), joint_own))
    joint_proj = gather_last(joint_own, ax, by, a2, b2)

    first_low = after(first_low, outer_own)
    outer_ax, outer_by = gather_first(outer_own)
    return_own = gather_piece(after(return_weight, outer_own))
    joint_add = jnp.concatenate([query_add, jnp.zeros_like(query_add), value_add])
    projected = jnp.dot(first_low, joint_proj, preferred_element_type=jnp.float32)
    projected = (projected + joint_add).astype(LOW)
    projected = after(projected, outer_ax, outer_by)
    outer_a2, outer_b2 = gather_second(outer_own, outer_ax, outer_by)
    attended = attend_forward(jnp.stack([length, step]), projected)
    attended = after(attended, outer_a2, outer_b2, return_own)
    return_ax, return_by = gather_first(return_own)
    outer = gather_last(outer_own, outer_ax, outer_by, outer_a2, outer_b2)
    outproj_full, hidden_full = outer[:, :D], outer[:, D:]
    mid = stream + jnp.dot(attended, outproj_full, preferred_element_type=jnp.float32) + output_add
    second_out, second_hat, second_inv = layer_norm(mid, gain_two, shift_two)
    second_low = second_out.astype(LOW)
    second_low = after(second_low, return_ax, return_by)
    return_a2, return_b2 = gather_second(return_own, return_ax, return_by)
    activ, slope = hidden_layer(second_low, hidden_full, hidden_add)
    activ, slope, return_a2, return_b2 = lax.optimization_barrier(
        (activ, slope, return_a2, return_b2)
    )
    return_full = gather_last(return_own, return_ax, return_by, return_a2, return_b2)

    return_send = grad_half(other, scale, activ, grad_pad)
    return_got = swap(return_send, 0)
    grad_hidden, grad_hidden_add = hidden_back(after(grad_pad, return_send), return_full, slope)
    return_pair = grad_half(mine, scale, activ, after(grad_pad, grad_hidden), return_got)
    return_one = sum_first(return_pair)

    hidden_send = grad_half(other, scale, after(second_low, return_pair), grad_hidden, tile_m=1024)
    hidden_got = swap(hidden_send, 0)
    hidden_pair = grad_half(
        mine, scale, after(second_low, hidden_send), grad_hidden, hidden_got, tile_m=1024
    )
    grad_hidden = after(grad_hidden, hidden_pair, *return_one)
    return_two = sum_second(*return_one)
    hidden_one = sum_first(hidden_pair)
    grad_second = dot_nt(grad_hidden, hidden_full)
    grad_mid_norm, grad_gain_two, grad_shift_two = norm_back(
        grad_second, second_hat, second_inv, gain_two
    )
    grad_mid = grad_pad.astype(jnp.float32) + grad_mid_norm
    grad_branch = grad_mid.astype(LOW)
    grad_output_add = jnp.sum(grad_branch.astype(jnp.float32), axis=0)
    grad_branch = after(grad_branch, *return_two)
    return_piece = sum_third(*return_two)
    output_send = grad_half(other, scale, attended, grad_branch)
    output_got = swap(output_send, 0)
    grad_att = dot_nt(after(grad_branch, output_send), outproj_full).astype(LOW)
    output_pair = grad_half(mine, scale, attended, after(grad_branch, grad_att), output_got)
    grad_att = after(grad_att, output_pair, *hidden_one)
    hidden_two = sum_second(*hidden_one)
    output_one = sum_first(output_pair)
    numbers = jnp.stack([length, step, 1 - core])
    heads_other = attend_backward(numbers, projected, grad_att)
    joint_send = grad_half(other, scale, first_low, heads_other, tile_m=1024)
    joint_got = swap(joint_send, 0)
    grad_att = after(grad_att, joint_send, *hidden_two, *output_one, return_piece)
    hidden_piece = sum_third(*hidden_two)
    output_two = sum_second(*output_one)
    return_w_out = sum_last(return_piece, 1)
    numbers = jnp.stack([length, step, core])
    heads_mine = attend_backward(numbers, projected, grad_att)
    joint_pair = grad_half(
        mine, scale, first_low, after(heads_mine, *output_two), joint_got, tile_m=1024
    )
    joint_one = sum_first(joint_pair)
    output_piece = sum_third(*output_two)
    heads_other = after(heads_other, joint_pair)
    low_heads = jnp.where(core == 0, heads_mine, heads_other)
    high_heads = jnp.where(core == 0, heads_other, heads_mine)
    grad_first = 0.0
    for i in range(3):
        base = i * D
        grad_first = grad_first + dot_nt(low_heads[i], joint_proj[:, base : base + 512])
        grad_first = grad_first + dot_nt(high_heads[i], joint_proj[:, base + 512 : base + D])
    head_sums = [
        jnp.concatenate([jnp.sum(h[i].astype(jnp.float32), axis=0) for h in (low_heads, high_heads)])
        for i in (0, 2)
    ]
    grad_query_add, grad_value_add = head_sums
    grad_stream_norm, grad_gain_one, grad_shift_one = norm_back(
        grad_first, first_hat, first_inv, gain_one
    )
    grad_stream = grad_mid + grad_stream_norm
    tokens_grad = grad_stream[:ROWS].astype(LOW)
    in_rows = (row_index < ROWS)[:, None]
    grad_table = jnp.dot(
        jnp.where(in_rows, spread, 0.0).T, grad_stream, precision=lax.Precision.HIGHEST
    )
    activ = after(activ, grad_stream, *joint_one)
    joint_two = sum_second(*joint_one)
    hidden_w_out = sum_last(hidden_piece, 1)
    outproj_out = sum_last(output_piece, 1)
    returned = jnp.dot(activ, return_full, preferred_element_type=jnp.float32) + return_add
    block_out = (mid + returned)[:ROWS].astype(LOW)
    joint_piece = sum_third(*joint_two)
    joint_out = sum_last(joint_piece, 3)
    grad_return_add = jnp.sum(output_grad.astype(jnp.float32), axis=0)
    table_rows = grad_table.reshape(SMALL_LEN, fsdp_size, -1).transpose(1, 0, 2)
    small_grads = (
        grad_gain_one,
        grad_shift_one,
        grad_query_add,
        grad_value_add,
        grad_output_add,
        grad_gain_two,
        grad_shift_two,
        grad_return_add,
        grad_hidden_add,
        table_rows,
    )
    packed = jnp.concatenate([v.reshape(fsdp_size, -1) for v in small_grads], axis=1) * factor
    packed = jnp.pad(packed, ((0, 0), (0, pad))).reshape(fsdp_size, -1, 128)
    summed = small_sum(packed).reshape(-1)
    small_outs = [summed[o : o + n] for o, n in zip(offsets, sizes)]
    return (
        block_out,
        tokens_grad,
        small_outs[9].reshape(SMALL_LEN, -1),
        small_outs[0],
        small_outs[1],
        joint_out,
        small_outs[2],
        small_outs[3],
        outproj_out,
        small_outs[4],
        small_outs[5],
        small_outs[6],
        hidden_w_out,
        small_outs[8],
        return_w_out,
        small_outs[7],
    )


def solution(mesh):
    in_specs = (
        P(("dp", "fsdp"), None),
        P(("dp", "fsdp"), None),
        P("dp"),
        P(),
        P(),
        P(None, "fsdp"),
        P("fsdp"),
        P("fsdp"),
        P("fsdp", None),
        P("fsdp"),
        P("fsdp"),
        P("fsdp", None),
        P("fsdp"),
        P("fsdp"),
        P("fsdp"),
        P("fsdp", None),
        P("fsdp"),
        P("fsdp", None),
        P("fsdp"),
    )
    out_specs = (
        P(("dp", "fsdp"), None),
        P(("dp", "fsdp"), None),
        P(None, "fsdp"),
        P("fsdp"),
        P("fsdp"),
        P("fsdp", None),
        P("fsdp"),
        P("fsdp"),
        P("fsdp", None),
        P("fsdp"),
        P("fsdp"),
        P("fsdp"),
        P("fsdp", None),
        P("fsdp"),
        P("fsdp", None),
        P("fsdp"),
    )
    return jax.shard_map(
        per_device, mesh=mesh, in_specs=in_specs, out_specs=out_specs, check_vma=False
    )
```

```python
from functools import partial

import jax
import jax.numpy as jnp
from jax import lax
from jax.experimental import pallas as pl
from jax.experimental.pallas import tpu as pltpu
from jax.sharding import PartitionSpec as P

D = 1024
HEADS = 16
HEAD_DIM = 64
SG = 7
LG = 12
SMALL_LEN = 50
LARGE_LEN = 145
ROWS = 1450
PAD = 1472
GROUP = 8
WINDOW = 176
WINDOWS = 10
PAIRS = 4
ROW_TILE = 368
FAR = -1e30
LOW = jnp.bfloat16
ANYWHERE = pl.BlockSpec(memory_space=pl.ANY)


EPS = 1e-06


def grid_fraction(index):
    scaled = jnp.maximum((2 * index + 1) * SG - LG, 0)
    lower = scaled // (2 * LG)
    return (scaled - 2 * LG * lower).astype(jnp.float32) / (2.0 * LG)


def interp_table(position_source):
    position = jnp.arange(LARGE_LEN, dtype=jnp.int32)
    patch = jnp.maximum(position - 1, 0)
    frac_row = grid_fraction(patch // LG)
    frac_col = grid_fraction(patch % LG)
    weights = jnp.stack(
        [
            (1.0 - frac_row) * (1.0 - frac_col),
            (1.0 - frac_row) * frac_col,
            frac_row * (1.0 - frac_col),
            frac_row * frac_col,
        ],
        axis=1,
    )
    class_row = (jnp.arange(4, dtype=jnp.int32) == 0).astype(jnp.float32)
    weights = jnp.where((position == 0)[:, None], class_row[None, :], weights)
    onehot = (
        position_source[:, :, None] == jnp.arange(SMALL_LEN, dtype=jnp.int32)[None, None, :]
    ).astype(jnp.float32)
    return jnp.sum(weights[:, :, None] * onehot, axis=1)


def layer_norm(values, gain, shift):
    average = jnp.mean(values, axis=-1, keepdims=True)
    centred = values - average
    variance = jnp.mean(centred * centred, axis=-1, keepdims=True)
    inv_std = lax.rsqrt(variance + EPS)
    normed = centred * inv_std
    return (normed * gain + shift, normed, inv_std)


def norm_back(grad_norm, normed, inv_std, gain):
    scaled = grad_norm * gain
    inner = (
        scaled
        - jnp.mean(scaled, axis=-1, keepdims=True)
        - normed * jnp.mean(scaled * normed, axis=-1, keepdims=True)
    )
    return (inv_std * inner, jnp.sum(grad_norm * normed, axis=0), jnp.sum(grad_norm, axis=0))

def dot_nt(left, right):
    return lax.dot_general(
        left, right, (((1,), (1,)), ((), ())), preferred_element_type=jnp.float32
    )


def dot_nn(left, right):
    return lax.dot_general(
        left, right, (((1,), (0,)), ((), ())), preferred_element_type=jnp.float32
    )


def dot_tn(left, right):
    return lax.dot_general(
        left, right, (((0,), (0,)), ((), ())), preferred_element_type=jnp.float32
    )


def cost(flops, moved):
    return pl.CostEstimate(flops=int(flops), transcendentals=0, bytes_accessed=int(moved))


def after(value, *others):
    return lax.optimization_barrier((value, *others))[0]


def sync(*values):
    return lax.optimization_barrier(values)


def window_start(window, step):
    return pl.multiple_of(jnp.minimum(window * step // 16 * 16, PAD - WINDOW), 16)


def image_of(row, length, step):
    image = jnp.where(row >= length, 1, 0) + jnp.where(row >= 2 * length, 1, 0)
    return jnp.where(row < 0, -1, jnp.where(row >= step, 3, image))


def fill_masks(mask_ref, length, step):
    def one(window, carry):
        base = window_start(window, step) - window * step
        shape = (WINDOW, WINDOW)
        rows = image_of(lax.broadcasted_iota(jnp.int32, shape, 0) + base, length, step)
        cols = image_of(lax.broadcasted_iota(jnp.int32, shape, 1) + base, length, step)
        mask_ref[window] = jnp.where(rows == cols, 0.0, FAR).astype(jnp.float32)
        return carry

    lax.fori_loop(0, WINDOWS, one, 0)


def split_heads(value):
    lane = lax.broadcasted_iota(jnp.int32, value.shape, 1)
    zero = jnp.zeros_like(value)
    return jnp.where(lane < HEAD_DIM, value, zero), jnp.where(lane < HEAD_DIM, zero, value)


def slabs(refs, at):
    return [ref[at, i : i + 128] for ref in refs for i in range(0, ref.shape[1], 128)]


def join_heads(even, odd):
    lane = lax.broadcasted_iota(jnp.int32, even.shape, 1)
    return jnp.where(lane < HEAD_DIM, even, odd)


def keep_rows(ref, start, first, value):
    row = lax.broadcasted_iota(jnp.int32, value.shape, 0) + start
    value = jnp.where(row < ROWS, value, 0.0)
    at = pl.ds(start, WINDOW)
    old = ref[at, :].astype(jnp.float32)
    ref[at, :] = jnp.where(row >= first, value, old).astype(ref.dtype)


def forward_kernel(s_ref, q_ref, k_ref, v_ref, *refs):
    o_ref, mask_ref = refs[-2:]
    length, step = s_ref[0], s_ref[1]
    fill_masks(mask_ref, length, step)

    def one(window, carry):
        start = window_start(window, step)
        at = pl.ds(start, WINDOW)
        query = [h for v in slabs([q_ref], at) for h in split_heads(v * LOW(0.125))]
        keys, values = slabs([k_ref], at), slabs([v_ref], at)
        mask = mask_ref[window]
        each = range(2 * PAIRS)
        scores = [dot_nt(query[i], keys[i // 2]) + mask for i in each]
        top = [jnp.max(v, axis=1, keepdims=True) for v in scores]
        raised = [jnp.exp(scores[i] - top[i]) for i in each]
        total = [jnp.sum(v, axis=1, keepdims=True) for v in raised]
        out = [dot_nn(raised[i].astype(LOW), values[i // 2]) for i in each]
        out = [out[i] * (1.0 / total[i]) for i in each]
        for j in range(PAIRS):
            piece = join_heads(out[2 * j], out[2 * j + 1])
            keep_rows(o_ref.at[:, 128 * j : 128 * j + 128], start, window * step, piece)
        return carry

    lax.fori_loop(0, WINDOWS, one, 0)


def backward_kernel(s_ref, *refs):
    (q_refs, k_refs, v_refs, g_refs, out_refs), mask_ref = (
        [refs[2 * i : 2 * i + 2] for i in range(5)],
        refs[10],
    )
    length, step = s_ref[0], s_ref[1]
    fill_masks(mask_ref, length, step)

    def one(window, carry):
        start = window_start(window, step)
        at = pl.ds(start, WINDOW)
        query = [h for v in slabs(q_refs, at) for h in split_heads(v * LOW(0.125))]
        grad = [h for v in slabs(g_refs, at) for h in split_heads(v)]
        keys, values = slabs(k_refs, at), slabs(v_refs, at)
        mask = mask_ref[window]
        each = range(len(query))
        scores = [dot_nt(keys[i // 2], query[i]) + mask for i in each]
        grad_probs = [dot_nt(values[i // 2], grad[i]) for i in each]
        top = [jnp.max(v, axis=0, keepdims=True) for v in scores]
        raised = [jnp.exp(scores[i] - top[i]) for i in each]
        scale = [1.0 / jnp.sum(v, axis=0, keepdims=True) for v in raised]
        probs = [raised[i] * scale[i] for i in each]
        inner = [jnp.sum(grad_probs[i] * probs[i], axis=0, keepdims=True) for i in each]
        grad_scores = [(probs[i] * (grad_probs[i] - inner[i])).astype(LOW) for i in each]
        grad_v = [dot_nn(probs[i].astype(LOW), grad[i]) for i in each]
        grad_k = [dot_nn(grad_scores[i], query[i]) for i in each]
        grad_q = [dot_tn(grad_scores[i], keys[i // 2]) for i in each]
        first = window * step
        for j in range(len(keys)):
            out = out_refs[j // 2]
            cols = slice(j % 2 * 128, j % 2 * 128 + 128)
            both = join_heads(grad_q[2 * j], grad_q[2 * j + 1]) * 0.125
            keep_rows(out.at[0, :, cols], start, first, both)
            keep_rows(out.at[1, :, cols], start, first, grad_k[2 * j] + grad_k[2 * j + 1])
            keep_rows(out.at[2, :, cols], start, first, grad_v[2 * j] + grad_v[2 * j + 1])
        return carry

    lax.fori_loop(0, WINDOWS, one, 0)


def attend_forward(lengths, projected, half, before=None):
    width = 128 * PAIRS
    blocks = D // width

    def part(base):
        return pl.BlockSpec((PAD, width), lambda i, s: (0, half + base))

    return pl.pallas_call(
        forward_kernel,
        out_shape=jax.ShapeDtypeStruct((PAD, D), LOW),
        grid_spec=pltpu.PrefetchScalarGridSpec(
            num_scalar_prefetch=1,
            grid=(1,),
            in_specs=[part(0), part(blocks), part(2 * blocks)] + [ANYWHERE] * (before is not None),
            out_specs=part(0),
            scratch_shapes=[pltpu.VMEM((WINDOWS, WINDOW, WINDOW), jnp.float32)],
        ),
        input_output_aliases={} if before is None else {4: 0},
        cost_estimate=cost(1e10, 1e7),
        name="attend_forward",
    )(lengths, projected, projected, projected, *([] if before is None else [before]))


def attend_backward(numbers, projected, grad):
    width = D // 4

    def part(base, i):
        return pl.BlockSpec((PAD, width), lambda n, s: (0, s[2 + i] + base))

    return pl.pallas_call(
        backward_kernel,
        out_shape=[jax.ShapeDtypeStruct((3, PAD, width), LOW)] * 2,
        grid_spec=pltpu.PrefetchScalarGridSpec(
            num_scalar_prefetch=1,
            grid=(1,),
            in_specs=[part(base, i) for base in (0, 4, 8, 0) for i in (0, 1)],
            out_specs=[pl.BlockSpec((3, PAD, width), lambda n, s: (0, 0, 0))] * 2,
            scratch_shapes=[pltpu.VMEM((WINDOWS, WINDOW, WINDOW), jnp.float32)],
        ),
        cost_estimate=cost(2e10, 1e7),
        name="attend_backward",
    )(numbers, *([projected] * 6), grad, grad)


def hidden_kernel(rows, x_ref, w_ref, b_ref, activ_ref, slope_ref):
    for i in range(PAD // rows):
        at = slice(i * rows, (i + 1) * rows)
        hidden = dot_nn(x_ref[at, :], w_ref[...]) + b_ref[...]
        cdf = 0.5 * lax.erf(hidden * 0.7071067811865476) + 0.5
        density = jnp.exp(-0.5 * hidden * hidden) * 0.3989422804014327
        activ_ref[at, :] = (hidden * cdf).astype(LOW)
        slope_ref[at, :] = (cdf + hidden * density).astype(LOW)


def hidden_layer(second, weight, bias):
    width = bias.shape[0]
    tile = 512
    return pl.pallas_call(
        partial(hidden_kernel, 184),
        out_shape=[jax.ShapeDtypeStruct((PAD, width), LOW)] * 2,
        grid=(width // tile,),
        in_specs=[
            pl.BlockSpec((PAD, D), lambda n: (0, 0)),
            pl.BlockSpec((D, tile), lambda n: (0, n)),
            pl.BlockSpec((1, tile), lambda n: (0, n)),
        ],
        out_specs=[pl.BlockSpec((PAD, tile), lambda n: (0, n))] * 2,
        cost_estimate=cost(2.4e10, 4e7),
        name="hidden_layer",
    )(second, weight, bias.reshape(1, width))


def hidden_back_kernel(shards, steps, rows, s_ref, g_ref, slope_ref, *refs):
    parts, (out_ref, sum_ref, full), (held, sem) = refs[:5], refs[5:8], refs[8:]
    finish = fetch(shards, s_ref, parts, held, full, sem, steps)
    tile = out_ref.shape[1]
    weight = held[pl.ds(pl.multiple_of(pl.program_id(0) * tile, tile), tile), :]
    total = jnp.zeros_like(sum_ref)
    for i in range(PAD // rows):
        at = slice(i * rows, (i + 1) * rows)
        grad = dot_nt(g_ref[at, :], weight) * slope_ref[at, :].astype(jnp.float32)
        grad = grad.astype(LOW)
        out_ref[at, :] = grad
        total = total + column_sum(grad.astype(jnp.float32))
    sum_ref[...] = total
    finish()


def hidden_back(grad, slope, shard, sets):
    width = slope.shape[1]
    tile = 512
    steps = width // tile
    return pl.pallas_call(
        partial(hidden_back_kernel, lax.axis_size("fsdp"), steps, 368),
        out_shape=[
            jax.ShapeDtypeStruct((PAD, width), LOW),
            jax.ShapeDtypeStruct((1, width), jnp.float32),
            fetch_shape(shard),
        ],
        grid_spec=pltpu.PrefetchScalarGridSpec(
            num_scalar_prefetch=1,
            grid=(steps,),
            in_specs=[
                pl.BlockSpec((PAD, D), lambda n, s: (0, 0)),
                pl.BlockSpec((PAD, tile), lambda n, s: (0, n)),
            ]
            + [ANYWHERE] * 5,
            out_specs=[
                pl.BlockSpec((PAD, tile), lambda n, s: (0, n)),
                pl.BlockSpec((1, tile), lambda n, s: (0, n)),
                ANYWHERE,
            ],
            scratch_shapes=fetch_scratch(shard),
        ),
        cost_estimate=cost(1.8e10, 4e7),
        name="hidden_back",
    )(fetch_numbers(), grad, slope, shard, *sets)


def normalise(value):
    average = jnp.mean(value, axis=-1, keepdims=True)
    centred = value - average
    inv_std = lax.rsqrt(jnp.mean(centred * centred, axis=-1, keepdims=True) + EPS)
    return centred * inv_std, inv_std


def back_through_norm(grad, normed, inv_std, gain):
    scaled = grad * gain
    inner = (
        scaled
        - jnp.mean(scaled, axis=-1, keepdims=True)
        - normed * jnp.mean(scaled * normed, axis=-1, keepdims=True)
    )
    return inv_std * inner


def column_sum(value):
    return jnp.sum(value, axis=0, keepdims=True)


def rows_of(width, stacked=0):
    if stacked:
        return pl.BlockSpec((stacked, ROW_TILE, width), lambda i, *s: (0, i, 0))
    return pl.BlockSpec((ROW_TILE, width), lambda i, *s: (i, 0))


def whole(*shape):
    return pl.BlockSpec(shape, lambda i, *s: (0,) * len(shape))


def project_kernel(shards, steps, s_ref, a_ref, b_ref, *refs):
    parts, (out_ref, full), (held, sem) = refs[:5], refs[5:7], refs[7:]
    finish = fetch(shards, s_ref, parts, held, full, sem, steps)
    out_ref[...] = (dot_nn(a_ref[...], held[...]) + b_ref[...]).astype(LOW)
    finish()


def project(first, bias, shard, sets):
    width = shard.shape[1]
    steps = PAD // ROW_TILE
    return pl.pallas_call(
        partial(project_kernel, lax.axis_size("fsdp"), steps),
        out_shape=[jax.ShapeDtypeStruct((PAD, width), LOW), fetch_shape(shard)],
        grid_spec=pltpu.PrefetchScalarGridSpec(
            num_scalar_prefetch=1,
            grid=(steps,),
            in_specs=[rows_of(D), whole(1, width)] + [ANYWHERE] * 5,
            out_specs=[rows_of(width), ANYWHERE],
            scratch_shapes=fetch_scratch(shard),
        ),
        cost_estimate=cost(2 * PAD * D * width, 2e7),
        name="project",
    )(fetch_numbers(), first, bias.reshape(1, width), shard, *sets)


def branch_kernel(shards, steps, s_ref, a_ref, stream_ref, vec_ref, *refs):
    parts, (mid_ref, second_ref, full), (held, sem) = refs[:5], refs[5:8], refs[8:]
    finish = fetch(shards, s_ref, parts, held, full, sem, steps)
    weight = held[:, held.shape[1] - D :]
    mid = stream_ref[...] + dot_nn(a_ref[...], weight) + vec_ref[0:1, :]
    mid_ref[...] = mid
    normed, _ = normalise(mid)
    second_ref[...] = (normed * vec_ref[1:2, :] + vec_ref[2:3, :]).astype(LOW)
    finish()


def branch(attended, stream, vectors, shard, sets):
    steps = PAD // ROW_TILE
    return pl.pallas_call(
        partial(branch_kernel, lax.axis_size("fsdp"), steps),
        out_shape=[
            jax.ShapeDtypeStruct((PAD, D), jnp.float32),
            jax.ShapeDtypeStruct((PAD, D), LOW),
            fetch_shape(shard),
        ],
        grid_spec=pltpu.PrefetchScalarGridSpec(
            num_scalar_prefetch=1,
            grid=(steps,),
            in_specs=[rows_of(D), rows_of(D), whole(3, D)] + [ANYWHERE] * 5,
            out_specs=[rows_of(D), rows_of(D), ANYWHERE],
            scratch_shapes=fetch_scratch(shard),
        ),
        cost_estimate=cost(2 * PAD * D * D, 3e7),
        name="branch",
    )(fetch_numbers(), attended, stream, vectors, shard, *sets)


def return_kernel(a_ref, w_ref, mid_ref, vec_ref, out_ref):
    value = mid_ref[...] + dot_nn(a_ref[...], w_ref[...]) + vec_ref[...]
    out_ref[...] = value.astype(LOW)


def return_layer(activ, weight, mid, bias):
    width = weight.shape[0]
    return pl.pallas_call(
        return_kernel,
        out_shape=jax.ShapeDtypeStruct((ROWS, D), LOW),
        grid=(PAD // ROW_TILE,),
        in_specs=[rows_of(width), whole(width, D), rows_of(D), whole(1, D)],
        out_specs=rows_of(D),
        cost_estimate=cost(2 * PAD * D * width, 3e7),
        name="return_layer",
    )(activ, weight, mid, bias.reshape(1, D))


def second_back_kernel(
    h_ref, w_ref, o_ref, mid_ref, g_ref, gain_ref, out_ref, low_ref, att_ref, sums_ref
):
    @pl.when(pl.program_id(0) == 0)
    def _():
        sums_ref[...] = jnp.zeros_like(sums_ref)

    grad = dot_nt(h_ref[...], w_ref[...])
    normed, inv_std = normalise(mid_ref[...])
    out = g_ref[...].astype(jnp.float32)
    sums_ref[3:4, :] += column_sum(out)
    out = out + back_through_norm(grad, normed, inv_std, gain_ref[...])
    out_ref[...] = out
    low = out.astype(LOW)
    low_ref[...] = low
    att_ref[...] = dot_nt(low, o_ref[...]).astype(LOW)
    sums_ref[0:1, :] += column_sum(grad * normed)
    sums_ref[1:2, :] += column_sum(grad)
    sums_ref[2:3, :] += column_sum(low.astype(jnp.float32))


def second_back(grad_hidden, joined, mid, grad, gain):
    width = grad_hidden.shape[1]
    return pl.pallas_call(
        second_back_kernel,
        out_shape=[
            jax.ShapeDtypeStruct((PAD, D), jnp.float32),
            jax.ShapeDtypeStruct((PAD, D), LOW),
            jax.ShapeDtypeStruct((PAD, D), LOW),
            jax.ShapeDtypeStruct((8, D), jnp.float32),
        ],
        grid=(PAD // ROW_TILE,),
        in_specs=[
            rows_of(width),
            whole(D, width),
            pl.BlockSpec((D, D), lambda i: (0, width // D)),
            rows_of(D),
            rows_of(D),
            whole(1, D),
        ],
        out_specs=[rows_of(D), rows_of(D), rows_of(D), whole(8, D)],
        cost_estimate=cost(2 * PAD * D * width, 4e7),
        name="second_back",
    )(grad_hidden, joined, joined, mid, grad, gain.reshape(1, D))


def first_back_kernel(s_ref, *refs):
    heads, w_refs, (stream_ref, mid_ref, spread_ref, gain_ref) = refs[:4], refs[4:16], refs[16:20]
    out_ref, table_ref, sums_ref, heads_ref = refs[20:]

    @pl.when(pl.program_id(0) == 0)
    def _():
        sums_ref[...] = jnp.zeros_like(sums_ref)
        table_ref[...] = jnp.zeros_like(table_ref)
        heads_ref[...] = jnp.zeros_like(heads_ref)

    grad = 0.0
    for j, ref in enumerate(heads):
        for t in range(3):
            grad = grad + dot_nt(ref[t], w_refs[3 * j + t][...])
    normed, inv_std = normalise(stream_ref[...])
    out = mid_ref[...] + back_through_norm(grad, normed, inv_std, gain_ref[...])
    out_ref[...] = out.astype(LOW)
    sums_ref[0:1, :] += column_sum(grad * normed)
    sums_ref[1:2, :] += column_sum(grad)
    table_ref[...] += lax.dot_general(
        spread_ref[...],
        out,
        (((0,), (0,)), ((), ())),
        precision=lax.Precision.HIGHEST,
        preferred_element_type=jnp.float32,
    )
    for j, ref in enumerate(heads):
        for i, t in enumerate((0, 2)):
            at = 2 * j + i
            heads_ref[at : at + 1, :] += column_sum(ref[t].astype(jnp.float32))


def first_back(quarters, heads, joined, stream, grad_mid, spread, gain):
    width = D // 4
    w_specs = [
        pl.BlockSpec((D, width), lambda i, s, j=j, t=t: (0, 4 * t + s[j]))
        for j in range(4)
        for t in range(3)
    ]
    slots = spread.shape[1]
    return pl.pallas_call(
        first_back_kernel,
        out_shape=[
            jax.ShapeDtypeStruct((ROWS, D), LOW),
            jax.ShapeDtypeStruct((slots, D), jnp.float32),
            jax.ShapeDtypeStruct((8, D), jnp.float32),
            jax.ShapeDtypeStruct((8, width), jnp.float32),
        ],
        grid_spec=pltpu.PrefetchScalarGridSpec(
            num_scalar_prefetch=1,
            grid=(PAD // ROW_TILE,),
            in_specs=[rows_of(width, 3)] * 4
            + w_specs
            + [rows_of(D), rows_of(D), rows_of(slots), whole(1, D)],
            out_specs=[rows_of(D), whole(slots, D), whole(8, D), whole(8, width)],
        ),
        cost_estimate=cost(2 * PAD * D * 3 * D, 4e7),
        name="first_back",
    )(quarters, *heads, *([joined] * 12), stream, grad_mid, spread, gain.reshape(1, D))


def widen_kernel(moves, count, *refs):
    for source, at, target, to, width in moves:
        for core in (0, 1):
            value = refs[source][0, core, :, at : at + width].astype(jnp.float32)
            refs[count + target][:, to[core] : to[core] + width] = value


def widen(sources, widths, moves):
    rows = sources[0].shape[1]
    return pl.pallas_call(
        partial(widen_kernel, moves, len(sources)),
        out_shape=[jax.ShapeDtypeStruct((4 * rows, w), jnp.float32) for w in widths],
        grid=(4,),
        in_specs=[
            pl.BlockSpec((1, 2, rows, v.shape[2]), lambda i: (i, 0, 0, 0)) for v in sources
        ],
        out_specs=[pl.BlockSpec((rows, w), lambda i: (i, 0)) for w in widths],
        cost_estimate=cost(1, 6e6),
        name="widen",
    )(*[v.reshape(4, 2, rows, v.shape[2]) for v in sources])


def grad_value(f_ref, a_ref, b_ref):
    if len(b_ref.shape) == 2:
        return dot_tn(a_ref[...], b_ref[...]) * f_ref[0]
    return jnp.concatenate([dot_tn(a_ref[...], b_ref[i]) for i in range(3)], axis=1) * f_ref[0]


def grad_send_kernel(c_ref, f_ref, a_ref, b_ref, out_ref):
    out_ref[...] = grad_value(f_ref, a_ref, b_ref).astype(LOW)


def grad_keep_kernel(planes, c_ref, f_ref, a_ref, b_ref, got_ref, keep_ref, send_ref):
    value = (grad_value(f_ref, a_ref, b_ref) + got_ref[...].astype(jnp.float32)).astype(LOW)
    core, place = c_ref[0], c_ref[1]
    rows = value.shape[0] // planes // 4
    for quarter in range(4):
        bits = place ^ quarter
        role = jnp.where(core == 0, bits, (bits >> 1) | ((bits & 1) << 1))
        for ref, near in ((keep_ref, 0), (send_ref, 1)):

            @pl.when(role % 2 == near)
            def _(ref=ref, quarter=quarter, role=role):
                for plane in range(planes):
                    at = (plane * 4 + quarter) * rows
                    ref[role // 2, plane] = value[at : at + rows]


def grad_half(numbers, factor, left, right, got=None, tile_m=1024, tile_n=512):
    rows = left.shape[1]
    shards = lax.axis_size("fsdp")
    stacked = right.ndim == 3
    cols = 3 * right.shape[2] if stacked else right.shape[1] // 2
    tile_n = cols if stacked else tile_n
    steps = cols // tile_n
    in_specs = [
        pl.BlockSpec(memory_space=pltpu.SMEM),
        pl.BlockSpec((PAD, tile_m), lambda m, n, c: (0, m)),
    ]
    if stacked:
        in_specs.append(pl.BlockSpec((3, PAD, cols // 3), lambda m, n, c: (0, 0, 0)))
    else:
        in_specs.append(pl.BlockSpec((PAD, tile_n), lambda m, n, c: (0, n + c[0] * steps)))
    flat_spec = pl.BlockSpec((tile_m, tile_n), lambda m, n, c: (m, n))
    operands = [numbers, factor, left, right]
    if got is None:
        kernel, name = grad_send_kernel, "grad_send"
        out_shape, out_specs = jax.ShapeDtypeStruct((rows, cols), LOW), flat_spec
    else:
        planes = tile_m * shards // rows
        part = rows // shards // 4
        kernel, name = partial(grad_keep_kernel, planes), "grad_keep"
        in_specs.append(flat_spec)
        operands.append(got)
        out_shape = [jax.ShapeDtypeStruct((2, shards, part, cols), LOW)] * 2
        out_specs = [pl.BlockSpec((2, planes, part, tile_n), lambda m, n, c: (0, m, 0, n))] * 2
    return pl.pallas_call(
        kernel,
        out_shape=out_shape,
        grid_spec=pltpu.PrefetchScalarGridSpec(
            num_scalar_prefetch=1,
            grid=(rows // tile_m, steps),
            in_specs=in_specs,
            out_specs=out_specs,
        ),
        cost_estimate=cost(2 * PAD * rows * cols, 1e7),
        name=name,
    )(*operands)


def swap(value, even, odd):
    size = lax.axis_size("dp")
    return lax.ppermute(value, "dp", [(i, i ^ (odd if i % 2 else even)) for i in range(size)])


def swap_core(value):
    return swap(value, 1, 1)


def swap_first(value):
    return swap(value, 2, 4)


def swap_second(value):
    return swap(value, 4, 2)


def own_piece(shard):
    part = shard.shape[0] // GROUP
    place = lax.axis_index("dp") % GROUP
    return lax.dynamic_slice_in_dim(shard, place * part, part, 0)


def gather_z(shard):
    shards = lax.axis_size("fsdp")
    piece = own_piece(shard)
    return jnp.stack(
        [
            lax.ppermute(piece, "fsdp", [((i + k) % shards, i) for i in range(shards)])
            for k in range(1, shards)
        ]
    )


def gather_z_native(shard):
    every = lax.all_gather(own_piece(shard), "fsdp", axis=0, tiled=False)
    shards = every.shape[0]
    twice = jnp.concatenate([every, every[:-1]], axis=0)
    return lax.dynamic_slice_in_dim(twice, lax.axis_index("fsdp") + 1, shards - 1, 0)


def gather_first(own):
    return own, swap_first(own)


def gather_second(own, got):
    both = jnp.stack([own, got])
    return both, swap_second(both)


def gather_core(both, far):
    return both, far, swap_core(both), swap_core(far)


def fetch_copies(shards, s_ref, refs, held, sem):
    own, sets = refs[0], refs[1:]
    place, row = s_ref[0], s_ref[1]
    rows = own.shape[0]
    part = rows // GROUP
    copies = [
        pltpu.make_async_copy(
            own, held.at[pl.ds(pl.multiple_of(row * rows, rows), rows), :], sem.at[0]
        )
    ]
    for flip in range(2):
        base = place ^ flip
        first = jnp.where(base % 2 == 0, 2, 4)
        for source, bits in (
            (sets[2 * flip].at[0], 0),
            (sets[2 * flip].at[1], first),
            (sets[2 * flip + 1].at[0], 6 - first),
            (sets[2 * flip + 1].at[1], 6),
        ):
            for k in range(1, shards):
                at = lax.rem(row + k, shards) * rows + (base ^ bits) * part
                target = held.at[pl.ds(pl.multiple_of(at, part), part), :]
                copies.append(pltpu.make_async_copy(source.at[k - 1], target, sem.at[len(copies)]))
    return copies


def fetch(shards, s_ref, refs, held, full, sem, steps):
    def keep():
        return pltpu.make_async_copy(held, full, sem.at[0])

    @pl.when(pl.program_id(0) == 0)
    def _():
        copies = fetch_copies(shards, s_ref, refs, held, sem)
        for copy in copies:
            copy.start()
        for copy in copies:
            copy.wait()
        keep().start()

    def finish():
        @pl.when(pl.program_id(0) == steps - 1)
        def _():
            keep().wait()

    return finish


def fetch_numbers():
    place = lax.axis_index("dp") % GROUP
    return jnp.stack([place, lax.axis_index("fsdp")]).astype(jnp.int32)


def fetch_scratch(shard):
    shards = lax.axis_size("fsdp")
    return [
        pltpu.VMEM((shards * shard.shape[0], shard.shape[1]), shard.dtype),
        pltpu.SemaphoreType.DMA((1 + 8 * (shards - 1),)),
    ]


def fetch_shape(shard):
    shards = lax.axis_size("fsdp")
    return jax.ShapeDtypeStruct((shards * shard.shape[0], shard.shape[1]), shard.dtype)


def plane_gather(value, axis):
    size = lax.axis_size("dp")
    groups = None
    if size > GROUP:
        groups = [[g * GROUP + i for i in range(GROUP)] for g in range(size // GROUP)]
    return lax.all_gather(value, "dp", axis=axis, tiled=False, axis_index_groups=groups)


def rest_sum(value):
    size = lax.axis_size("dp")
    if size == GROUP:
        return value
    groups = [[g * GROUP + i for g in range(size // GROUP)] for i in range(GROUP)]
    return lax.psum(value, "dp", axis_index_groups=groups)


def add_low(left, right):
    return (left.astype(jnp.float32) + right.astype(jnp.float32)).astype(LOW)


def sum_first(got, *keeps):
    keep = jnp.concatenate(keeps, axis=-1)
    return add_low(keep[0], got[0]), swap_second(add_low(keep[1], got[1]))


def sum_z(kept, got):
    both = add_low(kept, got)
    shards, part, cols = both.shape
    piece = lax.psum_scatter(
        both.reshape(shards * part, cols), "fsdp", scatter_dimension=0, tiled=True
    )
    return rest_sum(piece)


def sum_z_direct(value):
    shards = lax.axis_size("fsdp")
    me = lax.axis_index("fsdp")
    total = lax.dynamic_index_in_dim(value, me, 0, keepdims=False).astype(jnp.float32)
    for step in range(1, shards):
        send = lax.dynamic_index_in_dim(value, (me + step) % shards, 0, keepdims=False)
        got = lax.ppermute(send, "fsdp", [(i, (i + step) % shards) for i in range(shards)])
        total = total + got.astype(jnp.float32)
    return total


def small_sum(value):
    every = lax.all_gather(value.astype(LOW), "dp", axis=0, tiled=False)
    return jnp.sum(every.astype(jnp.float32), axis=0)


def small_gather(value):
    shards = lax.axis_size("fsdp")
    parts = [value] + [
        lax.ppermute(value, "fsdp", [(i, (i + k) % shards) for i in range(shards)])
        for k in range(1, shards)
    ]
    parts = parts[::-1]
    twice = jnp.stack(parts + parts)
    return lax.dynamic_slice_in_dim(twice, shards - 1 - lax.axis_index("fsdp"), shards, 0)


def per_device(
    tokens,
    output_grad,
    group_member,
    image_counts,
    position_source,
    position_table,
    first_gain,
    first_shift,
    input_proj,
    query_bias,
    value_bias,
    output_proj,
    output_bias,
    second_gain,
    second_shift,
    hidden_weight,
    hidden_bias,
    return_weight,
    return_bias,
):
    dp_size = lax.axis_size("dp")
    fsdp_size = lax.axis_size("fsdp")
    core = (lax.axis_index("dp") & 1).astype(jnp.int32)
    quarter = ((lax.axis_index("dp") % GROUP) >> 1).astype(jnp.int32)
    mine, other = jnp.stack([core, quarter]), jnp.stack([1 - core, quarter])
    small_parts = (
        first_gain,
        first_shift,
        query_bias,
        value_bias,
        output_bias,
        second_gain,
        second_shift,
        return_bias,
        hidden_bias,
        position_table.reshape(-1),
    )
    sizes = [v.shape[0] for v in small_parts]
    wide = first_gain.shape[0]
    joined = jnp.concatenate([v.reshape(-1, wide) for v in small_parts], axis=0)
    pad = -joined.shape[0] % 16 * wide
    joined = jnp.pad(joined, ((0, pad // wide), (0, 0)))
    joint_z = gather_z(input_proj)
    smalls = small_gather(joined).reshape(fsdp_size, -1)
    smalls = smalls.astype(jnp.float32)
    offsets = [sum(sizes[:i]) for i in range(len(sizes))]
    vectors = [smalls[:, o : o + n] for o, n in zip(offsets, sizes)]
    (
        gain_one,
        shift_one,
        query_add,
        value_add,
        output_add,
        gain_two,
        shift_two,
        return_add,
        hidden_add,
    ) = [v.reshape(-1) for v in vectors[:9]]
    table_full = (
        vectors[9].reshape(fsdp_size, SMALL_LEN, -1).transpose(1, 0, 2).reshape(SMALL_LEN, D)
    )
    member = group_member[0]
    is_large = member == 1
    length = jnp.where(is_large, LARGE_LEN, SMALL_LEN)
    step = jnp.where(is_large, LARGE_LEN, 3 * SMALL_LEN)
    group_high = dp_size * 7 // 16
    group_low = dp_size - group_high
    counts = image_counts.astype(jnp.float32)
    share = jnp.where(is_large, counts[1], counts[0]) / (counts[0] + counts[1])
    images = jnp.where(
        is_large,
        group_high * fsdp_size * (ROWS // LARGE_LEN),
        group_low * fsdp_size * (ROWS // SMALL_LEN),
    ).astype(jnp.float32)
    factor = share / images
    scale = factor.reshape(1)

    row_index = jnp.arange(PAD, dtype=jnp.int32)
    place = jnp.where(row_index < ROWS, row_index % length, -1)
    inter = interp_table(position_source)
    identity = (
        jnp.arange(LARGE_LEN, dtype=jnp.int32)[:, None]
        == jnp.arange(SMALL_LEN, dtype=jnp.int32)[None, :]
    ).astype(jnp.float32)
    mixing = jnp.where(is_large, inter, identity)
    picker = (place[:, None] == jnp.arange(LARGE_LEN, dtype=jnp.int32)[None, :]).astype(jnp.float32)
    spread = jnp.dot(picker, mixing, precision=lax.Precision.HIGHEST)
    position = jnp.dot(spread, table_full, precision=lax.Precision.HIGHEST)
    grad_pad = jnp.pad(output_grad, ((0, PAD - ROWS), (0, 0)))
    stream = jnp.pad(tokens, ((0, PAD - ROWS), (0, 0))).astype(jnp.float32) + position
    first_low = layer_norm(stream, gain_one, shift_one)[0].astype(LOW)

    lengths = jnp.stack([length, step])

    joint_one = gather_first(joint_z)
    hidden_shard = jnp.concatenate([hidden_weight, output_proj], axis=1)
    hidden_z = gather_z_native(after(hidden_shard, joint_z))
    joint_two = gather_second(*joint_one)
    joint_sets = gather_core(*joint_two)
    return_z = gather_z_native(after(return_weight, hidden_z))
    hidden_z = after(hidden_z, joint_two[1])
    first_low, grad_pad, hidden_z, *joint_sets = sync(first_low, grad_pad, hidden_z, *joint_sets)
    hidden_one = gather_first(hidden_z)
    joint_add = jnp.concatenate([query_add, jnp.zeros_like(query_add), value_add])
    projected, joint_full = project(first_low, joint_add, input_proj, joint_sets)
    projected, *hidden_one = sync(projected, *hidden_one)
    hidden_two = gather_second(*hidden_one)
    attended = attend_forward(lengths, after(projected, hidden_two[0]), 0)
    attended, return_z, *hidden_two = sync(attended, return_z, *hidden_two)
    hidden_sets = gather_core(*hidden_two)
    return_one = gather_first(return_z)
    attended = attend_forward(lengths, projected, 1, after(attended, hidden_two[1], return_one[0]))
    attended, *rest = sync(attended, *hidden_sets, *return_one)
    hidden_sets, return_one = rest[:4], rest[4:]
    return_two = gather_second(*return_one)
    mid, second, hidden_full = branch(
        after(attended, return_two[0]),
        stream,
        jnp.stack([output_add, gain_two, shift_two]),
        hidden_shard,
        hidden_sets,
    )
    activ, slope = hidden_layer(second, hidden_full, hidden_add)
    activ, slope, *return_two = sync(activ, slope, *return_two)
    return_sets = gather_core(*return_two)
    return_send = grad_half(other, scale, activ, grad_pad)
    return_send, *return_sets = sync(return_send, *return_sets)
    return_got = swap_core(return_send)
    grad_hidden, grad_hidden_add, return_full = hidden_back(
        after(grad_pad, return_send), slope, return_weight, return_sets
    )
    grad_hidden, return_got = sync(grad_hidden, return_got)
    return_keep, return_out = grad_half(mine, scale, activ, grad_pad, return_got)
    return_in = swap_first(return_out)
    hidden_send = grad_half(other, scale, after(second, return_out), grad_hidden)
    hidden_got = swap_core(hidden_send)
    grad_mid, grad_branch, grad_att, sums_two = second_back(
        after(grad_hidden, hidden_send), hidden_full, mid, grad_pad, gain_two
    )
    grad_branch, hidden_got, return_in = sync(grad_branch, hidden_got, return_in)
    return_kept, return_in = sum_first(return_in, return_keep)
    hidden_keep, hidden_out = grad_half(
        mine, scale, after(second, return_kept), grad_hidden, hidden_got
    )
    hidden_out, grad_branch, return_in = sync(hidden_out, grad_branch, return_in)
    return_piece = sum_z(return_kept, return_in)
    hidden_in = swap_first(hidden_out)
    output_send = grad_half(other, scale, attended, grad_branch)
    output_got = swap_core(output_send)
    quarters = jnp.stack([2 * core, 2 - 2 * core, 2 * core + 1, 3 - 2 * core])
    mine_one, other_one = attend_backward(
        jnp.concatenate([lengths, quarters[:2]]), projected, after(grad_att, output_send)
    )
    mine_one, other_one, output_got, hidden_in = sync(mine_one, other_one, output_got, hidden_in)
    hidden_kept, hidden_in = sum_first(hidden_in, hidden_keep)
    joint_send = grad_half(other, scale, after(first_low, hidden_kept), other_one, tile_m=512)
    joint_send, return_piece = sync(joint_send, return_piece)
    joint_got = swap_core(joint_send)
    return_every = plane_gather(return_piece, axis=0)
    output_keep, output_out = grad_half(
        mine, scale, attended, after(grad_branch, joint_send), output_got
    )
    output_out, joint_got = sync(output_out, joint_got)
    joint_keep, joint_out = grad_half(mine, scale, first_low, mine_one, joint_got, tile_m=512)
    joint_out, hidden_in = sync(joint_out, hidden_in)
    hidden_piece = sum_z(hidden_kept, hidden_in)
    joint_out = jnp.concatenate([joint_out, output_out], axis=-1)
    joint_in = swap_first(joint_out)
    mine_two, other_two = attend_backward(
        jnp.concatenate([lengths, quarters[2:]]), projected, after(grad_att, joint_out)
    )
    mine_two, other_two, joint_in, return_every = sync(mine_two, other_two, joint_in, return_every)
    joint_kept, joint_in = sum_first(joint_in, joint_keep, output_keep)
    last_send = grad_half(other, scale, after(first_low, joint_kept), other_two, tile_m=512)
    last_got = swap_core(last_send)
    last_got, joint_in = sync(last_got, joint_in)
    joint_piece = sum_z(joint_kept, joint_in)
    last_keep, last_out = grad_half(mine, scale, first_low, mine_two, last_got, tile_m=512)
    last_in = swap_first(last_out)
    heads = sync(mine_one, other_one, mine_two, other_two, last_out)[:4]
    tokens_grad, grad_table, sums_one, head_sums = first_back(
        quarters, heads, joint_full, stream, grad_mid, spread, gain_one
    )
    tokens_grad, grad_table, sums_one, head_sums, last_in = sync(
        tokens_grad, grad_table, sums_one, head_sums, last_in
    )
    last_kept, last_in = sum_first(last_in, last_keep)
    hidden_every = plane_gather(hidden_piece, axis=0)
    joint_every = plane_gather(joint_piece, axis=0)

    head_sums = head_sums.reshape(2, 2, 2, -1).transpose(2, 1, 0, 3)
    head_sums = jnp.where(core == 0, head_sums, head_sums[:, ::-1])
    table_rows = grad_table.reshape(SMALL_LEN, fsdp_size, -1).transpose(1, 0, 2)
    small_grads = (
        sums_one[0],
        sums_one[1],
        head_sums[0],
        head_sums[1],
        sums_two[2],
        sums_two[0],
        sums_two[1],
        sums_two[3],
        grad_hidden_add,
        table_rows,
    )
    packed = jnp.concatenate([v.reshape(fsdp_size, -1) for v in small_grads], axis=1) * factor
    packed = jnp.pad(packed, ((0, 0), (0, pad))).reshape(fsdp_size, -1, 128).astype(LOW)
    packed, last_in = sync(packed, last_in)
    last_both = add_low(last_kept, last_in)
    last_piece = sum_z_direct(last_both).astype(LOW)
    small_piece = sum_z_direct(packed)
    block_out = return_layer(after(activ, packed, last_both), return_full, mid, return_add)
    block_out, last_piece, small_piece = sync(block_out, last_piece, small_piece)
    summed = small_sum(small_piece).reshape(-1)
    small_outs = [summed[o : o + n] for o, n in zip(offsets, sizes)]
    last_every = plane_gather(last_piece, axis=0)
    half, part = D // 2, D // 4
    (return_w_out,) = widen([return_every], [D], [(0, 0, 0, (0, half), half)])
    (hidden_w_out,) = widen([hidden_every], [4 * D], [(0, 0, 0, (0, 2 * D), 2 * D)])
    moves = [
        (i, t * part, 0, (t * D + i * part, t * D + half + i * part), part)
        for i in range(2)
        for t in range(3)
    ]
    joint_out, outproj_out = widen(
        [joint_every, last_every], [3 * D, D], moves + [(0, 3 * part, 1, (0, half), half)]
    )
    return (
        block_out,
        tokens_grad,
        small_outs[9].reshape(SMALL_LEN, -1),
        small_outs[0],
        small_outs[1],
        joint_out,
        small_outs[2],
        small_outs[3],
        outproj_out,
        small_outs[4],
        small_outs[5],
        small_outs[6],
        hidden_w_out,
        small_outs[8],
        return_w_out,
        small_outs[7],
    )


def solution(mesh):
    in_specs = (
        P(("dp", "fsdp"), None),
        P(("dp", "fsdp"), None),
        P("dp"),
        P(),
        P(),
        P(None, "fsdp"),
        P("fsdp"),
        P("fsdp"),
        P("fsdp", None),
        P("fsdp"),
        P("fsdp"),
        P("fsdp", None),
        P("fsdp"),
        P("fsdp"),
        P("fsdp"),
        P("fsdp", None),
        P("fsdp"),
        P("fsdp", None),
        P("fsdp"),
    )
    out_specs = (
        P(("dp", "fsdp"), None),
        P(("dp", "fsdp"), None),
        P(None, "fsdp"),
        P("fsdp"),
        P("fsdp"),
        P("fsdp", None),
        P("fsdp"),
        P("fsdp"),
        P("fsdp", None),
        P("fsdp"),
        P("fsdp"),
        P("fsdp"),
        P("fsdp", None),
        P("fsdp"),
        P("fsdp", None),
        P("fsdp"),
    )
    return jax.shard_map(
        per_device, mesh=mesh, in_specs=in_specs, out_specs=out_specs, check_vma=False
    )
```

```python
from functools import partial

import jax
import jax.numpy as jnp
from jax import lax
from jax.experimental import pallas as pl
from jax.experimental.pallas import tpu as pltpu
from jax.sharding import PartitionSpec as P

D = 1024
HEADS = 16
HEAD_DIM = 64
SG = 7
LG = 12
SMALL_LEN = 50
LARGE_LEN = 145
ROWS = 1450
PAD = 1472
GROUP = 8
WINDOW = 176
WINDOWS = 10
ROW_TILE = 368
FAR = -1e30
LOW = jnp.bfloat16
ANYWHERE = pl.BlockSpec(memory_space=pl.ANY)


EPS = 1e-06


def grid_fraction(index):
    scaled = jnp.maximum((2 * index + 1) * SG - LG, 0)
    lower = scaled // (2 * LG)
    return (scaled - 2 * LG * lower).astype(jnp.float32) / (2.0 * LG)


def interp_table(position_source):
    position = jnp.arange(LARGE_LEN, dtype=jnp.int32)
    patch = jnp.maximum(position - 1, 0)
    frac_row = grid_fraction(patch // LG)
    frac_col = grid_fraction(patch % LG)
    weights = jnp.stack(
        [
            (1.0 - frac_row) * (1.0 - frac_col),
            (1.0 - frac_row) * frac_col,
            frac_row * (1.0 - frac_col),
            frac_row * frac_col,
        ],
        axis=1,
    )
    class_row = (jnp.arange(4, dtype=jnp.int32) == 0).astype(jnp.float32)
    weights = jnp.where((position == 0)[:, None], class_row[None, :], weights)
    onehot = (
        position_source[:, :, None] == jnp.arange(SMALL_LEN, dtype=jnp.int32)[None, None, :]
    ).astype(jnp.float32)
    return jnp.sum(weights[:, :, None] * onehot, axis=1)


def dot_nt(left, right):
    return lax.dot_general(
        left, right, (((1,), (1,)), ((), ())), preferred_element_type=jnp.float32
    )


def dot_nn(left, right):
    return lax.dot_general(
        left, right, (((1,), (0,)), ((), ())), preferred_element_type=jnp.float32
    )


def dot_tn(left, right):
    return lax.dot_general(
        left, right, (((0,), (0,)), ((), ())), preferred_element_type=jnp.float32
    )


def cost(flops, moved):
    return pl.CostEstimate(flops=int(flops), transcendentals=0, bytes_accessed=int(moved))


def after(value, *others):
    return lax.optimization_barrier((value, *others))[0]


def sync(*values):
    return lax.optimization_barrier(values)


def window_start(window, step):
    return pl.multiple_of(jnp.minimum(window * step // 16 * 16, PAD - WINDOW), 16)


def image_of(row, length, step):
    image = jnp.where(row >= length, 1, 0) + jnp.where(row >= 2 * length, 1, 0)
    return jnp.where(row < 0, -1, jnp.where(row >= step, 3, image))


def mask_kernel(s_ref, mask_ref):
    length, step = s_ref[0], s_ref[1]

    def one(window, carry):
        base = window_start(window, step) - window * step
        shape = (WINDOW, 2 * WINDOW)
        rows = image_of(lax.broadcasted_iota(jnp.int32, shape, 0) + base, length, step)
        cols = lax.broadcasted_iota(jnp.int32, shape, 1)
        cols = jnp.where(cols < WINDOW, cols, cols - WINDOW)
        cols = image_of(cols + base, length, step)
        mask_ref[window] = jnp.where(rows == cols, 0.0, FAR).astype(jnp.float32)
        return carry

    lax.fori_loop(0, WINDOWS, one, 0)


def image_masks(lengths):
    return pl.pallas_call(
        mask_kernel,
        out_shape=jax.ShapeDtypeStruct((WINDOWS, WINDOW, 2 * WINDOW), jnp.float32),
        in_specs=[pl.BlockSpec(memory_space=pltpu.SMEM)],
        name="image_masks",
    )(lengths)


MASKS = pl.BlockSpec((WINDOWS, WINDOW, 2 * WINDOW), lambda i, s: (0, 0, 0))


def split_heads(value):
    lane = lax.broadcasted_iota(jnp.int32, value.shape, 1)
    zero = jnp.zeros_like(value)
    even, odd = jnp.where(lane < HEAD_DIM, value, zero), jnp.where(lane < HEAD_DIM, zero, value)
    return jnp.concatenate([even, odd], axis=0)


def slabs(refs, at):
    return [ref[at, i : i + 128] for ref in refs for i in range(0, ref.shape[1], 128)]


def join_heads(value):
    even, odd = value[:WINDOW], value[WINDOW:]
    lane = lax.broadcasted_iota(jnp.int32, even.shape, 1)
    return jnp.where(lane < HEAD_DIM, even, odd)


def keep_rows(ref, start, first, value):
    row = lax.broadcasted_iota(jnp.int32, value.shape, 0) + start
    value = jnp.where(row < ROWS, value, 0.0)
    at = pl.ds(start, WINDOW)
    old = ref[at, :].astype(jnp.float32)
    ref[at, :] = jnp.where(row >= first, value, old).astype(ref.dtype)


def forward_kernel(s_ref, mask_ref, q_ref, k_ref, v_ref, o_ref):
    step = s_ref[1]

    def one(window, carry):
        start = window_start(window, step)
        at = pl.ds(start, WINDOW)
        query = [split_heads(v * LOW(0.125)) for v in slabs([q_ref], at)]
        keys, values = slabs([k_ref], at), slabs([v_ref], at)
        mask = mask_ref[window]
        each = range(len(keys))
        scores = [dot_nt(keys[i], query[i]) + mask for i in each]
        top = [jnp.max(v, axis=0, keepdims=True) for v in scores]
        raised = [jnp.exp(scores[i] - top[i]) for i in each]
        scale = [1.0 / jnp.sum(v, axis=0, keepdims=True) for v in raised]
        out = [dot_tn((raised[i] * scale[i]).astype(LOW), values[i]) for i in each]
        for j in each:
            cols = slice(128 * j, 128 * j + 128)
            keep_rows(o_ref.at[:, cols], start, window * step, join_heads(out[j]))
        return carry

    lax.fori_loop(0, WINDOWS, one, 0)


def backward_kernel(s_ref, mask_ref, *refs):
    q_refs, k_refs, v_refs, g_refs, out_refs = [refs[2 * i : 2 * i + 2] for i in range(5)]
    step = s_ref[1]

    def one(window, carry):
        start = window_start(window, step)
        at = pl.ds(start, WINDOW)
        query = [split_heads(v * LOW(0.125)) for v in slabs(q_refs, at)]
        grad = [split_heads(v) for v in slabs(g_refs, at)]
        keys, values = slabs(k_refs, at), slabs(v_refs, at)
        mask = mask_ref[window]
        each = range(len(keys))
        scores = [dot_nt(keys[i], query[i]) + mask for i in each]
        grad_probs = [dot_nt(values[i], grad[i]) for i in each]
        top = [jnp.max(v, axis=0, keepdims=True) for v in scores]
        raised = [jnp.exp(scores[i] - top[i]) for i in each]
        scale = [1.0 / jnp.sum(v, axis=0, keepdims=True) for v in raised]
        probs = [raised[i] * scale[i] for i in each]
        inner = [jnp.sum(grad_probs[i] * probs[i], axis=0, keepdims=True) for i in each]
        grad_scores = [(probs[i] * (grad_probs[i] - inner[i])).astype(LOW) for i in each]
        grad_v = [dot_nn(probs[i].astype(LOW), grad[i]) for i in each]
        grad_k = [dot_nn(grad_scores[i], query[i]) for i in each]
        grad_q = [dot_tn(grad_scores[i], keys[i]) for i in each]
        first = window * step
        for j in each:
            out = out_refs[j // 2]
            cols = slice(j % 2 * 128, j % 2 * 128 + 128)
            keep_rows(out.at[0, :, cols], start, first, join_heads(grad_q[j]) * 0.125)
            keep_rows(out.at[1, :, cols], start, first, grad_k[j])
            keep_rows(out.at[2, :, cols], start, first, grad_v[j])
        return carry

    lax.fori_loop(0, WINDOWS, one, 0)


def attend_forward(lengths, masks, projected):
    def part(base):
        return pl.BlockSpec((PAD, D), lambda i, s: (0, base))

    return pl.pallas_call(
        forward_kernel,
        out_shape=jax.ShapeDtypeStruct((PAD, D), LOW),
        grid_spec=pltpu.PrefetchScalarGridSpec(
            num_scalar_prefetch=1,
            grid=(1,),
            in_specs=[MASKS, part(0), part(1), part(2)],
            out_specs=part(0),
        ),
        cost_estimate=cost(2e10, 1e7),
        name="attend_forward",
    )(lengths, masks, projected, projected, projected)


def attend_backward(numbers, masks, projected, grad):
    width = D // 4

    def part(base, i):
        return pl.BlockSpec((PAD, width), lambda n, s: (0, s[2 + i] + base))

    return pl.pallas_call(
        backward_kernel,
        out_shape=[jax.ShapeDtypeStruct((3, PAD, width), LOW)] * 2,
        grid_spec=pltpu.PrefetchScalarGridSpec(
            num_scalar_prefetch=1,
            grid=(1,),
            in_specs=[MASKS] + [part(base, i) for base in (0, 4, 8, 0) for i in (0, 1)],
            out_specs=[pl.BlockSpec((3, PAD, width), lambda n, s: (0, 0, 0))] * 2,
        ),
        cost_estimate=cost(2e10, 1e7),
        name="attend_backward",
    )(numbers, masks, *([projected] * 6), grad, grad)


def hidden_kernel(shards, steps, rows, s_ref, x_ref, b_ref, *refs):
    parts, (activ_ref, slope_ref, full), (held, sem) = refs[:5], refs[5:8], refs[8:]
    step = pl.program_id(0)
    tile = activ_ref.shape[1]
    half = held.shape[1] // 2

    def columns(i):
        return fetch_copies(shards, s_ref, parts, held, sem.at[i], i * half, i * half, half)

    def keep():
        return pltpu.make_async_copy(held, full, sem.at[0, 0])

    @pl.when(step == 0)
    def _():
        start_wait(columns(0), wait=False)
        start_wait(columns(1), wait=False)
        start_wait(columns(0), start=False)

    @pl.when(step == steps // 2)
    def _():
        start_wait(columns(1), start=False)
        keep().start()

    weight = held[:, pl.ds(pl.multiple_of(step * tile, tile), tile)]
    for i in range(PAD // rows):
        at = slice(i * rows, (i + 1) * rows)
        hidden = dot_nn(x_ref[at, :], weight) + b_ref[...]
        cdf = 0.5 * lax.erf(hidden * 0.7071067811865476) + 0.5
        density = jnp.exp(-0.5 * hidden * hidden) * 0.3989422804014327
        activ_ref[at, :] = (hidden * cdf).astype(LOW)
        slope_ref[at, :] = (cdf + hidden * density).astype(LOW)

    @pl.when(step == steps - 1)
    def _():
        keep().wait()


def hidden_layer(second, bias, shard, sets):
    width = bias.shape[0]
    tile = 512
    steps = width // tile
    return pl.pallas_call(
        partial(hidden_kernel, lax.axis_size("fsdp"), steps, 736),
        out_shape=[jax.ShapeDtypeStruct((PAD, width), LOW)] * 2 + [fetch_shape(shard, width)],
        grid_spec=pltpu.PrefetchScalarGridSpec(
            num_scalar_prefetch=1,
            grid=(steps,),
            in_specs=[
                pl.BlockSpec((PAD, D), lambda n, s: (0, 0)),
                pl.BlockSpec((1, tile), lambda n, s: (0, n)),
            ]
            + [ANYWHERE] * 5,
            out_specs=[pl.BlockSpec((PAD, tile), lambda n, s: (0, n))] * 2 + [ANYWHERE],
            scratch_shapes=fetch_scratch(shard, width, 2),
        ),
        cost_estimate=cost(2.4e10, 4e7),
        name="hidden_layer",
    )(fetch_numbers(), second, bias.reshape(1, width), shard, *sets)


def hidden_back_kernel(shards, steps, rows, s_ref, g_ref, slope_ref, *refs):
    parts, (out_ref, sum_ref, full), (held, sem) = refs[:5], refs[5:8], refs[8:]
    step = pl.program_id(0)
    per = steps // shards
    tile = out_ref.shape[1]

    def copies():
        return fetch_copies(shards, s_ref, parts, held, sem)

    def keep():
        return pltpu.make_async_copy(held, full, sem.at[0])

    @pl.when(step == 0)
    def _():
        every = copies()
        start_wait(every, wait=False)
        start_wait(every[:1], start=False)

    for k in range(1, shards):

        @pl.when(step == k * per)
        def _(k=k):
            start_wait(copies()[k :: shards - 1], start=False)
            if k == shards - 1:
                keep().start()

    block = lax.rem(s_ref[1] + step // per, shards) * per + step % per
    weight = held[pl.ds(pl.multiple_of(block * tile, tile), tile), :]
    total = jnp.zeros_like(sum_ref)
    for i in range(PAD // rows):
        at = slice(i * rows, (i + 1) * rows)
        grad = dot_nt(g_ref[at, :], weight) * slope_ref[at, :].astype(jnp.float32)
        grad = grad.astype(LOW)
        out_ref[at, :] = grad
        total = total + column_sum(grad.astype(jnp.float32))
    sum_ref[...] = total

    @pl.when(step == steps - 1)
    def _():
        keep().wait()


def hidden_back(grad, slope, shard, sets):
    width = slope.shape[1]
    tile = 512
    steps = width // tile
    shards = lax.axis_size("fsdp")
    per = steps // shards

    def block(n, s):
        return lax.rem(s[1] + n // per, shards) * per + n % per

    cols = pl.BlockSpec((PAD, tile), lambda n, s: (0, block(n, s)))
    return pl.pallas_call(
        partial(hidden_back_kernel, shards, steps, 368),
        out_shape=[
            jax.ShapeDtypeStruct((PAD, width), LOW),
            jax.ShapeDtypeStruct((1, width), jnp.float32),
            fetch_shape(shard),
        ],
        grid_spec=pltpu.PrefetchScalarGridSpec(
            num_scalar_prefetch=1,
            grid=(steps,),
            in_specs=[pl.BlockSpec((PAD, D), lambda n, s: (0, 0)), cols] + [ANYWHERE] * 5,
            out_specs=[cols, pl.BlockSpec((1, tile), lambda n, s: (0, block(n, s))), ANYWHERE],
            scratch_shapes=fetch_scratch(shard),
        ),
        cost_estimate=cost(1.8e10, 4e7),
        name="hidden_back",
    )(fetch_numbers(), grad, slope, shard, *sets)


def normalise(value):
    average = jnp.mean(value, axis=-1, keepdims=True)
    centred = value - average
    inv_std = lax.rsqrt(jnp.mean(centred * centred, axis=-1, keepdims=True) + EPS)
    return centred * inv_std, inv_std


def back_through_norm(grad, normed, inv_std, gain):
    scaled = grad * gain
    inner = (
        scaled
        - jnp.mean(scaled, axis=-1, keepdims=True)
        - normed * jnp.mean(scaled * normed, axis=-1, keepdims=True)
    )
    return inv_std * inner


def column_sum(value):
    return jnp.sum(value, axis=0, keepdims=True)


VECTORS = pl.BlockSpec((8, D), lambda i, *s: (0, 0))
GAIN_ONE, SHIFT_ONE, QUERY, VALUE, OUTPUT, GAIN_TWO, SHIFT_TWO, RETURN = [
    slice(i, i + 1) for i in range(8)
]


def rows_of(width, stacked=0):
    if stacked:
        return pl.BlockSpec((stacked, ROW_TILE, width), lambda i, *s: (0, i, 0))
    return pl.BlockSpec((ROW_TILE, width), lambda i, *s: (i, 0))


def whole(*shape):
    return pl.BlockSpec(shape, lambda i, *s: (0,) * len(shape))


def embed_kernel(tokens_ref, spread_ref, table_ref, vec_ref, stream_ref, first_ref):
    row = lax.broadcasted_iota(jnp.int32, stream_ref.shape, 0) + pl.program_id(0) * ROW_TILE
    tokens = jnp.where(row < ROWS, tokens_ref[...].astype(jnp.float32), 0.0)
    stream = tokens + dot_nn(spread_ref[...], table_ref[...])
    stream_ref[...] = stream
    normed, _ = normalise(stream)
    first_ref[...] = (normed * vec_ref[GAIN_ONE, :] + vec_ref[SHIFT_ONE, :]).astype(LOW)


def embed(tokens, spread, table, vectors):
    slots = spread.shape[1]
    return pl.pallas_call(
        embed_kernel,
        out_shape=[
            jax.ShapeDtypeStruct((PAD, D), jnp.float32),
            jax.ShapeDtypeStruct((PAD, D), LOW),
        ],
        grid=(PAD // ROW_TILE,),
        in_specs=[rows_of(D), rows_of(slots), whole(slots, D), VECTORS],
        out_specs=[rows_of(D), rows_of(D)],
        cost_estimate=cost(1e9, 1.5e7),
        name="embed",
    )(tokens, spread, table, vectors)


def project_kernel(shards, steps, s_ref, a_ref, b_ref, *refs):
    parts, (out_ref, full), (held, sem) = refs[:5], refs[5:7], refs[7:]
    finish = fetch(shards, s_ref, parts, held, full, sem, steps)
    query, value = b_ref[QUERY, :], b_ref[VALUE, :]
    bias = jnp.concatenate([query, jnp.zeros_like(query), value], axis=1)
    out_ref[...] = (dot_nn(a_ref[...], held[...]) + bias).astype(LOW)
    finish()


def project(first, vectors, shard, sets):
    width = shard.shape[1]
    steps = PAD // ROW_TILE
    return pl.pallas_call(
        partial(project_kernel, lax.axis_size("fsdp"), steps),
        out_shape=[jax.ShapeDtypeStruct((PAD, width), LOW), fetch_shape(shard)],
        grid_spec=pltpu.PrefetchScalarGridSpec(
            num_scalar_prefetch=1,
            grid=(steps,),
            in_specs=[rows_of(D), VECTORS] + [ANYWHERE] * 5,
            out_specs=[rows_of(width), ANYWHERE],
            scratch_shapes=fetch_scratch(shard),
        ),
        cost_estimate=cost(2 * PAD * D * width, 2e7),
        name="project",
    )(fetch_numbers(), first, vectors, shard, *sets)


def branch_kernel(shards, steps, s_ref, a_ref, stream_ref, vec_ref, *refs):
    parts, (mid_ref, second_ref, full), (held, sem) = refs[:5], refs[5:8], refs[8:]
    first = parts[0].shape[1] - D
    finish = fetch(shards, s_ref, parts, held, full, sem, steps, first)
    mid = stream_ref[...] + dot_nn(a_ref[...], held[...]) + vec_ref[OUTPUT, :]
    mid_ref[...] = mid
    normed, _ = normalise(mid)
    second_ref[...] = (normed * vec_ref[GAIN_TWO, :] + vec_ref[SHIFT_TWO, :]).astype(LOW)
    finish()


def branch(attended, stream, vectors, shard, sets):
    steps = PAD // ROW_TILE
    return pl.pallas_call(
        partial(branch_kernel, lax.axis_size("fsdp"), steps),
        out_shape=[
            jax.ShapeDtypeStruct((PAD, D), jnp.float32),
            jax.ShapeDtypeStruct((PAD, D), LOW),
            fetch_shape(shard, D),
        ],
        grid_spec=pltpu.PrefetchScalarGridSpec(
            num_scalar_prefetch=1,
            grid=(steps,),
            in_specs=[rows_of(D), rows_of(D), VECTORS] + [ANYWHERE] * 5,
            out_specs=[rows_of(D), rows_of(D), ANYWHERE],
            scratch_shapes=fetch_scratch(shard, D),
        ),
        cost_estimate=cost(2 * PAD * D * D, 3e7),
        name="branch",
    )(fetch_numbers(), attended, stream, vectors, shard, *sets)


def return_kernel(a_ref, w_ref, mid_ref, vec_ref, out_ref):
    value = mid_ref[...] + dot_nn(a_ref[...], w_ref[...]) + vec_ref[RETURN, :]
    out_ref[...] = value.astype(LOW)


def return_layer(activ, weight, mid, vectors):
    width = weight.shape[0]
    return pl.pallas_call(
        return_kernel,
        out_shape=jax.ShapeDtypeStruct((ROWS, D), LOW),
        grid=(PAD // ROW_TILE,),
        in_specs=[rows_of(width), whole(width, D), rows_of(D), VECTORS],
        out_specs=rows_of(D),
        cost_estimate=cost(2 * PAD * D * width, 3e7),
        name="return_layer",
    )(activ, weight, mid, vectors)


def second_back_kernel(
    h_ref, w_ref, o_ref, mid_ref, g_ref, gain_ref, out_ref, low_ref, att_ref, sums_ref
):
    @pl.when(pl.program_id(0) == 0)
    def _():
        sums_ref[...] = jnp.zeros_like(sums_ref)

    grad = dot_nt(h_ref[...], w_ref[...])
    normed, inv_std = normalise(mid_ref[...])
    out = g_ref[...].astype(jnp.float32)
    sums_ref[3:4, :] += column_sum(out)
    out = out + back_through_norm(grad, normed, inv_std, gain_ref[GAIN_TWO, :])
    out_ref[...] = out
    low = out.astype(LOW)
    low_ref[...] = low
    att_ref[...] = dot_nt(low, o_ref[...]).astype(LOW)
    sums_ref[0:1, :] += column_sum(low.astype(jnp.float32))
    sums_ref[1:2, :] += column_sum(grad * normed)
    sums_ref[2:3, :] += column_sum(grad)


def second_back(grad_hidden, weight, output, mid, grad, vectors):
    width = grad_hidden.shape[1]
    return pl.pallas_call(
        second_back_kernel,
        out_shape=[
            jax.ShapeDtypeStruct((PAD, D), jnp.float32),
            jax.ShapeDtypeStruct((PAD, D), LOW),
            jax.ShapeDtypeStruct((PAD, D), LOW),
            jax.ShapeDtypeStruct((8, D), jnp.float32),
        ],
        grid=(PAD // ROW_TILE,),
        in_specs=[
            rows_of(width),
            whole(D, width),
            whole(D, D),
            rows_of(D),
            rows_of(D),
            VECTORS,
        ],
        out_specs=[rows_of(D), rows_of(D), rows_of(D), whole(8, D)],
        cost_estimate=cost(2 * PAD * D * width, 4e7),
        name="second_back",
    )(grad_hidden, weight, output, mid, grad, vectors)


def first_back_kernel(s_ref, *refs):
    heads, w_refs, (stream_ref, mid_ref, spread_ref, gain_ref) = refs[:4], refs[4:16], refs[16:20]
    out_ref, table_ref, sums_ref = refs[20:]

    @pl.when(pl.program_id(0) == 0)
    def _():
        sums_ref[...] = jnp.zeros_like(sums_ref)
        table_ref[...] = jnp.zeros_like(table_ref)

    grad = 0.0
    for j, ref in enumerate(heads):
        for t in range(3):
            grad = grad + dot_nt(ref[t], w_refs[3 * j + t][...])
    normed, inv_std = normalise(stream_ref[...])
    out = mid_ref[...] + back_through_norm(grad, normed, inv_std, gain_ref[GAIN_ONE, :])
    low = out.astype(LOW)
    out_ref[...] = low
    rest = (out - low.astype(jnp.float32)).astype(LOW)
    table_ref[...] += dot_tn(spread_ref[...], low) + dot_tn(spread_ref[...], rest)
    sums_ref[0:1, :] += column_sum(grad * normed)
    sums_ref[1:2, :] += column_sum(grad)
    for j, ref in enumerate(heads):
        width = ref.shape[2]
        at = pl.ds(pl.multiple_of(s_ref[j] * width, width), width)
        sums_ref[2:3, at] += column_sum(ref[0].astype(jnp.float32))
        sums_ref[3:4, at] += column_sum(ref[2].astype(jnp.float32))


def first_back(quarters, heads, joined, stream, grad_mid, spread, vectors):
    width = D // 4
    w_specs = [
        pl.BlockSpec((D, width), lambda i, s, j=j, t=t: (0, 4 * t + s[j]))
        for j in range(4)
        for t in range(3)
    ]
    slots = spread.shape[1]
    return pl.pallas_call(
        first_back_kernel,
        out_shape=[
            jax.ShapeDtypeStruct((ROWS, D), LOW),
            jax.ShapeDtypeStruct((slots, D), jnp.float32),
            jax.ShapeDtypeStruct((8, D), jnp.float32),
        ],
        grid_spec=pltpu.PrefetchScalarGridSpec(
            num_scalar_prefetch=1,
            grid=(PAD // ROW_TILE,),
            in_specs=[rows_of(width, 3)] * 4
            + w_specs
            + [rows_of(D), rows_of(D), rows_of(slots), VECTORS],
            out_specs=[rows_of(D), whole(slots, D), whole(8, D)],
        ),
        cost_estimate=cost(2 * PAD * D * 3 * D, 4e7),
        name="first_back",
    )(quarters, *heads, *([joined] * 12), stream, grad_mid, spread, vectors)


def widen_kernel(moves, count, *refs):
    for source, at, target, block, to, width in moves:
        rows = refs[source].shape[2]
        down = slice(block * rows, (block + 1) * rows)
        for core in (0, 1):
            value = refs[source][0, core, :, at : at + width].astype(jnp.float32)
            refs[count + target][down, to[core] : to[core] + width] = value


def widen(sources, shapes, moves):
    rows = sources[0].shape[1]
    return pl.pallas_call(
        partial(widen_kernel, moves, len(sources)),
        out_shape=[jax.ShapeDtypeStruct((4 * n * rows, w), jnp.float32) for n, w in shapes],
        grid=(4,),
        in_specs=[
            pl.BlockSpec((1, 2, rows, v.shape[2]), lambda i: (i, 0, 0, 0)) for v in sources
        ],
        out_specs=[pl.BlockSpec((n * rows, w), lambda i: (i, 0)) for n, w in shapes],
        cost_estimate=cost(1, 6e6),
        name="widen",
    )(*[v.reshape(4, 2, rows, v.shape[2]) for v in sources])


def grad_value(f_ref, a_ref, b_ref):
    if len(b_ref.shape) == 2:
        return dot_tn(a_ref[...], b_ref[...]) * f_ref[0]
    return jnp.concatenate([dot_tn(a_ref[...], b_ref[i]) for i in range(3)], axis=1) * f_ref[0]


def grad_send_kernel(c_ref, f_ref, a_ref, b_ref, out_ref):
    out_ref[...] = grad_value(f_ref, a_ref, b_ref).astype(LOW)


def grad_keep_kernel(planes, c_ref, f_ref, a_ref, b_ref, got_ref, *refs):
    keep_ref, send_ref = refs[-2:]
    value = (grad_value(f_ref, a_ref, b_ref) + got_ref[...].astype(jnp.float32)).astype(LOW)
    core, place = c_ref[0], c_ref[1]
    rows = value.shape[0] // planes // 4
    for quarter in range(4):
        bits = place ^ quarter
        role = jnp.where(core == 0, bits, (bits >> 1) | ((bits & 1) << 1))
        for ref, near in ((keep_ref, 0), (send_ref, 1)):

            @pl.when(role % 2 == near)
            def _(ref=ref, quarter=quarter, role=role):
                for plane in range(planes):
                    at = (plane * 4 + quarter) * rows
                    ref[role // 2, plane] = value[at : at + rows]


def grad_half(
    numbers, factor, left, right, got=None, tile_m=1024, tile_n=512, width=None, first=0, into=()
):
    rows = left.shape[1]
    shards = lax.axis_size("fsdp")
    stacked = right.ndim == 3
    cols = 3 * right.shape[2] if stacked else right.shape[1] // 2
    tile_n = cols if stacked else tile_n
    steps = cols // tile_n
    in_specs = [
        pl.BlockSpec(memory_space=pltpu.SMEM),
        pl.BlockSpec((PAD, tile_m), lambda m, n, c: (0, m)),
    ]
    if stacked:
        in_specs.append(pl.BlockSpec((3, PAD, cols // 3), lambda m, n, c: (0, 0, 0)))
    else:
        in_specs.append(pl.BlockSpec((PAD, tile_n), lambda m, n, c: (0, n + c[0] * steps)))
    flat_spec = pl.BlockSpec((tile_m, tile_n), lambda m, n, c: (m, n))
    operands = [numbers, factor, left, right]
    if got is None:
        kernel, name = grad_send_kernel, "grad_send"
        out_shape, out_specs = jax.ShapeDtypeStruct((rows, cols), LOW), flat_spec
    else:
        planes = tile_m * shards // rows
        part = rows // shards // 4
        kernel, name = partial(grad_keep_kernel, planes), "grad_keep"
        in_specs.append(flat_spec)
        operands.append(got)
        out_shape = [jax.ShapeDtypeStruct((2, shards, part, width or cols), LOW)] * 2
        out_specs = [
            pl.BlockSpec((2, planes, part, tile_n), lambda m, n, c: (0, m, 0, n + first // tile_n))
        ] * 2
        in_specs += [ANYWHERE] * len(into)
        operands += into
    return pl.pallas_call(
        kernel,
        out_shape=out_shape,
        grid_spec=pltpu.PrefetchScalarGridSpec(
            num_scalar_prefetch=1,
            grid=(rows // tile_m, steps),
            in_specs=in_specs,
            out_specs=out_specs,
        ),
        input_output_aliases={5 + i: i for i in range(len(into))},
        cost_estimate=cost(2 * PAD * rows * cols, 1e7),
        name=name,
    )(*operands)


def swap(value, even, odd):
    size = lax.axis_size("dp")
    return lax.ppermute(value, "dp", [(i, i ^ (odd if i % 2 else even)) for i in range(size)])


def swap_core(value):
    return swap(value, 1, 1)


def swap_first(value):
    return swap(value, 2, 4)


def swap_second(value):
    return swap(value, 4, 2)


def own_piece(shard):
    part = shard.shape[0] // GROUP
    place = lax.axis_index("dp") % GROUP
    return lax.dynamic_slice_in_dim(shard, place * part, part, 0)


def from_above(piece):
    shards = lax.axis_size("fsdp")
    return [
        lax.ppermute(piece, "fsdp", [((i + k) % shards, i) for i in range(shards)])
        for k in range(1, shards)
    ]


def gather_z_native(piece):
    return lax.all_gather(piece, "fsdp", axis=0, tiled=False)


def others(every):
    shards = every.shape[0]
    twice = jnp.concatenate([every, every[:-1]], axis=0)
    return lax.dynamic_slice_in_dim(twice, lax.axis_index("fsdp") + 1, shards - 1, 0)


def gather_first(own):
    return own, swap_first(own)


def gather_second(own, got):
    both = jnp.stack([own, got])
    return both, swap_second(both)


def gather_core(both, far):
    return both, far, swap_core(both), swap_core(far)


def fetch_copies(shards, s_ref, refs, held, sem, first=0, at_col=0, cols=None):
    own, sets = refs[0], refs[1:]
    place, row = s_ref[0], s_ref[1]
    rows = own.shape[0]
    cols = cols or own.shape[1]
    part = rows // GROUP
    source_cols, held_cols = pl.ds(first, cols), pl.ds(at_col, cols)
    copies = [
        pltpu.make_async_copy(
            own.at[:, source_cols],
            held.at[pl.ds(pl.multiple_of(row * rows, rows), rows), held_cols],
            sem.at[0],
        )
    ]
    for flip in range(2):
        base = place ^ flip
        first_bits = jnp.where(base % 2 == 0, 2, 4)
        for source, bits in (
            (sets[2 * flip].at[0], 0),
            (sets[2 * flip].at[1], first_bits),
            (sets[2 * flip + 1].at[0], 6 - first_bits),
            (sets[2 * flip + 1].at[1], 6),
        ):
            for k in range(1, shards):
                at = lax.rem(row + k, shards) * rows + (base ^ bits) * part
                target = held.at[pl.ds(pl.multiple_of(at, part), part), held_cols]
                copies.append(
                    pltpu.make_async_copy(
                        source.at[k - 1, :, source_cols], target, sem.at[len(copies)]
                    )
                )
    return copies


def start_wait(copies, start=True, wait=True):
    for copy in copies if start else ():
        copy.start()
    for copy in copies if wait else ():
        copy.wait()


def fetch(shards, s_ref, refs, held, full, sem, steps, first=0):
    def keep():
        return pltpu.make_async_copy(held, full, sem.at[0])

    @pl.when(pl.program_id(0) == 0)
    def _():
        start_wait(fetch_copies(shards, s_ref, refs, held, sem, first, 0, held.shape[1]))
        keep().start()

    def finish():
        @pl.when(pl.program_id(0) == steps - 1)
        def _():
            keep().wait()

    return finish


def fetch_numbers():
    place = lax.axis_index("dp") % GROUP
    return jnp.stack([place, lax.axis_index("fsdp")]).astype(jnp.int32)


def fetch_scratch(shard, cols=None, sets=1):
    shards = lax.axis_size("fsdp")
    count = 1 + 8 * (shards - 1)
    return [
        pltpu.VMEM((shards * shard.shape[0], cols or shard.shape[1]), shard.dtype),
        pltpu.SemaphoreType.DMA((count,) if sets == 1 else (sets, count)),
    ]


def fetch_shape(shard, cols=None):
    shards = lax.axis_size("fsdp")
    return jax.ShapeDtypeStruct((shards * shard.shape[0], cols or shard.shape[1]), shard.dtype)


def plane_gather(value, axis):
    size = lax.axis_size("dp")
    groups = None
    if size > GROUP:
        groups = [[g * GROUP + i for i in range(GROUP)] for g in range(size // GROUP)]
    return lax.all_gather(value, "dp", axis=axis, tiled=False, axis_index_groups=groups)


def rest_sum(value):
    size = lax.axis_size("dp")
    if size == GROUP:
        return value
    groups = [[g * GROUP + i for g in range(size // GROUP)] for i in range(GROUP)]
    return lax.psum(value, "dp", axis_index_groups=groups)


def add_low(left, right):
    return (left.astype(jnp.float32) + right.astype(jnp.float32)).astype(LOW)


def sum_first(got, keep):
    return add_low(keep[0], got[0]), swap_second(add_low(keep[1], got[1]))


def sum_z(both):
    shards, part, cols = both.shape
    piece = lax.psum_scatter(
        both.reshape(shards * part, cols), "fsdp", scatter_dimension=0, tiled=True
    )
    return rest_sum(piece)


def sum_z_direct(value):
    shards = lax.axis_size("fsdp")
    me = lax.axis_index("fsdp")
    total = lax.dynamic_index_in_dim(value, me, 0, keepdims=False).astype(jnp.float32)
    for step in range(1, shards):
        send = lax.dynamic_index_in_dim(value, (me + step) % shards, 0, keepdims=False)
        got = lax.ppermute(send, "fsdp", [(i, (i + step) % shards) for i in range(shards)])
        total = total + got.astype(jnp.float32)
    return total


def pack_kernel(s_ref, piece_ref, *refs):
    out_ref, rows_ref = refs[-2:]
    width, first = rows_ref.shape[1], piece_ref.shape[1]
    out_ref[:, :first] = piece_ref[...]
    rows_ref[...] = jnp.zeros_like(rows_ref)
    row = 0
    for ref in refs[:-2]:
        if len(ref.shape) == 2:
            rows_ref[row : row + ref.shape[0], :] = ref[...]
            row += ref.shape[0]
            continue
        for i in range(0, ref.shape[0], width):
            rows_ref[row : row + 1, :] = ref[i : i + width].reshape(1, width)
            row += 1
    tall = out_ref.shape[0]
    for i in range(rows_ref.shape[0] // tall):
        at = first + i * width
        out_ref[:, at : at + width] = rows_ref[i * tall : (i + 1) * tall, :]


def pack(shard, vectors, table):
    rows, cols = shard.shape
    tall, width = rows // GROUP, vectors[0].shape[0]
    wide = cols + 64 // tall * width
    place = (lax.axis_index("dp") % GROUP).astype(jnp.int32).reshape(1)
    return pl.pallas_call(
        pack_kernel,
        out_shape=jax.ShapeDtypeStruct((tall, wide), LOW),
        grid_spec=pltpu.PrefetchScalarGridSpec(
            num_scalar_prefetch=1,
            grid=(1,),
            in_specs=[pl.BlockSpec((tall, cols), lambda i, s: (s[0], 0))]
            + [pl.BlockSpec(v.shape, lambda i, s: (0,)) for v in vectors]
            + [pl.BlockSpec(table.shape, lambda i, s: (0, 0))],
            out_specs=pl.BlockSpec((tall, wide), lambda i, s: (0, 0)),
            scratch_shapes=[pltpu.VMEM((64, width), LOW)],
        ),
        cost_estimate=cost(1, 1e5),
        name="pack",
    )(place, shard, *vectors, table)


def unpack_kernel(s_ref, *refs):
    parts, (out_ref, table_ref, rows_ref) = refs[:-3], refs[-3:]
    width = rows_ref.shape[1]
    tall = parts[0].shape[0]
    table_ref[...] = jnp.zeros_like(table_ref)
    for k, ref in enumerate(parts):
        at = lax.rem(s_ref[0] + k, len(parts)) * width
        at = pl.ds(pl.multiple_of(at, width), width)
        for i in range(64 // tall):
            rows_ref[i * tall : (i + 1) * tall, :] = ref[:, i * width : (i + 1) * width]
        out_ref[:, at] = rows_ref[...].astype(jnp.float32)
        table = rows_ref[12 : 12 + SMALL_LEN, :]
        table_ref[0:SMALL_LEN, at] = table
        table_ref[64 : 64 + SMALL_LEN, at] = table


def unpack(parts, first, width):
    shards = len(parts)
    tall = parts[0].shape[0]
    wide = parts[0].shape[1] - first
    return pl.pallas_call(
        unpack_kernel,
        out_shape=[
            jax.ShapeDtypeStruct((64, shards * width), jnp.float32),
            jax.ShapeDtypeStruct((128, shards * width), LOW),
        ],
        grid=(1,),
        in_specs=[pl.BlockSpec(memory_space=pltpu.SMEM)]
        + [pl.BlockSpec((tall, wide), lambda i: (0, first // wide))] * shards,
        out_specs=[
            pl.BlockSpec((64, shards * width), lambda i: (0, 0)),
            pl.BlockSpec((128, shards * width), lambda i: (0, 0)),
        ],
        scratch_shapes=[pltpu.VMEM((64, width), LOW)],
        cost_estimate=cost(1, 1e6),
        name="unpack",
    )(lax.axis_index("fsdp").astype(jnp.int32).reshape(1), *parts)


def per_device(
    tokens,
    output_grad,
    group_member,
    image_counts,
    position_source,
    position_table,
    first_gain,
    first_shift,
    input_proj,
    query_bias,
    value_bias,
    output_proj,
    output_bias,
    second_gain,
    second_shift,
    hidden_weight,
    hidden_bias,
    return_weight,
    return_bias,
):
    dp_size = lax.axis_size("dp")
    fsdp_size = lax.axis_size("fsdp")
    core = (lax.axis_index("dp") & 1).astype(jnp.int32)
    quarter = ((lax.axis_index("dp") % GROUP) >> 1).astype(jnp.int32)
    mine, other = jnp.stack([core, quarter]), jnp.stack([1 - core, quarter])
    vectors = (
        first_gain,
        first_shift,
        query_bias,
        value_bias,
        output_bias,
        second_gain,
        second_shift,
        return_bias,
        hidden_bias,
    )
    packed_own = pack(input_proj, vectors, position_table)
    parts = from_above(packed_own)
    hidden_shard = jnp.concatenate([hidden_weight, output_proj], axis=1)
    hidden_own = own_piece(hidden_weight)
    output_own = own_piece(output_proj)
    return_z = own_piece(return_weight)
    member = group_member[0]
    is_large = member == 1
    length = jnp.where(is_large, LARGE_LEN, SMALL_LEN)
    step = jnp.where(is_large, LARGE_LEN, 3 * SMALL_LEN)
    group_high = dp_size * 7 // 16
    group_low = dp_size - group_high
    counts = image_counts.astype(jnp.float32)
    share = jnp.where(is_large, counts[1], counts[0]) / (counts[0] + counts[1])
    images = jnp.where(
        is_large,
        group_high * fsdp_size * (ROWS // LARGE_LEN),
        group_low * fsdp_size * (ROWS // SMALL_LEN),
    ).astype(jnp.float32)
    factor = share / images
    scale = factor.reshape(1)

    row_index = jnp.arange(PAD, dtype=jnp.int32)
    place = jnp.where(row_index < ROWS, row_index % length, -1)
    inter = interp_table(position_source)
    identity = (
        jnp.arange(LARGE_LEN, dtype=jnp.int32)[:, None]
        == jnp.arange(SMALL_LEN, dtype=jnp.int32)[None, :]
    ).astype(jnp.float32)
    mixing = jnp.where(is_large, inter, identity)
    picker = (place[:, None] == jnp.arange(LARGE_LEN, dtype=jnp.int32)[None, :]).astype(jnp.float32)
    spread = jnp.dot(picker, mixing, precision=lax.Precision.HIGHEST)
    lengths = jnp.stack([length, step])
    upper = spread.astype(LOW)
    lower = (spread - upper.astype(jnp.float32)).astype(LOW)
    spread_low = jnp.concatenate(
        [jnp.pad(v, ((0, 0), (0, 64 - SMALL_LEN))) for v in (upper, lower)], axis=1
    )

    quarters = jnp.stack([2 * core, 2 - 2 * core, 2 * core + 1, 3 - 2 * core])
    numbers_one = jnp.concatenate([lengths, quarters[:2]])
    numbers_two = jnp.concatenate([lengths, quarters[2:]])
    spread_low, scale, mine, other, lengths, numbers_one, numbers_two, hidden_own, *parts = sync(
        spread_low, scale, mine, other, lengths, numbers_one, numbers_two, hidden_own, *parts
    )
    joint_z = jnp.stack([v[:, : 3 * D] for v in parts])
    smalls, table_pair = unpack([packed_own] + parts, 3 * D, first_gain.shape[0])
    hidden_add = smalls[8:12].reshape(4, fsdp_size, -1).transpose(1, 0, 2).reshape(-1)
    joint_one = gather_first(joint_z)
    hidden_z = gather_z_native(after(hidden_own, joint_z))
    output_z = from_above(after(output_own, joint_z))
    stream, first_low = embed(tokens, spread_low, table_pair, smalls)
    first_low, *joint_one = sync(first_low, *joint_one)
    joint_two = gather_second(*joint_one)
    output_grad, lengths, _ = sync(output_grad, lengths, joint_two[0])
    masks = image_masks(lengths)
    grad_pad = jnp.pad(output_grad, ((0, PAD - ROWS), (0, 0)))
    output_z = jnp.stack(output_z)
    *joint_two, hidden_z, output_z, hidden_add, return_z, grad_pad, masks = sync(
        *joint_two, hidden_z, output_z, hidden_add, return_z, grad_pad, masks
    )
    joint_sets = gather_core(*joint_two)
    first_low, *joint_sets = sync(first_low, *joint_sets)
    hidden_one = gather_first(jnp.concatenate([others(hidden_z), output_z], axis=-1))
    return_early, *return_late = from_above(return_z)
    projected, joint_full = project(
        after(first_low, hidden_one[0]), smalls, input_proj, joint_sets
    )
    projected, return_early, *hidden_one = sync(projected, return_early, *hidden_one)
    hidden_two = gather_second(*hidden_one)
    projected = after(projected, hidden_two[0])
    attended = attend_forward(lengths, masks, projected)
    attended, *rest = sync(attended, *hidden_two, *return_late)
    hidden_two, return_late = rest[:2], rest[2:]
    hidden_sets = gather_core(*hidden_two)
    return_one = gather_first(jnp.stack([return_early, *return_late]))
    attended, *hidden_sets = sync(attended, *hidden_sets)
    mid, second, outproj_full = branch(
        after(attended, return_one[0]),
        stream,
        smalls,
        hidden_shard,
        hidden_sets,
    )
    second, *return_one = sync(second, *return_one)
    return_two = gather_second(*return_one)
    activ, slope, hidden_full = hidden_layer(
        after(second, return_two[0]), hidden_add, hidden_shard, hidden_sets
    )
    activ, slope, *return_two = sync(activ, slope, *return_two)
    return_sets = gather_core(*return_two)
    return_send = grad_half(other, scale, activ, grad_pad)
    return_send, *return_sets = sync(return_send, *return_sets)
    return_got = swap_core(return_send)
    grad_hidden, grad_hidden_add, return_full = hidden_back(
        after(grad_pad, return_send), slope, return_weight, return_sets
    )
    grad_hidden, return_got = sync(grad_hidden, return_got)
    return_keep, return_out = grad_half(mine, scale, activ, grad_pad, return_got)
    return_in = swap_first(return_out)
    hidden_send = grad_half(other, scale, after(second, return_out), grad_hidden)
    hidden_got = swap_core(hidden_send)
    grad_mid, grad_branch, grad_att, sums_two = second_back(
        after(grad_hidden, hidden_send), hidden_full, outproj_full, mid, grad_pad, smalls
    )
    grad_branch, hidden_got, return_in = sync(grad_branch, hidden_got, return_in)
    return_kept, return_in = sum_first(return_in, return_keep)
    hidden_keep, hidden_out = grad_half(
        mine, scale, after(second, return_kept), grad_hidden, hidden_got
    )
    hidden_out, grad_branch, return_in = sync(hidden_out, grad_branch, return_in)
    hidden_in = swap_first(hidden_out)
    output_send = grad_half(other, scale, attended, grad_branch)
    output_got = swap_core(output_send)
    return_piece = sum_z(add_low(return_kept, return_in))
    mine_one, other_one = attend_backward(
        numbers_one, masks, projected, after(grad_att, output_send)
    )
    mine_one, other_one, output_got, hidden_in, return_piece = sync(
        mine_one, other_one, output_got, hidden_in, return_piece
    )
    hidden_kept, hidden_in = sum_first(hidden_in, hidden_keep)
    joint_send = grad_half(other, scale, after(first_low, hidden_kept), other_one, tile_m=512)
    joint_got = swap_core(joint_send)
    wide = dict(width=5 * D // 4)
    output_pair = grad_half(
        mine,
        scale,
        attended,
        after(grad_branch, joint_send),
        output_got,
        tile_n=256,
        first=3 * D // 4,
        **wide,
    )
    *output_pair, joint_got = sync(*output_pair, joint_got)
    joint_keep, joint_out = grad_half(
        mine, scale, first_low, mine_one, joint_got, tile_m=512, into=output_pair, **wide
    )
    joint_out, hidden_in = sync(joint_out, hidden_in)
    joint_in = swap_first(joint_out)
    hidden_piece = sum_z(add_low(hidden_kept, hidden_in))
    mine_two, other_two = attend_backward(
        numbers_two, masks, projected, after(grad_att, joint_out)
    )
    mine_two, other_two, joint_in, hidden_piece = sync(mine_two, other_two, joint_in, hidden_piece)
    joint_kept, joint_in = sum_first(joint_in, joint_keep)
    last_send = grad_half(other, scale, after(first_low, joint_kept), other_two, tile_m=512)
    last_got = swap_core(last_send)
    last_keep, last_out = grad_half(mine, scale, first_low, mine_two, last_got, tile_m=512)
    last_out, joint_in = sync(last_out, joint_in)
    joint_piece = sum_z(add_low(joint_kept, joint_in))
    last_in = swap_first(last_out)
    heads = sync(mine_one, other_one, mine_two, other_two, last_out)[:4]
    tokens_grad, grad_table, sums_one = first_back(
        quarters, heads, joint_full, stream, grad_mid, spread_low, smalls
    )
    tokens_grad, grad_table, sums_one, last_in, joint_piece = sync(
        tokens_grad, grad_table, sums_one, last_in, joint_piece
    )
    last_kept, last_in = sum_first(last_in, last_keep)
    rows = joint_piece.shape[0]
    blocks = return_piece.shape[0] // rows
    pieces = [return_piece[i * rows : (i + 1) * rows] for i in range(blocks)]
    pieces += [hidden_piece, joint_piece]
    return_cols, hidden_cols = blocks * return_piece.shape[1], hidden_piece.shape[1]
    every = plane_gather(jnp.concatenate(pieces, axis=1), axis=0)

    grad_table = grad_table[:SMALL_LEN] + grad_table[64 : 64 + SMALL_LEN]
    hidden_rows = grad_hidden_add.reshape(fsdp_size, 4, -1).transpose(1, 0, 2).reshape(4, D)
    packed = jnp.concatenate([sums_one[:4], sums_two[:4], hidden_rows, grad_table], axis=0) * scale[0]
    packed = jnp.pad(packed, ((0, smalls.shape[0] - packed.shape[0]), (0, 0))).astype(LOW)
    packed = packed.reshape(packed.shape[0], fsdp_size, -1).transpose(1, 0, 2)
    packed, last_in = sync(packed, last_in)
    last_both = add_low(last_kept, last_in)
    last_cols = last_both.shape[-1]
    packed = packed.reshape(fsdp_size, rows, -1)
    last_both = jnp.concatenate([last_both, packed], axis=-1)
    last_piece = sum_z_direct(last_both).astype(LOW)
    block_out = return_layer(after(activ, last_both), return_full, mid, smalls)
    block_out, last_piece = sync(block_out, last_piece)
    small_rows = 12 + SMALL_LEN
    wide = first_gain.shape[0]
    small_piece = last_piece[:, last_cols:].reshape(-1, wide)[:small_rows].reshape(rows, -1)
    last_piece = jnp.concatenate([last_piece[:, :last_cols], small_piece], axis=1)
    last_every = plane_gather(rest_sum(last_piece), axis=0)
    summed = jnp.sum(last_every[:, :, last_cols:].astype(jnp.float32), axis=0)
    summed = summed.reshape(small_rows, -1)
    half, part = D // 2, D // 4
    moves = [(0, i * half, 0, i, (0, half), half) for i in range(blocks)]
    moves.append((0, return_cols, 1, 0, (0, 2 * D), 2 * D))
    for t in range(3):
        to = (t * D, t * D + half)
        moves.append((0, return_cols + hidden_cols + t * part, 2, 0, to, part))
        moves.append((1, t * part, 2, 0, (to[0] + part, to[1] + part), part))
    moves.append((0, return_cols + hidden_cols + 3 * part, 3, 0, (0, half), half))
    return_w_out, hidden_w_out, joint_out, outproj_out = widen(
        [every, last_every], [(blocks, D), (1, 4 * D), (1, 3 * D), (1, D)], moves
    )
    return (
        block_out,
        tokens_grad,
        summed[12 : 12 + SMALL_LEN],
        summed[0],
        summed[1],
        joint_out,
        summed[2],
        summed[3],
        outproj_out,
        summed[4],
        summed[5],
        summed[6],
        hidden_w_out,
        summed[8:12].reshape(-1),
        return_w_out,
        summed[7],
    )


def solution(mesh):
    in_specs = (
        P(("dp", "fsdp"), None),
        P(("dp", "fsdp"), None),
        P("dp"),
        P(),
        P(),
        P(None, "fsdp"),
        P("fsdp"),
        P("fsdp"),
        P("fsdp", None),
        P("fsdp"),
        P("fsdp"),
        P("fsdp", None),
        P("fsdp"),
        P("fsdp"),
        P("fsdp"),
        P("fsdp", None),
        P("fsdp"),
        P("fsdp", None),
        P("fsdp"),
    )
    out_specs = (
        P(("dp", "fsdp"), None),
        P(("dp", "fsdp"), None),
        P(None, "fsdp"),
        P("fsdp"),
        P("fsdp"),
        P("fsdp", None),
        P("fsdp"),
        P("fsdp"),
        P("fsdp", None),
        P("fsdp"),
        P("fsdp"),
        P("fsdp"),
        P("fsdp", None),
        P("fsdp"),
        P("fsdp", None),
        P("fsdp"),
    )
    return jax.shard_map(
        per_device, mesh=mesh, in_specs=in_specs, out_specs=out_specs, check_vma=False
    )
```

```python
from functools import partial

import jax
import jax.numpy as jnp
from jax import lax
from jax.experimental import pallas as pl
from jax.experimental.pallas import tpu as pltpu
from jax.sharding import PartitionSpec as P

D = 1024
HEADS = 16
HEAD_DIM = 64
SG = 7
LG = 12
SMALL_LEN = 50
LARGE_LEN = 145
ROWS = 1450
PAD = 1472
GROUP = 8
WINDOW = 176
WINDOWS = 10
ROW_TILE = 368
FAR = -1e30
LOW = jnp.bfloat16
ANYWHERE = pl.BlockSpec(memory_space=pl.ANY)


EPS = 1e-06


def grid_fraction(index):
    scaled = jnp.maximum((2 * index + 1) * SG - LG, 0)
    lower = scaled // (2 * LG)
    return (scaled - 2 * LG * lower).astype(jnp.float32) / (2.0 * LG)


def interp_table(position_source):
    position = jnp.arange(LARGE_LEN, dtype=jnp.int32)
    patch = jnp.maximum(position - 1, 0)
    frac_row = grid_fraction(patch // LG)
    frac_col = grid_fraction(patch % LG)
    weights = jnp.stack(
        [
            (1.0 - frac_row) * (1.0 - frac_col),
            (1.0 - frac_row) * frac_col,
            frac_row * (1.0 - frac_col),
            frac_row * frac_col,
        ],
        axis=1,
    )
    class_row = (jnp.arange(4, dtype=jnp.int32) == 0).astype(jnp.float32)
    weights = jnp.where((position == 0)[:, None], class_row[None, :], weights)
    onehot = (
        position_source[:, :, None] == jnp.arange(SMALL_LEN, dtype=jnp.int32)[None, None, :]
    ).astype(jnp.float32)
    return jnp.sum(weights[:, :, None] * onehot, axis=1)


def dot_nt(left, right):
    return lax.dot_general(
        left, right, (((1,), (1,)), ((), ())), preferred_element_type=jnp.float32
    )


def dot_nn(left, right):
    return lax.dot_general(
        left, right, (((1,), (0,)), ((), ())), preferred_element_type=jnp.float32
    )


def dot_tn(left, right):
    return lax.dot_general(
        left, right, (((0,), (0,)), ((), ())), preferred_element_type=jnp.float32
    )


def cost(flops, moved):
    return pl.CostEstimate(flops=int(flops), transcendentals=0, bytes_accessed=int(moved))


def after(value, *others):
    return lax.optimization_barrier((value, *others))[0]


def sync(*values):
    return lax.optimization_barrier(values)


def window_start(window, step):
    return pl.multiple_of(jnp.minimum(window * step // 16 * 16, PAD - WINDOW), 16)


def image_of(row, length, step):
    image = jnp.where(row >= length, 1, 0) + jnp.where(row >= 2 * length, 1, 0)
    return jnp.where(row < 0, -1, jnp.where(row >= step, 3, image))


def mask_kernel(s_ref, mask_ref):
    length, step = s_ref[0], s_ref[1]

    def one(window, carry):
        base = window_start(window, step) - window * step
        shape = (WINDOW, 2 * WINDOW)
        rows = image_of(lax.broadcasted_iota(jnp.int32, shape, 0) + base, length, step)
        cols = lax.broadcasted_iota(jnp.int32, shape, 1)
        cols = jnp.where(cols < WINDOW, cols, cols - WINDOW)
        cols = image_of(cols + base, length, step)
        mask_ref[window] = jnp.where(rows == cols, 0.0, FAR).astype(jnp.float32)
        return carry

    lax.fori_loop(0, WINDOWS, one, 0)


def image_masks(lengths):
    return pl.pallas_call(
        mask_kernel,
        out_shape=jax.ShapeDtypeStruct((WINDOWS, WINDOW, 2 * WINDOW), jnp.float32),
        in_specs=[pl.BlockSpec(memory_space=pltpu.SMEM)],
        name="image_masks",
    )(lengths)


MASKS = pl.BlockSpec((WINDOWS, WINDOW, 2 * WINDOW), lambda i, s: (0, 0, 0))


def split_heads(value):
    lane = lax.broadcasted_iota(jnp.int32, value.shape, 1)
    zero = jnp.zeros_like(value)
    even, odd = jnp.where(lane < HEAD_DIM, value, zero), jnp.where(lane < HEAD_DIM, zero, value)
    return jnp.concatenate([even, odd], axis=0)


def slabs(refs, at):
    return [ref[at, i : i + 128] for ref in refs for i in range(0, ref.shape[1], 128)]


def join_heads(value):
    even, odd = value[:WINDOW], value[WINDOW:]
    lane = lax.broadcasted_iota(jnp.int32, even.shape, 1)
    return jnp.where(lane < HEAD_DIM, even, odd)


def keep_rows(ref, start, first, value):
    row = lax.broadcasted_iota(jnp.int32, value.shape, 0) + start
    value = jnp.where(row < ROWS, value, 0.0)
    at = pl.ds(start, WINDOW)
    old = ref[at, :].astype(jnp.float32)
    ref[at, :] = jnp.where(row >= first, value, old).astype(ref.dtype)


def forward_kernel(s_ref, mask_ref, q_ref, k_ref, v_ref, o_ref):
    step = s_ref[1]

    def one(window, carry):
        start = window_start(window, step)
        at = pl.ds(start, WINDOW)
        query = [split_heads(v * LOW(0.125)) for v in slabs([q_ref], at)]
        keys, values = slabs([k_ref], at), slabs([v_ref], at)
        mask = mask_ref[window]
        each = range(len(keys))
        scores = [dot_nt(keys[i], query[i]) + mask for i in each]
        top = [jnp.max(v, axis=0, keepdims=True) for v in scores]
        raised = [jnp.exp(scores[i] - top[i]) for i in each]
        scale = [1.0 / jnp.sum(v, axis=0, keepdims=True) for v in raised]
        out = [dot_tn((raised[i] * scale[i]).astype(LOW), values[i]) for i in each]
        for j in each:
            cols = slice(128 * j, 128 * j + 128)
            keep_rows(o_ref.at[:, cols], start, window * step, join_heads(out[j]))
        return carry

    lax.fori_loop(0, WINDOWS, one, 0)


def backward_kernel(s_ref, mask_ref, *refs):
    q_refs, k_refs, v_refs, g_refs, out_refs = [refs[2 * i : 2 * i + 2] for i in range(5)]
    step = s_ref[1]

    def one(window, carry):
        start = window_start(window, step)
        at = pl.ds(start, WINDOW)
        query = [split_heads(v * LOW(0.125)) for v in slabs(q_refs, at)]
        grad = [split_heads(v) for v in slabs(g_refs, at)]
        keys, values = slabs(k_refs, at), slabs(v_refs, at)
        mask = mask_ref[window]
        each = range(len(keys))
        scores = [dot_nt(keys[i], query[i]) + mask for i in each]
        grad_probs = [dot_nt(values[i], grad[i]) for i in each]
        top = [jnp.max(v, axis=0, keepdims=True) for v in scores]
        raised = [jnp.exp(scores[i] - top[i]) for i in each]
        scale = [1.0 / jnp.sum(v, axis=0, keepdims=True) for v in raised]
        probs = [raised[i] * scale[i] for i in each]
        inner = [jnp.sum(grad_probs[i] * probs[i], axis=0, keepdims=True) for i in each]
        grad_scores = [(probs[i] * (grad_probs[i] - inner[i])).astype(LOW) for i in each]
        grad_v = [dot_nn(probs[i].astype(LOW), grad[i]) for i in each]
        grad_k = [dot_nn(grad_scores[i], query[i]) for i in each]
        grad_q = [dot_tn(grad_scores[i], keys[i]) for i in each]
        first = window * step
        for j in each:
            out = out_refs[j // 2]
            cols = slice(j % 2 * 128, j % 2 * 128 + 128)
            keep_rows(out.at[0, :, cols], start, first, join_heads(grad_q[j]) * 0.125)
            keep_rows(out.at[1, :, cols], start, first, grad_k[j])
            keep_rows(out.at[2, :, cols], start, first, grad_v[j])
        return carry

    lax.fori_loop(0, WINDOWS, one, 0)


def attend_forward(lengths, masks, projected):
    def part(base):
        return pl.BlockSpec((PAD, D), lambda i, s: (0, base))

    return pl.pallas_call(
        forward_kernel,
        out_shape=jax.ShapeDtypeStruct((PAD, D), LOW),
        grid_spec=pltpu.PrefetchScalarGridSpec(
            num_scalar_prefetch=1,
            grid=(1,),
            in_specs=[MASKS, part(0), part(1), part(2)],
            out_specs=part(0),
        ),
        cost_estimate=cost(2e10, 1e7),
        name="attend_forward",
    )(lengths, masks, projected, projected, projected)


def attend_backward(numbers, masks, projected, grad):
    width = D // 4

    def part(base, i):
        return pl.BlockSpec((PAD, width), lambda n, s: (0, s[2 + i] + base))

    return pl.pallas_call(
        backward_kernel,
        out_shape=[jax.ShapeDtypeStruct((3, PAD, width), LOW)] * 2,
        grid_spec=pltpu.PrefetchScalarGridSpec(
            num_scalar_prefetch=1,
            grid=(1,),
            in_specs=[MASKS] + [part(base, i) for base in (0, 4, 8, 0) for i in (0, 1)],
            out_specs=[pl.BlockSpec((3, PAD, width), lambda n, s: (0, 0, 0))] * 2,
        ),
        cost_estimate=cost(2e10, 1e7),
        name="attend_backward",
    )(numbers, masks, *([projected] * 6), grad, grad)


def hidden_kernel(shards, steps, rows, s_ref, x_ref, b_ref, *refs):
    parts, (activ_ref, slope_ref, full), (held, sem) = refs[:5], refs[5:8], refs[8:]
    step = pl.program_id(0)
    tile = activ_ref.shape[1]
    half = held.shape[1] // 2

    def columns(i):
        return fetch_copies(shards, s_ref, parts, held, sem.at[i], i * half, i * half, half)

    def keep():
        return pltpu.make_async_copy(held, full, sem.at[0, 0])

    @pl.when(step == 0)
    def _():
        start_wait(columns(0), wait=False)
        start_wait(columns(1), wait=False)
        start_wait(columns(0), start=False)

    @pl.when(step == steps // 2)
    def _():
        start_wait(columns(1), start=False)
        keep().start()

    weight = held[:, pl.ds(pl.multiple_of(step * tile, tile), tile)]
    for i in range(PAD // rows):
        at = slice(i * rows, (i + 1) * rows)
        hidden = dot_nn(x_ref[at, :], weight) + b_ref[...]
        cdf = 0.5 * lax.erf(hidden * 0.7071067811865476) + 0.5
        density = jnp.exp(-0.5 * hidden * hidden) * 0.3989422804014327
        activ_ref[at, :] = (hidden * cdf).astype(LOW)
        slope_ref[at, :] = (cdf + hidden * density).astype(LOW)

    @pl.when(step == steps - 1)
    def _():
        keep().wait()


def hidden_layer(second, bias, shard, sets):
    width = bias.shape[0]
    tile = 512
    steps = width // tile
    return pl.pallas_call(
        partial(hidden_kernel, lax.axis_size("fsdp"), steps, 736),
        out_shape=[jax.ShapeDtypeStruct((PAD, width), LOW)] * 2 + [fetch_shape(shard, width)],
        grid_spec=pltpu.PrefetchScalarGridSpec(
            num_scalar_prefetch=1,
            grid=(steps,),
            in_specs=[
                pl.BlockSpec((PAD, D), lambda n, s: (0, 0)),
                pl.BlockSpec((1, tile), lambda n, s: (0, n)),
            ]
            + [ANYWHERE] * 5,
            out_specs=[pl.BlockSpec((PAD, tile), lambda n, s: (0, n))] * 2 + [ANYWHERE],
            scratch_shapes=fetch_scratch(shard, width, 2),
        ),
        cost_estimate=cost(2.4e10, 4e7),
        name="hidden_layer",
    )(fetch_numbers(), second, bias.reshape(1, width), shard, *sets)


def hidden_back_kernel(shards, steps, rows, s_ref, g_ref, slope_ref, *refs):
    parts, (out_ref, sum_ref, full), (held, sem) = refs[:5], refs[5:8], refs[8:]
    step = pl.program_id(0)
    per = steps // shards
    tile = out_ref.shape[1]

    def copies():
        return fetch_copies(shards, s_ref, parts, held, sem)

    def keep():
        return pltpu.make_async_copy(held, full, sem.at[0])

    @pl.when(step == 0)
    def _():
        every = copies()
        start_wait(every, wait=False)
        start_wait(every[:1], start=False)

    for k in range(1, shards):

        @pl.when(step == k * per)
        def _(k=k):
            start_wait(copies()[k :: shards - 1], start=False)
            if k == shards - 1:
                keep().start()

    block = lax.rem(s_ref[1] + step // per, shards) * per + step % per
    weight = held[pl.ds(pl.multiple_of(block * tile, tile), tile), :]
    total = jnp.zeros_like(sum_ref)
    for i in range(PAD // rows):
        at = slice(i * rows, (i + 1) * rows)
        grad = dot_nt(g_ref[at, :], weight) * slope_ref[at, :].astype(jnp.float32)
        grad = grad.astype(LOW)
        out_ref[at, :] = grad
        total = total + column_sum(grad.astype(jnp.float32))
    sum_ref[...] = total

    @pl.when(step == steps - 1)
    def _():
        keep().wait()


def hidden_back(grad, slope, shard, sets):
    width = slope.shape[1]
    tile = 512
    steps = width // tile
    shards = lax.axis_size("fsdp")
    per = steps // shards

    def block(n, s):
        return lax.rem(s[1] + n // per, shards) * per + n % per

    cols = pl.BlockSpec((PAD, tile), lambda n, s: (0, block(n, s)))
    return pl.pallas_call(
        partial(hidden_back_kernel, shards, steps, 368),
        out_shape=[
            jax.ShapeDtypeStruct((PAD, width), LOW),
            jax.ShapeDtypeStruct((1, width), jnp.float32),
            fetch_shape(shard),
        ],
        grid_spec=pltpu.PrefetchScalarGridSpec(
            num_scalar_prefetch=1,
            grid=(steps,),
            in_specs=[pl.BlockSpec((PAD, D), lambda n, s: (0, 0)), cols] + [ANYWHERE] * 5,
            out_specs=[cols, pl.BlockSpec((1, tile), lambda n, s: (0, block(n, s))), ANYWHERE],
            scratch_shapes=fetch_scratch(shard),
        ),
        cost_estimate=cost(1.8e10, 4e7),
        name="hidden_back",
    )(fetch_numbers(), grad, slope, shard, *sets)


def normalise(value):
    average = jnp.mean(value, axis=-1, keepdims=True)
    centred = value - average
    inv_std = lax.rsqrt(jnp.mean(centred * centred, axis=-1, keepdims=True) + EPS)
    return centred * inv_std, inv_std


def back_through_norm(grad, normed, inv_std, gain):
    scaled = grad * gain
    inner = (
        scaled
        - jnp.mean(scaled, axis=-1, keepdims=True)
        - normed * jnp.mean(scaled * normed, axis=-1, keepdims=True)
    )
    return inv_std * inner


def column_sum(value):
    return jnp.sum(value, axis=0, keepdims=True)


VECTORS = pl.BlockSpec((8, D), lambda i, *s: (0, 0))
GAIN_ONE, SHIFT_ONE, QUERY, VALUE, OUTPUT, GAIN_TWO, SHIFT_TWO, RETURN = [
    slice(i, i + 1) for i in range(8)
]


def rows_of(width, stacked=0):
    if stacked:
        return pl.BlockSpec((stacked, ROW_TILE, width), lambda i, *s: (0, i, 0))
    return pl.BlockSpec((ROW_TILE, width), lambda i, *s: (i, 0))


def whole(*shape):
    return pl.BlockSpec(shape, lambda i, *s: (0,) * len(shape))


def embed_kernel(tokens_ref, spread_ref, table_ref, vec_ref, stream_ref, first_ref):
    row = lax.broadcasted_iota(jnp.int32, stream_ref.shape, 0) + pl.program_id(0) * ROW_TILE
    tokens = jnp.where(row < ROWS, tokens_ref[...].astype(jnp.float32), 0.0)
    stream = tokens + dot_nn(spread_ref[...], table_ref[...])
    stream_ref[...] = stream
    normed, _ = normalise(stream)
    first_ref[...] = (normed * vec_ref[GAIN_ONE, :] + vec_ref[SHIFT_ONE, :]).astype(LOW)


def embed(tokens, spread, table, vectors):
    slots = spread.shape[1]
    return pl.pallas_call(
        embed_kernel,
        out_shape=[
            jax.ShapeDtypeStruct((PAD, D), jnp.float32),
            jax.ShapeDtypeStruct((PAD, D), LOW),
        ],
        grid=(PAD // ROW_TILE,),
        in_specs=[rows_of(D), rows_of(slots), whole(slots, D), VECTORS],
        out_specs=[rows_of(D), rows_of(D)],
        cost_estimate=cost(1e9, 1.5e7),
        name="embed",
    )(tokens, spread, table, vectors)


def project_kernel(shards, steps, s_ref, a_ref, b_ref, *refs):
    parts, (out_ref, full), (held, sem) = refs[:5], refs[5:7], refs[7:]
    finish = fetch(shards, s_ref, parts, held, full, sem, steps)
    query, value = b_ref[QUERY, :], b_ref[VALUE, :]
    bias = jnp.concatenate([query, jnp.zeros_like(query), value], axis=1)
    out_ref[...] = (dot_nn(a_ref[...], held[...]) + bias).astype(LOW)
    finish()


def project(first, vectors, shard, sets):
    width = shard.shape[1]
    steps = PAD // ROW_TILE
    return pl.pallas_call(
        partial(project_kernel, lax.axis_size("fsdp"), steps),
        out_shape=[jax.ShapeDtypeStruct((PAD, width), LOW), fetch_shape(shard)],
        grid_spec=pltpu.PrefetchScalarGridSpec(
            num_scalar_prefetch=1,
            grid=(steps,),
            in_specs=[rows_of(D), VECTORS] + [ANYWHERE] * 5,
            out_specs=[rows_of(width), ANYWHERE],
            scratch_shapes=fetch_scratch(shard),
        ),
        cost_estimate=cost(2 * PAD * D * width, 2e7),
        name="project",
    )(fetch_numbers(), first, vectors, shard, *sets)


def branch_kernel(shards, steps, s_ref, a_ref, stream_ref, vec_ref, *refs):
    parts, (mid_ref, second_ref, full), (held, sem) = refs[:5], refs[5:8], refs[8:]
    first = parts[0].shape[1] - D
    finish = fetch(shards, s_ref, parts, held, full, sem, steps, first)
    mid = stream_ref[...] + dot_nn(a_ref[...], held[...]) + vec_ref[OUTPUT, :]
    mid_ref[...] = mid
    normed, _ = normalise(mid)
    second_ref[...] = (normed * vec_ref[GAIN_TWO, :] + vec_ref[SHIFT_TWO, :]).astype(LOW)
    finish()


def branch(attended, stream, vectors, shard, sets):
    steps = PAD // ROW_TILE
    return pl.pallas_call(
        partial(branch_kernel, lax.axis_size("fsdp"), steps),
        out_shape=[
            jax.ShapeDtypeStruct((PAD, D), jnp.float32),
            jax.ShapeDtypeStruct((PAD, D), LOW),
            fetch_shape(shard, D),
        ],
        grid_spec=pltpu.PrefetchScalarGridSpec(
            num_scalar_prefetch=1,
            grid=(steps,),
            in_specs=[rows_of(D), rows_of(D), VECTORS] + [ANYWHERE] * 5,
            out_specs=[rows_of(D), rows_of(D), ANYWHERE],
            scratch_shapes=fetch_scratch(shard, D),
        ),
        cost_estimate=cost(2 * PAD * D * D, 3e7),
        name="branch",
    )(fetch_numbers(), attended, stream, vectors, shard, *sets)


def return_kernel(a_ref, w_ref, mid_ref, vec_ref, out_ref):
    value = mid_ref[...] + dot_nn(a_ref[...], w_ref[...]) + vec_ref[RETURN, :]
    out_ref[...] = value.astype(LOW)


def return_layer(activ, weight, mid, vectors):
    width = weight.shape[0]
    return pl.pallas_call(
        return_kernel,
        out_shape=jax.ShapeDtypeStruct((ROWS, D), LOW),
        grid=(PAD // ROW_TILE,),
        in_specs=[rows_of(width), whole(width, D), rows_of(D), VECTORS],
        out_specs=rows_of(D),
        cost_estimate=cost(2 * PAD * D * width, 3e7),
        name="return_layer",
    )(activ, weight, mid, vectors)


def second_back_kernel(
    h_ref, w_ref, o_ref, mid_ref, g_ref, gain_ref, out_ref, low_ref, att_ref, sums_ref
):
    @pl.when(pl.program_id(0) == 0)
    def _():
        sums_ref[...] = jnp.zeros_like(sums_ref)

    grad = dot_nt(h_ref[...], w_ref[...])
    normed, inv_std = normalise(mid_ref[...])
    out = g_ref[...].astype(jnp.float32)
    sums_ref[3:4, :] += column_sum(out)
    out = out + back_through_norm(grad, normed, inv_std, gain_ref[GAIN_TWO, :])
    out_ref[...] = out
    low = out.astype(LOW)
    low_ref[...] = low
    att_ref[...] = dot_nt(low, o_ref[...]).astype(LOW)
    sums_ref[0:1, :] += column_sum(low.astype(jnp.float32))
    sums_ref[1:2, :] += column_sum(grad * normed)
    sums_ref[2:3, :] += column_sum(grad)


def second_back(grad_hidden, weight, output, mid, grad, vectors):
    width = grad_hidden.shape[1]
    return pl.pallas_call(
        second_back_kernel,
        out_shape=[
            jax.ShapeDtypeStruct((PAD, D), jnp.float32),
            jax.ShapeDtypeStruct((PAD, D), LOW),
            jax.ShapeDtypeStruct((PAD, D), LOW),
            jax.ShapeDtypeStruct((8, D), jnp.float32),
        ],
        grid=(PAD // ROW_TILE,),
        in_specs=[
            rows_of(width),
            whole(D, width),
            whole(D, D),
            rows_of(D),
            rows_of(D),
            VECTORS,
        ],
        out_specs=[rows_of(D), rows_of(D), rows_of(D), whole(8, D)],
        cost_estimate=cost(2 * PAD * D * width, 4e7),
        name="second_back",
    )(grad_hidden, weight, output, mid, grad, vectors)


def first_back_kernel(s_ref, *refs):
    heads, w_refs, (stream_ref, mid_ref, spread_ref, gain_ref) = refs[:4], refs[4:16], refs[16:20]
    out_ref, table_ref, sums_ref = refs[20:]

    @pl.when(pl.program_id(0) == 0)
    def _():
        sums_ref[...] = jnp.zeros_like(sums_ref)
        table_ref[...] = jnp.zeros_like(table_ref)

    grad = 0.0
    for j, ref in enumerate(heads):
        for t in range(3):
            grad = grad + dot_nt(ref[t], w_refs[3 * j + t][...])
    normed, inv_std = normalise(stream_ref[...])
    out = mid_ref[...] + back_through_norm(grad, normed, inv_std, gain_ref[GAIN_ONE, :])
    low = out.astype(LOW)
    out_ref[...] = low
    rest = (out - low.astype(jnp.float32)).astype(LOW)
    table_ref[...] += dot_tn(spread_ref[...], low) + dot_tn(spread_ref[...], rest)
    sums_ref[0:1, :] += column_sum(grad * normed)
    sums_ref[1:2, :] += column_sum(grad)
    for j, ref in enumerate(heads):
        width = ref.shape[2]
        at = pl.ds(pl.multiple_of(s_ref[j] * width, width), width)
        sums_ref[2:3, at] += column_sum(ref[0].astype(jnp.float32))
        sums_ref[3:4, at] += column_sum(ref[2].astype(jnp.float32))


def first_back(quarters, heads, joined, stream, grad_mid, spread, vectors):
    width = D // 4
    w_specs = [
        pl.BlockSpec((D, width), lambda i, s, j=j, t=t: (0, 4 * t + s[j]))
        for j in range(4)
        for t in range(3)
    ]
    slots = spread.shape[1]
    return pl.pallas_call(
        first_back_kernel,
        out_shape=[
            jax.ShapeDtypeStruct((ROWS, D), LOW),
            jax.ShapeDtypeStruct((slots, D), jnp.float32),
            jax.ShapeDtypeStruct((8, D), jnp.float32),
        ],
        grid_spec=pltpu.PrefetchScalarGridSpec(
            num_scalar_prefetch=1,
            grid=(PAD // ROW_TILE,),
            in_specs=[rows_of(width, 3)] * 4
            + w_specs
            + [rows_of(D), rows_of(D), rows_of(slots), VECTORS],
            out_specs=[rows_of(D), whole(slots, D), whole(8, D)],
        ),
        cost_estimate=cost(2 * PAD * D * 3 * D, 4e7),
        name="first_back",
    )(quarters, *heads, *([joined] * 12), stream, grad_mid, spread, vectors)


def widen_kernel(moves, count, *refs):
    for source, at, target, block, to, width in moves:
        rows = refs[source].shape[2]
        down = slice(block * rows, (block + 1) * rows)
        for core in (0, 1):
            value = refs[source][0, core, :, at : at + width].astype(jnp.float32)
            refs[count + target][down, to[core] : to[core] + width] = value


def widen(sources, shapes, moves):
    rows = sources[0].shape[1]
    return pl.pallas_call(
        partial(widen_kernel, moves, len(sources)),
        out_shape=[jax.ShapeDtypeStruct((4 * n * rows, w), jnp.float32) for n, w in shapes],
        grid=(4,),
        in_specs=[
            pl.BlockSpec((1, 2, rows, v.shape[2]), lambda i: (i, 0, 0, 0)) for v in sources
        ],
        out_specs=[pl.BlockSpec((n * rows, w), lambda i: (i, 0)) for n, w in shapes],
        cost_estimate=cost(1, 6e6),
        name="widen",
    )(*[v.reshape(4, 2, rows, v.shape[2]) for v in sources])


def grad_value(f_ref, a_ref, b_ref):
    if len(b_ref.shape) == 2:
        return dot_tn(a_ref[...], b_ref[...]) * f_ref[0]
    return jnp.concatenate([dot_tn(a_ref[...], b_ref[i]) for i in range(3)], axis=1) * f_ref[0]


def grad_send_kernel(c_ref, f_ref, a_ref, b_ref, out_ref):
    out_ref[...] = grad_value(f_ref, a_ref, b_ref).astype(LOW)


def grad_keep_kernel(planes, c_ref, f_ref, a_ref, b_ref, got_ref, *refs):
    keep_ref, send_ref = refs[-2:]
    value = (grad_value(f_ref, a_ref, b_ref) + got_ref[...].astype(jnp.float32)).astype(LOW)
    core, place = c_ref[0], c_ref[1]
    rows = value.shape[0] // planes // 4
    for quarter in range(4):
        bits = place ^ quarter
        role = jnp.where(core == 0, bits, (bits >> 1) | ((bits & 1) << 1))
        for ref, near in ((keep_ref, 0), (send_ref, 1)):

            @pl.when(role % 2 == near)
            def _(ref=ref, quarter=quarter, role=role):
                for plane in range(planes):
                    at = (plane * 4 + quarter) * rows
                    ref[role // 2, plane] = value[at : at + rows]


def grad_half(
    numbers, factor, left, right, got=None, tile_m=1024, tile_n=512, width=None, first=0, into=()
):
    rows = left.shape[1]
    shards = lax.axis_size("fsdp")
    stacked = right.ndim == 3
    cols = 3 * right.shape[2] if stacked else right.shape[1] // 2
    tile_n = cols if stacked else tile_n
    steps = cols // tile_n
    in_specs = [
        pl.BlockSpec(memory_space=pltpu.SMEM),
        pl.BlockSpec((PAD, tile_m), lambda m, n, c: (0, m)),
    ]
    if stacked:
        in_specs.append(pl.BlockSpec((3, PAD, cols // 3), lambda m, n, c: (0, 0, 0)))
    else:
        in_specs.append(pl.BlockSpec((PAD, tile_n), lambda m, n, c: (0, n + c[0] * steps)))
    flat_spec = pl.BlockSpec((tile_m, tile_n), lambda m, n, c: (m, n))
    operands = [numbers, factor, left, right]
    if got is None:
        kernel, name = grad_send_kernel, "grad_send"
        out_shape, out_specs = jax.ShapeDtypeStruct((rows, cols), LOW), flat_spec
    else:
        planes = tile_m * shards // rows
        part = rows // shards // 4
        kernel, name = partial(grad_keep_kernel, planes), "grad_keep"
        in_specs.append(flat_spec)
        operands.append(got)
        out_shape = [jax.ShapeDtypeStruct((2, shards, part, width or cols), LOW)] * 2
        out_specs = [
            pl.BlockSpec((2, planes, part, tile_n), lambda m, n, c: (0, m, 0, n + first // tile_n))
        ] * 2
        in_specs += [ANYWHERE] * len(into)
        operands += into
    return pl.pallas_call(
        kernel,
        out_shape=out_shape,
        grid_spec=pltpu.PrefetchScalarGridSpec(
            num_scalar_prefetch=1,
            grid=(rows // tile_m, steps),
            in_specs=in_specs,
            out_specs=out_specs,
        ),
        input_output_aliases={5 + i: i for i in range(len(into))},
        cost_estimate=cost(2 * PAD * rows * cols, 1e7),
        name=name,
    )(*operands)


def swap(value, even, odd):
    size = lax.axis_size("dp")
    return lax.ppermute(value, "dp", [(i, i ^ (odd if i % 2 else even)) for i in range(size)])


def swap_core(value):
    return swap(value, 1, 1)


def swap_first(value):
    return swap(value, 2, 4)


def swap_second(value):
    return swap(value, 4, 2)


def own_piece(shard):
    part = shard.shape[0] // GROUP
    place = lax.axis_index("dp") % GROUP
    return lax.dynamic_slice_in_dim(shard, place * part, part, 0)


def from_above(piece):
    shards = lax.axis_size("fsdp")
    return [
        lax.ppermute(piece, "fsdp", [((i + k) % shards, i) for i in range(shards)])
        for k in range(1, shards)
    ]


def gather_z_native(piece):
    return lax.all_gather(piece, "fsdp", axis=0, tiled=False)


def others(every):
    shards = every.shape[0]
    twice = jnp.concatenate([every, every[:-1]], axis=0)
    return lax.dynamic_slice_in_dim(twice, lax.axis_index("fsdp") + 1, shards - 1, 0)


def gather_first(own):
    return own, swap_first(own)


def gather_second(own, got):
    both = jnp.stack([own, got])
    return both, swap_second(both)


def gather_core(both, far):
    return both, far, swap_core(both), swap_core(far)


def fetch_copies(shards, s_ref, refs, held, sem, first=0, at_col=0, cols=None):
    own, sets = refs[0], refs[1:]
    place, row = s_ref[0], s_ref[1]
    rows = own.shape[0]
    cols = cols or own.shape[1]
    part = rows // GROUP
    source_cols, held_cols = pl.ds(first, cols), pl.ds(at_col, cols)
    copies = [
        pltpu.make_async_copy(
            own.at[:, source_cols],
            held.at[pl.ds(pl.multiple_of(row * rows, rows), rows), held_cols],
            sem.at[0],
        )
    ]
    for flip in range(2):
        base = place ^ flip
        first_bits = jnp.where(base % 2 == 0, 2, 4)
        for source, bits in (
            (sets[2 * flip].at[0], 0),
            (sets[2 * flip].at[1], first_bits),
            (sets[2 * flip + 1].at[0], 6 - first_bits),
            (sets[2 * flip + 1].at[1], 6),
        ):
            for k in range(1, shards):
                at = lax.rem(row + k, shards) * rows + (base ^ bits) * part
                target = held.at[pl.ds(pl.multiple_of(at, part), part), held_cols]
                copies.append(
                    pltpu.make_async_copy(
                        source.at[k - 1, :, source_cols], target, sem.at[len(copies)]
                    )
                )
    return copies


def start_wait(copies, start=True, wait=True):
    for copy in copies if start else ():
        copy.start()
    for copy in copies if wait else ():
        copy.wait()


def fetch(shards, s_ref, refs, held, full, sem, steps, first=0):
    def keep():
        return pltpu.make_async_copy(held, full, sem.at[0])

    @pl.when(pl.program_id(0) == 0)
    def _():
        start_wait(fetch_copies(shards, s_ref, refs, held, sem, first, 0, held.shape[1]))
        keep().start()

    def finish():
        @pl.when(pl.program_id(0) == steps - 1)
        def _():
            keep().wait()

    return finish


def fetch_numbers():
    place = lax.axis_index("dp") % GROUP
    return jnp.stack([place, lax.axis_index("fsdp")]).astype(jnp.int32)


def fetch_scratch(shard, cols=None, sets=1):
    shards = lax.axis_size("fsdp")
    count = 1 + 8 * (shards - 1)
    return [
        pltpu.VMEM((shards * shard.shape[0], cols or shard.shape[1]), shard.dtype),
        pltpu.SemaphoreType.DMA((count,) if sets == 1 else (sets, count)),
    ]


def fetch_shape(shard, cols=None):
    shards = lax.axis_size("fsdp")
    return jax.ShapeDtypeStruct((shards * shard.shape[0], cols or shard.shape[1]), shard.dtype)


def plane_gather(value, axis):
    size = lax.axis_size("dp")
    groups = None
    if size > GROUP:
        groups = [[g * GROUP + i for i in range(GROUP)] for g in range(size // GROUP)]
    return lax.all_gather(value, "dp", axis=axis, tiled=False, axis_index_groups=groups)


def rest_sum(value):
    size = lax.axis_size("dp")
    if size == GROUP:
        return value
    groups = [[g * GROUP + i for g in range(size // GROUP)] for i in range(GROUP)]
    return lax.psum(value, "dp", axis_index_groups=groups)


def add_low(left, right):
    return (left.astype(jnp.float32) + right.astype(jnp.float32)).astype(LOW)


def sum_first(got, keep):
    return add_low(keep[0], got[0]), swap_second(add_low(keep[1], got[1]))


def sum_z(both):
    shards, part, cols = both.shape
    piece = lax.psum_scatter(
        both.reshape(shards * part, cols), "fsdp", scatter_dimension=0, tiled=True
    )
    return rest_sum(piece)


def sum_z_direct(value):
    shards = lax.axis_size("fsdp")
    me = lax.axis_index("fsdp")
    total = lax.dynamic_index_in_dim(value, me, 0, keepdims=False).astype(jnp.float32)
    for step in range(1, shards):
        send = lax.dynamic_index_in_dim(value, (me + step) % shards, 0, keepdims=False)
        got = lax.ppermute(send, "fsdp", [(i, (i + step) % shards) for i in range(shards)])
        total = total + got.astype(jnp.float32)
    return total


def pack_kernel(s_ref, piece_ref, *refs):
    out_ref, rows_ref = refs[-2:]
    width, first = rows_ref.shape[1], piece_ref.shape[1]
    out_ref[:, :first] = piece_ref[...]
    rows_ref[...] = jnp.zeros_like(rows_ref)
    row = 0
    for ref in refs[:-2]:
        if len(ref.shape) == 2:
            rows_ref[row : row + ref.shape[0], :] = ref[...]
            row += ref.shape[0]
            continue
        for i in range(0, ref.shape[0], width):
            rows_ref[row : row + 1, :] = ref[i : i + width].reshape(1, width)
            row += 1
    tall = out_ref.shape[0]
    for i in range(rows_ref.shape[0] // tall):
        at = first + i * width
        out_ref[:, at : at + width] = rows_ref[i * tall : (i + 1) * tall, :]


def pack(shard, vectors, table):
    rows, cols = shard.shape
    tall, width = rows // GROUP, vectors[0].shape[0]
    wide = cols + 64 // tall * width
    place = (lax.axis_index("dp") % GROUP).astype(jnp.int32).reshape(1)
    return pl.pallas_call(
        pack_kernel,
        out_shape=jax.ShapeDtypeStruct((tall, wide), LOW),
        grid_spec=pltpu.PrefetchScalarGridSpec(
            num_scalar_prefetch=1,
            grid=(1,),
            in_specs=[pl.BlockSpec((tall, cols), lambda i, s: (s[0], 0))]
            + [pl.BlockSpec(v.shape, lambda i, s: (0,)) for v in vectors]
            + [pl.BlockSpec(table.shape, lambda i, s: (0, 0))],
            out_specs=pl.BlockSpec((tall, wide), lambda i, s: (0, 0)),
            scratch_shapes=[pltpu.VMEM((64, width), LOW)],
        ),
        cost_estimate=cost(1, 1e5),
        name="pack",
    )(place, shard, *vectors, table)


def unpack_kernel(s_ref, *refs):
    parts, (out_ref, table_ref, rest_ref, rows_ref) = refs[:-4], refs[-4:]
    width, first = rows_ref.shape[1], rest_ref.shape[2]
    tall = parts[0].shape[0]
    table_ref[...] = jnp.zeros_like(table_ref)
    for k, ref in enumerate(parts):
        at = lax.rem(s_ref[0] + k, len(parts)) * width
        at = pl.ds(pl.multiple_of(at, width), width)
        for i in range(64 // tall):
            source = first + i * width
            rows_ref[i * tall : (i + 1) * tall, :] = ref[:, source : source + width]
        if k:
            rest_ref[k - 1] = ref[:, :first]
        out_ref[:, at] = rows_ref[...].astype(jnp.float32)
        table = rows_ref[12 : 12 + SMALL_LEN, :]
        table_ref[0:SMALL_LEN, at] = table
        table_ref[64 : 64 + SMALL_LEN, at] = table


def unpack(parts, first, width):
    shards = len(parts)
    tall, wide = parts[0].shape
    return pl.pallas_call(
        unpack_kernel,
        out_shape=[
            jax.ShapeDtypeStruct((64, shards * width), jnp.float32),
            jax.ShapeDtypeStruct((128, shards * width), LOW),
            jax.ShapeDtypeStruct((shards - 1, tall, first), LOW),
        ],
        grid=(1,),
        in_specs=[pl.BlockSpec(memory_space=pltpu.SMEM)]
        + [pl.BlockSpec((tall, wide), lambda i: (0, 0))] * shards,
        out_specs=[
            pl.BlockSpec((64, shards * width), lambda i: (0, 0)),
            pl.BlockSpec((128, shards * width), lambda i: (0, 0)),
            pl.BlockSpec((shards - 1, tall, first), lambda i: (0, 0, 0)),
        ],
        scratch_shapes=[pltpu.VMEM((64, width), LOW)],
        cost_estimate=cost(1, 1e6),
        name="unpack",
    )(lax.axis_index("fsdp").astype(jnp.int32).reshape(1), *parts)


def per_device(
    tokens,
    output_grad,
    group_member,
    image_counts,
    position_source,
    position_table,
    first_gain,
    first_shift,
    input_proj,
    query_bias,
    value_bias,
    output_proj,
    output_bias,
    second_gain,
    second_shift,
    hidden_weight,
    hidden_bias,
    return_weight,
    return_bias,
):
    dp_size = lax.axis_size("dp")
    fsdp_size = lax.axis_size("fsdp")
    core = (lax.axis_index("dp") & 1).astype(jnp.int32)
    quarter = ((lax.axis_index("dp") % GROUP) >> 1).astype(jnp.int32)
    mine, other = jnp.stack([core, quarter]), jnp.stack([1 - core, quarter])
    vectors = (
        first_gain,
        first_shift,
        query_bias,
        value_bias,
        output_bias,
        second_gain,
        second_shift,
        return_bias,
        hidden_bias,
    )
    packed_own = pack(input_proj, vectors, position_table)
    parts = from_above(packed_own)
    hidden_shard = jnp.concatenate([hidden_weight, output_proj], axis=1)
    hidden_own = own_piece(hidden_weight)
    output_own = own_piece(output_proj)
    return_z = own_piece(return_weight)
    member = group_member[0]
    is_large = member == 1
    length = jnp.where(is_large, LARGE_LEN, SMALL_LEN)
    step = jnp.where(is_large, LARGE_LEN, 3 * SMALL_LEN)
    group_high = dp_size * 7 // 16
    group_low = dp_size - group_high
    counts = image_counts.astype(jnp.float32)
    share = jnp.where(is_large, counts[1], counts[0]) / (counts[0] + counts[1])
    images = jnp.where(
        is_large,
        group_high * fsdp_size * (ROWS // LARGE_LEN),
        group_low * fsdp_size * (ROWS // SMALL_LEN),
    ).astype(jnp.float32)
    factor = share / images
    scale = factor.reshape(1)

    row_index = jnp.arange(PAD, dtype=jnp.int32)
    place = jnp.where(row_index < ROWS, row_index % length, -1)
    inter = interp_table(position_source)
    identity = (
        jnp.arange(LARGE_LEN, dtype=jnp.int32)[:, None]
        == jnp.arange(SMALL_LEN, dtype=jnp.int32)[None, :]
    ).astype(jnp.float32)
    mixing = jnp.where(is_large, inter, identity)
    picker = (place[:, None] == jnp.arange(LARGE_LEN, dtype=jnp.int32)[None, :]).astype(jnp.float32)
    spread = jnp.dot(picker, mixing, precision=lax.Precision.HIGHEST)
    lengths = jnp.stack([length, step])
    upper = spread.astype(LOW)
    lower = (spread - upper.astype(jnp.float32)).astype(LOW)
    spread_low = jnp.concatenate(
        [jnp.pad(v, ((0, 0), (0, 64 - SMALL_LEN))) for v in (upper, lower)], axis=1
    )

    quarters = jnp.stack([2 * core, 2 - 2 * core, 2 * core + 1, 3 - 2 * core])
    numbers_one = jnp.concatenate([lengths, quarters[:2]])
    numbers_two = jnp.concatenate([lengths, quarters[2:]])
    spread_low, scale, mine, other, lengths, numbers_one, numbers_two, hidden_own, *parts = sync(
        spread_low, scale, mine, other, lengths, numbers_one, numbers_two, hidden_own, *parts
    )
    smalls, table_pair, joint_z = unpack([packed_own] + parts, 3 * D, first_gain.shape[0])
    hidden_add = smalls[8:12].reshape(4, fsdp_size, -1).transpose(1, 0, 2).reshape(-1)
    joint_one = gather_first(joint_z)
    hidden_z = gather_z_native(after(hidden_own, joint_z))
    output_z = from_above(after(output_own, joint_z))
    stream, first_low = embed(tokens, spread_low, table_pair, smalls)
    first_low, *joint_one = sync(first_low, *joint_one)
    joint_two = gather_second(*joint_one)
    output_grad, lengths, _ = sync(output_grad, lengths, joint_two[0])
    masks = image_masks(lengths)
    grad_pad = jnp.pad(output_grad, ((0, PAD - ROWS), (0, 0)))
    output_z = jnp.stack(output_z)
    joint_sets = gather_core(*joint_two)
    hidden_z, output_z, hidden_add, return_z, grad_pad, masks, _ = sync(
        hidden_z, output_z, hidden_add, return_z, grad_pad, masks, joint_two[1]
    )
    first_low, *joint_sets = sync(first_low, *joint_sets)
    hidden_one = gather_first(jnp.concatenate([others(hidden_z), output_z], axis=-1))
    return_early, *return_late = from_above(return_z)
    projected, joint_full = project(
        after(first_low, hidden_one[0]), smalls, input_proj, joint_sets
    )
    projected, return_early, *hidden_one = sync(projected, return_early, *hidden_one)
    hidden_two = gather_second(*hidden_one)
    projected = after(projected, hidden_two[0])
    attended = attend_forward(lengths, masks, projected)
    attended, *rest = sync(attended, *hidden_two, *return_late)
    hidden_two, return_late = rest[:2], rest[2:]
    hidden_sets = gather_core(*hidden_two)
    return_one = gather_first(jnp.stack([return_early, *return_late]))
    attended, *hidden_sets = sync(attended, *hidden_sets)
    mid, second, outproj_full = branch(
        after(attended, return_one[0]),
        stream,
        smalls,
        hidden_shard,
        hidden_sets,
    )
    second, *return_one = sync(second, *return_one)
    return_two = gather_second(*return_one)
    activ, slope, hidden_full = hidden_layer(
        after(second, return_two[0]), hidden_add, hidden_shard, hidden_sets
    )
    activ, slope, *return_two = sync(activ, slope, *return_two)
    return_sets = gather_core(*return_two)
    return_send = grad_half(other, scale, activ, grad_pad)
    return_send, *return_sets = sync(return_send, *return_sets)
    return_got = swap_core(return_send)
    grad_hidden, grad_hidden_add, return_full = hidden_back(
        after(grad_pad, return_send), slope, return_weight, return_sets
    )
    grad_hidden, return_got = sync(grad_hidden, return_got)
    return_keep, return_out = grad_half(mine, scale, activ, grad_pad, return_got)
    return_in = swap_first(return_out)
    hidden_send = grad_half(other, scale, after(second, return_out), grad_hidden)
    hidden_got = swap_core(hidden_send)
    grad_mid, grad_branch, grad_att, sums_two = second_back(
        after(grad_hidden, hidden_send), hidden_full, outproj_full, mid, grad_pad, smalls
    )
    grad_branch, hidden_got, return_in = sync(grad_branch, hidden_got, return_in)
    return_kept, return_in = sum_first(return_in, return_keep)
    hidden_keep, hidden_out = grad_half(
        mine, scale, after(second, return_kept), grad_hidden, hidden_got
    )
    hidden_out, grad_branch, return_in = sync(hidden_out, grad_branch, return_in)
    hidden_in = swap_first(hidden_out)
    output_send = grad_half(other, scale, attended, grad_branch)
    output_got = swap_core(output_send)
    return_piece = sum_z(add_low(return_kept, return_in))
    mine_one, other_one = attend_backward(
        numbers_one, masks, projected, after(grad_att, output_send)
    )
    mine_one, other_one, output_got, hidden_in, return_piece = sync(
        mine_one, other_one, output_got, hidden_in, return_piece
    )
    hidden_kept, hidden_in = sum_first(hidden_in, hidden_keep)
    joint_send = grad_half(other, scale, after(first_low, hidden_kept), other_one, tile_m=512)
    joint_got = swap_core(joint_send)
    wide = dict(width=5 * D // 4)
    output_pair = grad_half(
        mine,
        scale,
        attended,
        after(grad_branch, joint_send),
        output_got,
        tile_n=256,
        first=3 * D // 4,
        **wide,
    )
    *output_pair, joint_got = sync(*output_pair, joint_got)
    joint_keep, joint_out = grad_half(
        mine, scale, first_low, mine_one, joint_got, tile_m=512, into=output_pair, **wide
    )
    joint_out, hidden_in = sync(joint_out, hidden_in)
    joint_in = swap_first(joint_out)
    hidden_piece = sum_z(add_low(hidden_kept, hidden_in))
    mine_two, other_two = attend_backward(
        numbers_two, masks, projected, after(grad_att, joint_out)
    )
    mine_two, other_two, joint_in, hidden_piece = sync(mine_two, other_two, joint_in, hidden_piece)
    joint_kept, joint_in = sum_first(joint_in, joint_keep)
    last_send = grad_half(other, scale, after(first_low, joint_kept), other_two, tile_m=512)
    last_got = swap_core(last_send)
    last_keep, last_out = grad_half(mine, scale, first_low, mine_two, last_got, tile_m=512)
    last_out, joint_in = sync(last_out, joint_in)
    joint_piece = sum_z(add_low(joint_kept, joint_in))
    last_in = swap_first(last_out)
    heads = sync(mine_one, other_one, mine_two, other_two, last_out)[:4]
    tokens_grad, grad_table, sums_one = first_back(
        quarters, heads, joint_full, stream, grad_mid, spread_low, smalls
    )
    tokens_grad, grad_table, sums_one, last_in, joint_piece = sync(
        tokens_grad, grad_table, sums_one, last_in, joint_piece
    )
    last_kept, last_in = sum_first(last_in, last_keep)
    rows = joint_piece.shape[0]
    blocks = return_piece.shape[0] // rows
    pieces = [return_piece[i * rows : (i + 1) * rows] for i in range(blocks)]
    pieces += [hidden_piece, joint_piece]
    return_cols, hidden_cols = blocks * return_piece.shape[1], hidden_piece.shape[1]
    every = plane_gather(jnp.concatenate(pieces, axis=1), axis=0)

    grad_table = grad_table[:SMALL_LEN] + grad_table[64 : 64 + SMALL_LEN]
    hidden_rows = grad_hidden_add.reshape(fsdp_size, 4, -1).transpose(1, 0, 2).reshape(4, D)
    packed = jnp.concatenate([sums_one[:4], sums_two[:4], hidden_rows, grad_table], axis=0) * scale[0]
    packed = jnp.pad(packed, ((0, smalls.shape[0] - packed.shape[0]), (0, 0))).astype(LOW)
    packed = packed.reshape(packed.shape[0], fsdp_size, -1).transpose(1, 0, 2)
    packed, last_in = sync(packed, last_in)
    last_both = add_low(last_kept, last_in)
    last_cols = last_both.shape[-1]
    packed = packed.reshape(fsdp_size, rows, -1)
    last_both = jnp.concatenate([last_both, packed], axis=-1)
    last_piece = sum_z_direct(last_both).astype(LOW)
    block_out = return_layer(after(activ, last_both), return_full, mid, smalls)
    block_out, last_piece = sync(block_out, last_piece)
    small_rows = 12 + SMALL_LEN
    wide = first_gain.shape[0]
    small_piece = last_piece[:, last_cols:].reshape(-1, wide)[:small_rows].reshape(rows, -1)
    last_piece = jnp.concatenate([last_piece[:, :last_cols], small_piece], axis=1)
    last_every = plane_gather(rest_sum(last_piece), axis=0)
    summed = jnp.sum(last_every[:, :, last_cols:].astype(jnp.float32), axis=0)
    summed = summed.reshape(small_rows, -1)
    half, part = D // 2, D // 4
    moves = [(0, i * half, 0, i, (0, half), half) for i in range(blocks)]
    moves.append((0, return_cols, 1, 0, (0, 2 * D), 2 * D))
    for t in range(3):
        to = (t * D, t * D + half)
        moves.append((0, return_cols + hidden_cols + t * part, 2, 0, to, part))
        moves.append((1, t * part, 2, 0, (to[0] + part, to[1] + part), part))
    moves.append((0, return_cols + hidden_cols + 3 * part, 3, 0, (0, half), half))
    return_w_out, hidden_w_out, joint_out, outproj_out = widen(
        [every, last_every], [(blocks, D), (1, 4 * D), (1, 3 * D), (1, D)], moves
    )
    return (
        block_out,
        tokens_grad,
        summed[12 : 12 + SMALL_LEN],
        summed[0],
        summed[1],
        joint_out,
        summed[2],
        summed[3],
        outproj_out,
        summed[4],
        summed[5],
        summed[6],
        hidden_w_out,
        summed[8:12].reshape(-1),
        return_w_out,
        summed[7],
    )


def solution(mesh):
    in_specs = (
        P(("dp", "fsdp"), None),
        P(("dp", "fsdp"), None),
        P("dp"),
        P(),
        P(),
        P(None, "fsdp"),
        P("fsdp"),
        P("fsdp"),
        P("fsdp", None),
        P("fsdp"),
        P("fsdp"),
        P("fsdp", None),
        P("fsdp"),
        P("fsdp"),
        P("fsdp"),
        P("fsdp", None),
        P("fsdp"),
        P("fsdp", None),
        P("fsdp"),
    )
    out_specs = (
        P(("dp", "fsdp"), None),
        P(("dp", "fsdp"), None),
        P(None, "fsdp"),
        P("fsdp"),
        P("fsdp"),
        P("fsdp", None),
        P("fsdp"),
        P("fsdp"),
        P("fsdp", None),
        P("fsdp"),
        P("fsdp"),
        P("fsdp"),
        P("fsdp", None),
        P("fsdp"),
        P("fsdp", None),
        P("fsdp"),
    )
    return jax.shard_map(
        per_device, mesh=mesh, in_specs=in_specs, out_specs=out_specs, check_vma=False
    )
```
